32 devices in a mesh: dp: 8 (over z, y), mp: 4 (over x, core).
Axes of the slice: x: 2, y: 2, z: 4, core: 2. Of those that a mesh axis runs over, the one named last changes fastest.
Arguments:
- patches: bfloat16 [16384, 768], P('dp'), may hold values from -6 to 6
- image_ids: int32 [16384], P('dp'), may hold values from 0 to 7, as said below
- patch_grid: int32 [2, 16384], P(None, 'dp'), may hold values from 0 to 31, as said below
- first_norm_gain: float32 [768], replicated, may hold values from 0.1 to 1.9
- first_norm_bias: float32 [768], replicated, may hold values from -1.8 to 1.8
- qkv_weight: bfloat16 [768, 3, 768], P(None, None, 'mp'), may hold values from -0.3125 to 0.3125
- qkv_bias: float32 [3, 768], P(None, 'mp'), may hold values from -1.8 to 1.8
- rope_freq: float32 [12, 64], P('mp'), may hold values from -1 to 1
- out_weight: bfloat16 [768, 768], P('mp'), may hold values from -0.625 to 0.625
- out_bias: float32 [768], replicated, may hold values from -1.8 to 1.8
- second_norm_gain: float32 [768], replicated, may hold values from 0.1 to 1.9
- second_norm_bias: float32 [768], replicated, may hold values from -1.8 to 1.8
- up_weight: bfloat16 [768, 3072], P(None, 'mp'), may hold values from -0.21875 to 0.21875
- up_bias: float32 [3072], P('mp'), may hold values from -1.8 to 1.8
- down_weight: bfloat16 [3072, 768], P('mp'), may hold values from -0.109375 to 0.109375
- down_bias: float32 [768], replicated, may hold values from -1.8 to 1.8
- out_grad: bfloat16 [16384, 768], P('dp'), may hold values from -6 to 6
Outputs:
- out: bfloat16 [16384, 768], P(('dp', 'mp'))
- patches_grad: bfloat16 [16384, 768], P(('dp', 'mp'))
- first_norm_gain_gradient: float32 [768], replicated
- ln1_bias_grad: float32 [768], replicated
- qkv_weight_grad: float32 [768, 3, 768], P(None, None, 'mp')
- qkv_bias_grad: float32 [3, 768], P(None, 'mp')
- rope_freq_grad: float32 [12, 64], P('mp')
- out_weight_grad: float32 [768, 768], P('mp')
- out_bias_grad: float32 [768], replicated
- second_norm_gain_gradient: float32 [768], replicated
- ln2_bias_grad: float32 [768], replicated
- up_weight_grad: float32 [768, 3072], P(None, 'mp')
- up_bias_grad: float32 [3072], P('mp')
- down_weight_grad: float32 [3072, 768], P('mp')
- down_bias_grad: float32 [768], replicated
The draws below stay inside these ranges and needn't reach their ends.
Inputs may be any that keep to these rules, and one draw needn't show every extreme that they name: `image_ids`: each sequence of 1024 consecutive patches holds 8 images as contiguous runs with ids 0 to 7 in order. `patch_grid`: within an image the patches come in row-major order over a grid of 8 to 32 columns; its last row may be partial.
All inputs are finite; a program needn't handle non-finite values.
Results may differ from the reference program's by a relative error of at most 0.018.
The reference program's roundings to bfloat16 on the way count: a program that leaves them out, or rounds other values in their place, can miss the bound.
Values may be sent and summed in bfloat16 or wider, within the bound.
No kernel may reach another device: no remote copies, remote signals or barrier semaphores. Data moves between devices by JAX's collectives and lax.ppermute only.
A program may use at most 192 MiB of HBM per device.

```python
import math
import jax
import jax.numpy as jnp
from jax import lax

D = 768
HEADS = 12
HD = 64
FF = 3072
LEN = 1024
IMAGES = 8
SEQS = 16
TOKENS = 16384
N_MP = 4


def packing(key):
    base_key = jax.random.fold_in(key, 7)

    def one_sequence(seq_key):
        cut_key, width_key = jax.random.split(seq_key)
        cuts = jnp.sort(jax.random.permutation(cut_key, LEN - 32)[:IMAGES - 1] + 32).astype(jnp.int32)
        spots = jnp.arange(LEN, dtype=jnp.int32)
        image_of = jnp.sum((spots[:, None] >= cuts[None, :]).astype(jnp.int32), axis=1)
        starts = jnp.concatenate([jnp.zeros((1,), jnp.int32), cuts])
        ends = jnp.concatenate([cuts, jnp.full((1,), LEN, jnp.int32)])
        counts = ends - starts
        candidates = jnp.arange(1, LEN + 1, dtype=jnp.int32)
        sides = jnp.sum((candidates[None, :] * candidates[None, :] < counts[:, None]).astype(jnp.int32), axis=1) + 1
        picks = jax.random.randint(width_key, (IMAGES,), 8, 33).astype(jnp.int32)
        widths = jnp.maximum(picks, sides)
        widths = jnp.where(jnp.arange(IMAGES, dtype=jnp.int32) == 0, 32, widths).astype(jnp.int32)
        inside = spots - starts[image_of]
        width_of = widths[image_of]
        return (image_of, inside // width_of, inside % width_of)
    seq_keys = jax.random.split(base_key, SEQS)
    image_of, grid_rows, grid_cols = jax.vmap(one_sequence)(seq_keys)
    return (image_of.reshape(TOKENS), jnp.stack([grid_rows.reshape(TOKENS), grid_cols.reshape(TOKENS)]))


def draw_image_ids(key, part):
    return packing(key)[0]


def draw_patch_grid(key, part):
    return packing(key)[1]


def levels(stream_key, dims, shards, low, largest):
    factor_of = 1.0
    for dim, blocks in shards:
        draws = jax.random.uniform(jax.random.fold_in(jax.random.fold_in(stream_key, 6), dim), (blocks,), jnp.float32, low / len(shards), largest / len(shards))
        factor_of = factor_of * jnp.repeat(jnp.exp(draws), dims[dim] // blocks).reshape((-1,) + (1,) * (len(dims) - 1 - dim))
    return factor_of


def gaussian(own_key, shape, scale, bound, cuts=(), held_as=jnp.bfloat16):
    level = levels(own_key, shape, cuts, -0.22, 0.18) if cuts else 1.0
    array = jax.random.normal(own_key, shape, jnp.float32) * scale * level
    return jnp.minimum(jnp.maximum(array, -bound), bound).astype(held_as)


def setup_inputs(seed: int = 0) -> dict:
    streams_of = jax.random.split(jax.random.key(seed), 18)
    patches = gaussian(streams_of[0], (TOKENS, D), 1.0, 6.0, ((0, 8),))
    image_ids = draw_image_ids(jax.random.fold_in(streams_of[17], 71), 0)
    patch_grid = draw_patch_grid(jax.random.fold_in(streams_of[17], 71), 0)
    first_norm_gain = jnp.clip(1.0 + 0.18 * jax.random.normal(streams_of[3], (D,), jnp.float32), 0.1, 1.9)
    first_norm_bias = gaussian(streams_of[4], (D,), 0.3, 1.8, (), jnp.float32)
    qkv_weight = gaussian(streams_of[5], (D, 3, D), (D // 2) ** -0.5, 0.3125, ((2, 4),))
    qkv_bias = gaussian(streams_of[6], (3, D), 0.3, 1.8, ((1, 4),), jnp.float32)
    rope_freq = jnp.clip(jax.random.uniform(streams_of[7], (HEADS, HD), jnp.float32, -1.0, 1.0) * levels(streams_of[7], (HEADS, HD), ((0, 4),), -0.4, 0.0), -1.0, 1.0)
    out_weight = gaussian(streams_of[8], (D, D), (D // 8) ** -0.5, 0.625, ((0, 4),))
    out_bias = gaussian(streams_of[9], (D,), 0.3, 1.8, (), jnp.float32)
    second_norm_gain = jnp.clip(1.0 + 0.18 * jax.random.normal(streams_of[10], (D,), jnp.float32), 0.1, 1.9)
    second_norm_bias = gaussian(streams_of[11], (D,), 0.3, 1.8, (), jnp.float32)
    up_weight = gaussian(streams_of[12], (D, FF), D ** -0.5, 0.21875, ((1, 4),))
    up_bias = gaussian(streams_of[13], (FF,), 0.3, 1.8, ((0, 4),), jnp.float32)
    down_weight = gaussian(streams_of[14], (FF, D), FF ** -0.5, 0.109375, ((0, 4),))
    down_bias = gaussian(streams_of[15], (D,), 0.3, 1.8, (), jnp.float32)
    out_grad = gaussian(streams_of[16], (TOKENS, D), 1.0, 6.0, ((0, 8),))
    return {"patches": patches, "image_ids": image_ids, "patch_grid": patch_grid, "first_norm_gain": first_norm_gain, "first_norm_bias": first_norm_bias, "qkv_weight": qkv_weight, "qkv_bias": qkv_bias, "rope_freq": rope_freq, "out_weight": out_weight, "out_bias": out_bias, "second_norm_gain": second_norm_gain, "second_norm_bias": second_norm_bias, "up_weight": up_weight, "up_bias": up_bias, "down_weight": down_weight, "down_bias": down_bias, "out_grad": out_grad}


@jax.custom_vjp
def low(v):
    return lax.optimization_barrier(v.astype(jnp.bfloat16)).astype(jnp.float32)

@jax.custom_vjp
def low_back(v):
    return v

def low_keep(v):
    return (low(v), None)

def low_pass(kept, grad):
    return (grad,)

def back_keep(v):
    return (v, None)

def back_low(kept, grad):
    return (low(grad),)
low.defvjp(low_keep, low_pass)
low_back.defvjp(back_keep, back_low)
masked_score = -1e+30
epsilon = 1e-06

def standardize_rows(values, norm_gain, offset):
    center = lax.optimization_barrier(jnp.mean(values, axis=-1, keepdims=True))
    centered = values - center
    spread = lax.optimization_barrier(jnp.mean(centered * centered, axis=-1, keepdims=True))
    return centered * lax.rsqrt(spread + epsilon) * norm_gain + offset

def rotary(values, frequency, row_pos, col_pos):
    half_dim = values.shape[-1] // 2
    angles = col_pos[:, None, None] * frequency[None, :, :half_dim] + row_pos[:, None, None] * frequency[None, :, half_dim:]
    cosine = jnp.cos(angles)
    sine_of = jnp.sin(angles)
    first_half = values[..., :half_dim]
    second_half = values[..., half_dim:]
    return jnp.concatenate([first_half * cosine - second_half * sine_of, first_half * sine_of + second_half * cosine], axis=-1)

def attention(query, keys, values, image_ids):
    highest = lax.Precision.HIGHEST

    def one_sequence(pieces_in):
        query_seq, keys_seq, values_seq, ids_seq = pieces_in
        scores = low_back(jnp.einsum('qhd,khd->hqk', query_seq, keys_seq, precision=highest) * HD ** (-0.5))
        scores = jnp.where((ids_seq[:, None] == ids_seq[None, :])[None], scores, masked_score)
        row_max = lax.optimization_barrier(jnp.max(scores, axis=-1, keepdims=True))
        expo_vals = jnp.exp(scores - row_max)
        probs_low = low(expo_vals / lax.optimization_barrier(jnp.sum(expo_vals, axis=-1, keepdims=True)))
        return jnp.einsum('hqk,khd->qhd', probs_low, values_seq, precision=highest)
    seq_count = query.shape[0] // LEN
    shaped = (query.reshape(seq_count, LEN, HEADS, HD), keys.reshape(seq_count, LEN, HEADS, HD), values.reshape(seq_count, LEN, HEADS, HD), image_ids.reshape(seq_count, LEN))
    return lax.map(jax.checkpoint(one_sequence), shaped).reshape(query.shape)

def block_forward(input_tokens, image_ids, grid, weights):
    first_norm_gain, first_norm_bias, qkv_weight, qkv_bias, rope_freq, out_weight, out_bias, second_norm_gain, second_norm_bias, up_weight, up_bias, down_weight, down_bias = weights
    highest = lax.Precision.HIGHEST
    row_count = input_tokens.shape[0]
    row_pos = grid[0].astype(jnp.float32)
    col_pos = grid[1].astype(jnp.float32)
    first_normalized_rows = low(standardize_rows(input_tokens, first_norm_gain, first_norm_bias))
    mixed = low_back(jnp.einsum('td,dce->tce', first_normalized_rows, qkv_weight, precision=highest) + qkv_bias[None])
    query = low(rotary(mixed[:, 0].reshape(row_count, HEADS, HD), rope_freq, row_pos, col_pos))
    keys = low(rotary(mixed[:, 1].reshape(row_count, HEADS, HD), rope_freq, row_pos, col_pos))
    values = low(mixed[:, 2].reshape(row_count, HEADS, HD))
    context = low(low_back(attention(query, keys, values, image_ids))).reshape(row_count, D)
    group_width = D // N_MP
    attn_total = jnp.zeros_like(input_tokens)
    for group_index in range(N_MP):
        begin_col = group_index * group_width
        attn_total = attn_total + low(jnp.dot(context[:, begin_col:begin_col + group_width], out_weight[begin_col:begin_col + group_width], precision=highest))
    attn_out = low_back(attn_total + out_bias)
    residual = input_tokens + attn_out
    normed_two = low(standardize_rows(residual, second_norm_gain, second_norm_bias))
    hidden_pre = low_back(jnp.dot(normed_two, up_weight, precision=highest) + up_bias)
    hidden = low(jax.nn.gelu(hidden_pre, approximate=False))
    group_units = FF // N_MP
    mlp_total = jnp.zeros_like(input_tokens)
    for group_index in range(N_MP):
        begin_unit = group_index * group_units
        mlp_total = mlp_total + low(jnp.dot(hidden[:, begin_unit:begin_unit + group_units], down_weight[begin_unit:begin_unit + group_units], precision=highest))
    mlp_out = low_back(mlp_total + down_bias)
    return residual + mlp_out

def reference(patches, image_ids, patch_grid, first_norm_gain, first_norm_bias, qkv_weight, qkv_bias, rope_freq, out_weight, out_bias, second_norm_gain, second_norm_bias, up_weight, up_bias, down_weight, down_bias, out_grad):
    params = (first_norm_gain, first_norm_bias, qkv_weight.astype(jnp.float32), qkv_bias, rope_freq, out_weight.astype(jnp.float32), out_bias, second_norm_gain, second_norm_bias, up_weight.astype(jnp.float32), up_bias, down_weight.astype(jnp.float32), down_bias)
    group_seqs = math.gcd(SEQS, 4)
    step_count = SEQS // group_seqs
    group_rows = group_seqs * LEN
    inputs_all = patches.reshape(step_count, group_rows, D)
    ids_all = image_ids.reshape(step_count, group_rows)
    grid_all = patch_grid.reshape(2, step_count, group_rows).transpose(1, 0, 2)
    cots_all = out_grad.reshape(step_count, group_rows, D)

    def scan_step(totals, pieces_in):
        block_in, block_ids, block_grid, block_cot = pieces_in

        def forward_fn(input_tokens, *weights):
            return block_forward(input_tokens, block_ids, block_grid, weights)
        result, pull = jax.vjp(forward_fn, block_in.astype(jnp.float32), *params)
        gradients = pull(block_cot.astype(jnp.float32))
        totals = tuple((before + extra for before, extra in zip(totals, gradients[1:])))
        return (totals, (result.astype(jnp.bfloat16), gradients[0].astype(jnp.bfloat16)))
    start_totals = tuple((jnp.zeros_like(param) for param in params))
    totals, (outputs, input_grads) = lax.scan(scan_step, start_totals, (inputs_all, ids_all, grid_all, cots_all))
    return (outputs.reshape(TOKENS, D), input_grads.reshape(TOKENS, D), totals[0], totals[1], totals[2], totals[3], totals[4], totals[5], totals[6], totals[7], totals[8], totals[9], totals[10], totals[11], totals[12])
```

```python
import functools
import math

import jax
import jax.numpy as jnp
from jax import lax
from jax.experimental import pallas as pl
from jax.experimental.pallas import tpu as pltpu
from jax.sharding import PartitionSpec as P

LEN = 1024
HD = 64
HALF = HD // 2
RB = 256
KB = 256

masked_score = -1e30
epsilon = 1e-06
SCALE = HD ** (-0.5)
SCALE2 = SCALE * math.log2(math.e)
SQRT_HALF = math.sqrt(0.5)
INV_SQRT_2PI = 1.0 / math.sqrt(2.0 * math.pi)

f32 = jnp.float32
bf16 = jnp.bfloat16

NN = (((1,), (0,)), ((), ()))
NT = (((1,), (1,)), ((), ()))
TN = (((0,), (0,)), ((), ()))


def mm(a, b, dims=NN):
    return lax.dot_general(a, b, dims, preferred_element_type=f32)


ANY = pl.BlockSpec(memory_space=pl.ANY)


def ignoring(count, kernel):
    return lambda c_ref, *refs: kernel(c_ref, *refs[count:])


def params(mib):
    return pltpu.CompilerParams(
        dimension_semantics=("arbitrary",), vmem_limit_bytes=mib * 1024 * 1024
    )


def hbm(shape, dtype):
    return pltpu.HBM(shape, dtype)


def stay(*arrays):
    return [pltpu.with_memory_space_constraint(a, pltpu.HBM) for a in arrays]


def cost(flops, nbytes, trans=0):
    return pl.CostEstimate(flops=int(flops), bytes_accessed=int(nbytes), transcendentals=int(trans))


def standardize(values):
    center = jnp.mean(values, axis=-1, keepdims=True)
    centered = values - center
    spread = jnp.mean(centered * centered, axis=-1, keepdims=True)
    inverse = lax.rsqrt(spread + epsilon)
    return centered * inverse, inverse


def column(row):
    n = row.shape[1]
    here = lax.broadcasted_iota(jnp.int32, (n, n), 0) == lax.broadcasted_iota(jnp.int32, (n, n), 1)
    return jnp.sum(jnp.where(here, row, 0.0), axis=1, keepdims=True)


def prepare_kernel(freq_ref, bias_ref, tab_ref, cols_ref):
    heads = freq_ref.shape[0]
    n = heads * HALF
    lane = lax.broadcasted_iota(jnp.int32, (HALF, 128), 1)
    spot = (lane & 31).astype(f32)
    part = lane >> 5
    for h in range(heads):
        freq = column(freq_ref[h : h + 1, :])
        for axis in range(2):
            angle = spot * freq[axis * HALF : (axis + 1) * HALF]
            for k, val in enumerate((jnp.cos(angle), jnp.sin(angle))):
                high = val.astype(bf16).astype(f32)
                rest = val - high
                mid = rest.astype(bf16).astype(f32)
                low = (rest - mid).astype(bf16).astype(f32)
                out = jnp.where(part == 0, high, jnp.where(part == 1, mid, jnp.where(part == 2, low, 0.0)))
                at = (axis * 2 + k) * n + h * HALF
                tab_ref[at : at + HALF, :] = out.astype(bf16)
    width = bias_ref.shape[1]
    for k in range(3):
        for h in range(heads):
            col = column(bias_ref[k : k + 1, h * HD : (h + 1) * HD])
            cols_ref[k * width + h * HD : k * width + (h + 1) * HD, :] = jnp.broadcast_to(col, (HD, 128))


def prepare(freq, bias):
    heads = freq.shape[0]
    return pl.pallas_call(
        prepare_kernel,
        out_shape=[
            jax.ShapeDtypeStruct((4 * heads * HALF, 128), bf16),
            jax.ShapeDtypeStruct((bias.shape[0] * bias.shape[1], 128), f32),
        ],
        name="prepare",
    )(freq, bias)


def lookup(tab_ref, grid_blk):
    n = tab_ref.shape[0] // 4
    rows = grid_blk.shape[1]
    spot = lax.broadcasted_iota(jnp.int32, (128, rows), 0) & 31
    one_r = jnp.where(spot == grid_blk[0:1, :], 1.0, 0.0).astype(bf16)
    one_c = jnp.where(spot == grid_blk[1:2, :], 1.0, 0.0).astype(bf16)
    by_c = mm(tab_ref[0 : 2 * n, :], one_c)
    by_r = mm(tab_ref[2 * n : 4 * n, :], one_r)
    cc, sc = by_c[:n], by_c[n:]
    cr, sr = by_r[:n], by_r[n:]
    return cc * cr - sc * sr, sc * cr + cc * sr


def proj_kernel(c_ref, x_ref, grid_ref, tab_ref, wt_ref, bias_ref, gain_ref, beta_ref, xhat_ref, q_ref, k_ref, v_ref):
    width = q_ref.shape[0]
    xhat, _ = standardize(x_ref[...].astype(f32))
    xhat_ref[...] = xhat.astype(bf16)
    normed = (xhat * gain_ref[...] + beta_ref[...]).astype(bf16)
    mixed = mm(wt_ref[...], normed, NT) + bias_ref[:, 0:1]
    cosine, sine = lookup(tab_ref, grid_ref[...])
    for which, ref in ((0, q_ref), (1, k_ref)):
        for h in range(width // HD):
            at = which * width + h * HD
            a1 = mixed[at : at + HALF]
            a2 = mixed[at + HALF : at + HD]
            c = cosine[h * HALF : (h + 1) * HALF]
            s = sine[h * HALF : (h + 1) * HALF]
            ref[h * HD : h * HD + HALF, :] = (a1 * c - a2 * s).astype(bf16)
            ref[h * HD + HALF : (h + 1) * HD, :] = (a1 * s + a2 * c).astype(bf16)
    v_ref[...] = mixed[2 * width : 3 * width].astype(bf16)


def project(seq, core, patches, grid, tab, wt, bias_cols, gain, beta, wait=()):
    d = patches.shape[1]
    wide = wt.shape[0]
    width = wide // 3
    steps = LEN // RB
    whole = lambda *shape: pl.BlockSpec(shape, lambda i, c: (0,) * len(shape), pipeline_mode=pl.Buffered(1))
    tall = pl.BlockSpec((width, RB), lambda i, c: (0, i))
    return pl.pallas_call(
        ignoring(len(wait), proj_kernel),
        grid_spec=pltpu.PrefetchScalarGridSpec(
            num_scalar_prefetch=1,
            grid=(steps,),
            in_specs=[ANY] * len(wait)
            + [
                pl.BlockSpec((RB, d), lambda i, c: (seq * steps + i, 0)),
                pl.BlockSpec((2, RB), lambda i, c: (0, seq * steps + i)),
                whole(*tab.shape),
                whole(*wt.shape),
                whole(*bias_cols.shape),
                whole(1, d),
                whole(1, d),
            ],
            out_specs=[pl.BlockSpec((RB, d), lambda i, c: (i, 0)), tall, tall, tall],
        ),
        out_shape=[hbm((LEN, d), bf16)] + [jax.ShapeDtypeStruct((width, LEN), bf16)] * 3,
        compiler_params=params(10),
        cost_estimate=cost(2 * LEN * d * wide, 2 * (2 * LEN * d + wide * (d + LEN))),
        name="project",
    )(core, *wait, *stay(patches), grid, tab, wt, bias_cols, gain, beta)


def key_range(ids_all, ids_blk):
    first = jnp.min(ids_blk)
    last = jnp.max(ids_blk)
    start = jnp.sum((ids_all < first).astype(jnp.int32))
    stop = jnp.sum((ids_all <= last).astype(jnp.int32))
    return start // KB, (stop + KB - 1) // KB


def same_image(idc_ref, at, ids_blk):
    ids_k = idc_ref[pl.ds(at, KB), :]
    ids_k = jnp.concatenate([ids_k] * (ids_blk.shape[1] // 128), axis=1)
    return ids_k == ids_blk


def rows_of(ref, h):
    return ref[h * HD : (h + 1) * HD, :]


def attend_kernel(c_ref, q_ref, k_ref, v_ref, idr_ref, idq_ref, idc_ref,
                  send_ref, keep_ref, ctx_ref, lse_ref, keys, scores, acc):
    step = pl.program_id(0)
    heads = q_ref.shape[0] // HD
    half = pl.num_programs(0) // 2

    @pl.when(step == 0)
    def _():
        for h in range(heads):
            keys[h] = jnp.transpose(rows_of(k_ref, h))

    ids_q = idq_ref[...]
    lo, hi = key_range(idr_ref[...], ids_q)

    def first_pass(kb, tops):
        at = pl.multiple_of(kb * KB, KB)
        same = same_image(idc_ref, at, ids_q)
        new = []
        for h in range(heads):
            s = mm(keys[h, pl.ds(at, KB), :], rows_of(q_ref, h))
            s = jnp.where(same, s, masked_score)
            scores[h, pl.ds(at, KB), :] = s
            new.append(jnp.maximum(tops[h], jnp.max(s, axis=0, keepdims=True)))
        return tuple(new)

    tops = lax.fori_loop(lo, hi, first_pass, tuple(jnp.full((1, RB), masked_score, f32) for _ in range(heads)))
    tops = tuple(top * SCALE2 for top in tops)
    acc[...] = jnp.zeros_like(acc)

    def second_pass(kb, totals):
        at = pl.multiple_of(kb * KB, KB)
        new = []
        for h in range(heads):
            p = jnp.exp2(scores[h, pl.ds(at, KB), :] * SCALE2 - tops[h])
            new.append(totals[h] + jnp.sum(p, axis=0, keepdims=True))
            acc[h * HD : (h + 1) * HD, :] += mm(v_ref[h * HD : (h + 1) * HD, pl.ds(at, KB)], p.astype(bf16))
        return tuple(new)

    totals = lax.fori_loop(lo, hi, second_pass, tuple(jnp.zeros((1, RB), f32) for _ in range(heads)))
    lse = jnp.zeros((8, RB), f32)
    row = lax.broadcasted_iota(jnp.int32, (8, RB), 0)
    for h in range(heads):
        ctx_ref[h * HD : (h + 1) * HD, :] = acc[h * HD : (h + 1) * HD, :] * (1.0 / totals[h])
        lse = jnp.where(row == h, tops[h] + jnp.log2(totals[h]), lse)
    lse_ref[...] = lse
    partial = ctx_ref[...].astype(bf16)

    @pl.when(step < half)
    def _():
        send_ref[...] = partial

    @pl.when(step >= half)
    def _():
        keep_ref[...] = partial


def attend(seq, core, q, k, v, ids_rows, ids_cols, wait=()):
    width = q.shape[0]
    steps = LEN // RB
    half = steps // 2
    heads = width // HD
    blk = lambda i, c: lax.rem(i + half * (1 - c[0]), steps)
    whole = lambda *shape: pl.BlockSpec(shape, lambda i, c: (0,) * len(shape), pipeline_mode=pl.Buffered(1))
    return pl.pallas_call(
        ignoring(len(wait), attend_kernel),
        grid_spec=pltpu.PrefetchScalarGridSpec(
            num_scalar_prefetch=1,
            grid=(steps,),
            in_specs=[ANY] * len(wait)
            + [
                pl.BlockSpec((width, RB), lambda i, c: (0, blk(i, c))),
                whole(width, LEN),
                whole(width, LEN),
                pl.BlockSpec((None, 1, LEN), lambda i, c: (seq, 0, 0)),
                pl.BlockSpec((None, 1, RB), lambda i, c: (seq, 0, blk(i, c))),
                pl.BlockSpec((LEN, 128), lambda i, c: (seq, 0)),
            ],
            out_specs=[
                pl.BlockSpec((width, RB), lambda i, c: (0, jnp.minimum(i, half - 1))),
                pl.BlockSpec((width, RB), lambda i, c: (0, jnp.maximum(i - half, 0))),
                pl.BlockSpec((width, RB), lambda i, c: (0, blk(i, c))),
                pl.BlockSpec((8, RB), lambda i, c: (0, blk(i, c))),
            ],
            scratch_shapes=[
                pltpu.VMEM((heads, LEN, HD), bf16),
                pltpu.VMEM((heads, LEN, RB), f32),
                pltpu.VMEM((width, RB), f32),
            ],
        ),
        out_shape=[
            jax.ShapeDtypeStruct((width, LEN // 2), bf16),
            jax.ShapeDtypeStruct((width, LEN // 2), bf16),
            hbm((width, LEN), f32),
            hbm((8, LEN), f32),
        ],
        compiler_params=params(10),
        cost_estimate=cost(8 * LEN * LEN * width, 12 * LEN * width, heads * LEN * LEN),
        name="attend",
    )(core, *wait, q, k, v, ids_rows, ids_rows, ids_cols)


def norm_two_kernel(c_ref, x_ref, *refs):
    groups = (len(refs) - 5) // 2
    ctx_refs, wo_refs = refs[:groups], refs[groups : 2 * groups]
    bias_ref, gain_ref, beta_ref, resid_ref, normed_ref = refs[2 * groups :]
    attn = bias_ref[...]
    for ctx_ref, wo_ref in zip(ctx_refs, wo_refs):
        attn = attn + mm(ctx_ref[...], wo_ref[...], TN).astype(bf16).astype(f32)
    resid = x_ref[...].astype(f32) + attn
    resid_ref[...] = resid
    xhat, _ = standardize(resid)
    normed_ref[...] = (xhat * gain_ref[...] + beta_ref[...]).astype(bf16)


def norm_two(seq, core, patches, ctxs, wos, bias, gain, beta, wait=()):
    width, rows = ctxs[0].shape
    d = patches.shape[1]
    steps = rows // RB
    blk = pl.BlockSpec((RB, d), lambda i, c: (i, 0))
    whole = lambda *shape: pl.BlockSpec(shape, lambda i, c: (0,) * len(shape), pipeline_mode=pl.Buffered(1))
    return pl.pallas_call(
        ignoring(len(wait), norm_two_kernel),
        grid_spec=pltpu.PrefetchScalarGridSpec(
            num_scalar_prefetch=1,
            grid=(steps,),
            in_specs=[ANY] * len(wait)
            + [pl.BlockSpec((RB, d), lambda i, c: ((2 * seq + c[0]) * steps + i, 0))]
            + [pl.BlockSpec((width, RB), lambda i, c: (0, i))] * len(ctxs)
            + [whole(width, d)] * len(wos)
            + [whole(1, d)] * 3,
            out_specs=[blk, blk],
        ),
        out_shape=[hbm((rows, d), f32), jax.ShapeDtypeStruct((rows, d), bf16)],
        compiler_params=params(10),
        cost_estimate=cost(2 * len(ctxs) * rows * d * width, 12 * rows * d),
        name="norm_two",
    )(core, *wait, *stay(patches), *ctxs, *wos, bias, gain, beta)


def store_halves(mine, outs, sums):
    count = outs[0].shape[0]
    for out, half in zip(outs, (1 - mine, mine)):
        for k in range(count):
            at = 0
            for acc in sums:
                rows = acc.shape[0] // (2 * count)
                spot = pl.ds(pl.multiple_of((half * count + k) * rows, 8), rows)
                out[k, at : at + rows, :] = acc[spot, :].astype(bf16)
                at += rows


def feed_kernel(first, last, c_ref, *refs):
    refs = list(refs)
    own_ref, other_ref, og_ref, up_ref, upb_ref, down_ref = refs[:6]
    refs = refs[6:]
    if not first:
        small0_ref, up0_ref, down0_ref = refs[:3]
        refs = refs[3:]
    mlp_send, mlp_keep, n2_send, n2_keep, small_out = refs[:5]
    outs = refs[5:-4]
    up_acc, down_acc, up_sum, down_sum = refs[-4:]
    step = pl.program_id(0)
    steps = pl.num_programs(0)
    half = steps // 2

    @pl.when(step == 0)
    def _():
        if first:
            up_acc[...] = jnp.zeros_like(up_acc)
            down_acc[...] = jnp.zeros_like(down_acc)
            up_sum[...] = jnp.zeros_like(up_sum)
            down_sum[...] = jnp.zeros_like(down_sum)
        else:
            up_acc[...] = up0_ref[...]
            down_acc[...] = down0_ref[...]
            up_sum[...] = small0_ref[0:1, :]
            down_sum[...] = small0_ref[1:2, :]

    normed = jnp.where(step < half, other_ref[...], own_ref[...])
    og = og_ref[...]
    pre = mm(normed, up_ref[...]) + upb_ref[...]
    phi_cap = 0.5 * (1.0 + lax.erf(pre * SQRT_HALF))
    hidden = (pre * phi_cap).astype(bf16)
    mlp = mm(hidden, down_ref[...]).astype(bf16)
    slope = phi_cap + pre * (jnp.exp(-0.5 * pre * pre) * INV_SQRT_2PI)
    grad = mm(og, down_ref[...], NT)
    pre_grad = (grad * slope).astype(bf16)
    n2 = mm(pre_grad, up_ref[...], NT).astype(bf16)
    down_acc[...] += mm(hidden, og, TN)
    up_acc[...] += mm(normed, pre_grad, TN)
    up_sum[...] += jnp.sum(pre_grad.astype(f32), axis=0, keepdims=True)
    down_sum[...] += jnp.sum(og.astype(f32), axis=0, keepdims=True)

    @pl.when(step < half)
    def _():
        mlp_send[...] = mlp
        n2_send[...] = n2

    @pl.when(step >= half)
    def _():
        mlp_keep[...] = mlp
        n2_keep[...] = n2

    @pl.when(step == steps - 1)
    def _():
        if last:
            store_halves(c_ref[1], outs, (up_acc, down_acc))
        else:
            outs[0][...] = up_acc[...]
            outs[1][...] = down_acc[...]
        small_out[0:1, :] = up_sum[...]
        small_out[1:2, :] = down_sum[...]
        small_out[2:8, :] = jnp.zeros((6, up_sum.shape[1]), f32)


def feed(seq, core, own, other, out_grad, up, up_bias, down, before=None, last=0, wait=()):
    d, units = up.shape
    steps = LEN // RB
    half = steps // 2
    first = before is None
    whole = lambda *shape: pl.BlockSpec(shape, lambda i, c: (0,) * len(shape), pipeline_mode=pl.Buffered(1))
    low = pl.BlockSpec((RB, d), lambda i, c: (jnp.minimum(i, half - 1), 0))
    high = pl.BlockSpec((RB, d), lambda i, c: (jnp.maximum(i - half, 0), 0))
    blk = lambda i, c: seq * steps + lax.rem(i + half * (1 - c[0]), steps)
    in_specs = [ANY] * len(wait) + [
        high, low,
        pl.BlockSpec((RB, d), lambda i, c: (blk(i, c), 0)),
        whole(d, units), whole(1, units), whole(units, d),
    ]
    args = [core, *wait, own, other, *stay(out_grad), up, up_bias, down]
    if not first:
        in_specs += [whole(8, d), whole(d, units), whole(units, d)]
        args += list(before)
    if last:
        grads = [(last, (d + units) // (2 * last), d)] * 2
        kind = bf16
    else:
        grads = [(d, units), (units, d)]
        kind = f32
    rows = jax.ShapeDtypeStruct((LEN // 2, d), bf16)
    return pl.pallas_call(
        ignoring(len(wait), functools.partial(feed_kernel, first, last)),
        grid_spec=pltpu.PrefetchScalarGridSpec(
            num_scalar_prefetch=1,
            grid=(steps,),
            in_specs=in_specs,
            out_specs=[low, high, low, high, whole(8, d)] + [whole(*g) for g in grads],
            scratch_shapes=[
                pltpu.VMEM((d, units), f32),
                pltpu.VMEM((units, d), f32),
                pltpu.VMEM((1, units), f32),
                pltpu.VMEM((1, d), f32),
            ],
        ),
        out_shape=[hbm(rows.shape, bf16), hbm(rows.shape, bf16), rows, rows, hbm((8, d), f32)]
        + [hbm(g, kind) for g in grads],
        compiler_params=params(28),
        cost_estimate=cost(12 * LEN * d * units, 2 * LEN * d * 4 + 12 * d * units, 2 * LEN * units),
        name="feed",
    )(*args)


def norm_two_back_kernel(first, c_ref, *refs):
    refs = list(refs)
    mine_ref, theirs_ref, resid_ref, og_ref, gain_ref = refs[:5]
    refs = refs[5:]
    if not first:
        small0_ref = refs[0]
        refs = refs[1:]
    rgrad_ref, branch_ref, small_ref = refs
    step = pl.program_id(0)

    @pl.when(step == 0)
    def _():
        if first:
            small_ref[...] = jnp.zeros_like(small_ref)
        else:
            small_ref[...] = small0_ref[...]

    grad = mine_ref[...].astype(f32) + theirs_ref[...].astype(f32)
    xhat, inverse = standardize(resid_ref[...])
    e = grad * gain_ref[...]
    back = inverse * (
        e - jnp.mean(e, axis=-1, keepdims=True) - xhat * jnp.mean(e * xhat, axis=-1, keepdims=True)
    )
    rgrad = og_ref[...].astype(f32) + back
    rgrad_ref[...] = rgrad
    branch = rgrad.astype(bf16)
    branch_ref[...] = branch
    small_ref[0:1, :] += jnp.sum(grad * xhat, axis=0, keepdims=True)
    small_ref[1:2, :] += jnp.sum(grad, axis=0, keepdims=True)
    small_ref[2:3, :] += jnp.sum(branch.astype(f32), axis=0, keepdims=True)


def norm_two_back(seq, core, mine, theirs, resid, out_grad, gain, before=None, wait=()):
    rows, d = mine.shape
    steps = rows // RB
    first = before is None
    blk = pl.BlockSpec((RB, d), lambda i, c: (i, 0))
    vec = pl.BlockSpec((1, d), lambda i, c: (0, 0))
    small = pl.BlockSpec((8, d), lambda i, c: (0, 0))
    in_specs = [ANY] * len(wait) + [blk, blk, blk, pl.BlockSpec((RB, d), lambda i, c: ((2 * seq + c[0]) * steps + i, 0)), vec]
    args = [core, *wait, mine, theirs, *stay(resid, out_grad), gain]
    if not first:
        in_specs.append(small)
        args.append(before)
    return pl.pallas_call(
        ignoring(len(wait), functools.partial(norm_two_back_kernel, first)),
        grid_spec=pltpu.PrefetchScalarGridSpec(
            num_scalar_prefetch=1, grid=(steps,), in_specs=in_specs, out_specs=[blk, blk, small]
        ),
        out_shape=[
            hbm((rows, d), f32),
            jax.ShapeDtypeStruct((rows, d), bf16),
            hbm((8, d), f32),
        ],
        compiler_params=params(12),
        cost_estimate=cost(20 * rows * d, 16 * rows * d),
        name="norm_two_back",
    )(*args)


def attend_back_kernel(first, pieces, c_ref, *refs):
    refs = list(refs)
    (own_ref, other_ref, q_ref, k_ref, v_ref, ctx_ref, lse_ref, idr_ref, idq_ref, idc_ref, wo_ref,
     wt_ref, tab_ref, grid_ref, xhat_ref, gain_ref, beta_ref) = refs[:17]
    refs = refs[17:]
    if not first:
        dwt0_ref, dwo0_ref, row0_ref, col0_ref, rope0_ref = refs[:5]
        refs = refs[5:]
    if pieces:
        small_two_ref, small_feed_ref, send_ref, keep_ref, small_ref = refs[:5]
        outs = refs[5:7]
        bucket = refs[7]
        refs = refs[8:]
        keys, vals, dq, dk, dv, dwt_acc, dwo_acc, row_acc, col_acc, rope_acc = refs
    else:
        send_ref, keep_ref, dwt_acc, dwo_acc, row_acc, col_acc, rope_acc = refs[:7]
        refs = refs[7:]
        keys, vals, dq, dk, dv = refs
    step = pl.program_id(0)
    steps = pl.num_programs(0) // 2
    half = steps // 2
    width = q_ref.shape[0]
    heads = width // HD
    c = c_ref[0]
    blk = lax.rem(step + half * (1 - c), steps)
    here = pl.ds(pl.multiple_of(blk * RB, RB), RB)

    @pl.when(step == 0)
    def _():
        for h in range(heads):
            keys[h] = jnp.transpose(rows_of(k_ref, h))
            vals[h] = jnp.transpose(rows_of(v_ref, h))
        dq[...] = jnp.zeros_like(dq)
        dk[...] = jnp.zeros_like(dk)
        dv[...] = jnp.zeros_like(dv)
        if first:
            dwt_acc[...] = jnp.zeros_like(dwt_acc)
            dwo_acc[...] = jnp.zeros_like(dwo_acc)
            row_acc[...] = jnp.zeros_like(row_acc)
            col_acc[...] = jnp.zeros_like(col_acc)
            rope_acc[...] = jnp.zeros_like(rope_acc)
        else:
            dwt_acc[...] = dwt0_ref[...]
            dwo_acc[...] = dwo0_ref[...]
            row_acc[...] = row0_ref[...]
            col_acc[...] = col0_ref[...]
            rope_acc[...] = rope0_ref[...]

    @pl.when(step < steps)
    def _():
        branch = jnp.where(step < half, other_ref[...], own_ref[...])
        ctx = ctx_ref[:, here]
        dctx = mm(wo_ref[...], branch, NT).astype(bf16)
        dwo_acc[...] += mm(ctx.astype(bf16), branch)
        prod = dctx.astype(f32) * ctx
        lse = lse_ref[:, here]
        ids_q = idq_ref[...]
        lo, hi = key_range(idr_ref[...], ids_q)
        parts = []
        for h in range(heads):
            sl = slice(h * HD, (h + 1) * HD)
            parts.append((q_ref[sl, here], dctx[sl], jnp.sum(prod[sl], axis=0, keepdims=True), lse[h : h + 1]))

        def body(kb, carry):
            at = pl.multiple_of(kb * KB, KB)
            there = pl.ds(at, KB)
            same = same_image(idc_ref, at, ids_q)
            for h in range(heads):
                sl = slice(h * HD, (h + 1) * HD)
                q_h, do_h, delta, lse_h = parts[h]
                s = mm(keys[h, there, :], q_h)
                p = jnp.exp2(jnp.where(same, s * SCALE2 - lse_h, masked_score))
                dp = mm(vals[h, there, :], do_h)
                ds = (p * (dp - delta)).astype(bf16)
                dq[sl, here] += mm(k_ref[sl, there], ds)
                dk[sl, there] += mm(q_h, ds, NT)
                dv[sl, there] += mm(do_h, p.astype(bf16), NT)
            return carry

        lax.fori_loop(lo, hi, body, 0)

    @pl.when(step >= steps)
    def _():
        place = grid_ref[...]
        cosine, sine = lookup(tab_ref, place)
        pieces = []
        angle = [None] * heads
        for turned, grads in ((q_ref, dq), (k_ref, dk)):
            for h in range(heads):
                b = grads[h * HD : (h + 1) * HD, here] * SCALE
                a = turned[h * HD : (h + 1) * HD, here].astype(f32)
                b1, b2 = b[:HALF], b[HALF:]
                co = cosine[h * HALF : (h + 1) * HALF]
                si = sine[h * HALF : (h + 1) * HALF]
                pieces.append((b1 * co + b2 * si).astype(bf16))
                pieces.append((b2 * co - b1 * si).astype(bf16))
                term = b2 * a[:HALF] - b1 * a[HALF:]
                angle[h] = term if angle[h] is None else angle[h] + term
        pieces.append(dv[:, here].astype(bf16))
        mixed_grad = jnp.concatenate(pieces, axis=0)
        angle = jnp.concatenate(angle, axis=0)
        rope_acc[...] += lax.dot_general(
            place.astype(f32), angle, NT, precision=lax.Precision.HIGHEST, preferred_element_type=f32
        )
        row_acc[...] += mm(jnp.ones((8, RB), bf16), mixed_grad, NT)
        col_acc[...] += mm(mixed_grad, jnp.ones((RB, 128), bf16))
        dwt_acc[...] += mm(mixed_grad, xhat_ref[...])
        partial = mm(mixed_grad, wt_ref[...], TN).astype(bf16)

        @pl.when(step < steps + half)
        def _():
            send_ref[...] = partial

        @pl.when(step >= steps + half)
        def _():
            keep_ref[...] = partial

    if pieces:
        @pl.when(step == 2 * steps - 1)
        def _():
            raw = dwt_acc[...]
            col = col_acc[:, 0:1]
            wt = wt_ref[...].astype(f32)
            bucket[...] = raw * gain_ref[...] + col * beta_ref[...]
            store_halves(c_ref[1], outs, (bucket, dwo_acc))
            small_ref[0:1, :] = jnp.sum(wt * raw, axis=0, keepdims=True)
            small_ref[1:2, :] = jnp.sum(wt * col, axis=0, keepdims=True)
            small_ref[2:5, :] = 0.5 * small_two_ref[0:3, :]
            small_ref[5:7, :] = small_feed_ref[0:2, :]
            small_ref[7:8, :] = jnp.concatenate(
                [row_acc[0:1, :], rope_acc[1:2, :], rope_acc[0:1, :]], axis=1
            )


def attend_back(seq, core, own, other, q, k, v, ctx, lse, ids_rows, ids_cols, wo, wt, tab, grid, xhat,
                gain, beta, before=None, pieces=0, small_two=None, small_feed=None, wait=()):
    width, d = wo.shape
    heads = width // HD
    steps = LEN // RB
    half = steps // 2
    first = before is None
    whole = lambda *shape: pl.BlockSpec(shape, lambda i, c: (0,) * len(shape), pipeline_mode=pl.Buffered(1))
    blk = lambda i, c: lax.rem(i + half * (1 - c[0]), steps)
    in_specs = [ANY] * len(wait) + [
        pl.BlockSpec((RB, d), lambda i, c: (jnp.clip(i - half, 0, half - 1), 0)),
        pl.BlockSpec((RB, d), lambda i, c: (jnp.minimum(i, half - 1), 0)),
        whole(width, LEN), whole(width, LEN), whole(width, LEN), whole(width, LEN), whole(8, LEN),
        pl.BlockSpec((None, 1, LEN), lambda i, c: (seq, 0, 0)),
        pl.BlockSpec((None, 1, RB), lambda i, c: (seq, 0, blk(i, c))),
        pl.BlockSpec((LEN, 128), lambda i, c: (seq, 0)),
        whole(width, d), whole(3 * width, d), whole(*tab.shape),
        pl.BlockSpec((2, RB), lambda i, c: (0, seq * steps + blk(i, c))),
        pl.BlockSpec((RB, d), lambda i, c: (jnp.where(i < steps, blk(0, c), blk(i, c)), 0)),
        whole(1, d), whole(1, d),
    ]
    args = [core, *wait, own, other, q, k, v, ctx, lse, ids_rows, ids_rows, ids_cols, wo, wt, tab, grid, xhat, gain, beta]
    sums = [(3 * width, d), (width, d), (8, 3 * width), (3 * width, 128), (2, heads * HALF)]
    if not first:
        in_specs += [whole(*s) for s in sums]
        args += list(before)
    if pieces:
        in_specs += [whole(8, d)] * 2
        args += [small_two, small_feed]
    out_specs = [
        pl.BlockSpec((RB, d), lambda i, c: (jnp.clip(i - steps, 0, half - 1), 0)),
        pl.BlockSpec((RB, d), lambda i, c: (jnp.clip(i - steps - half, 0, half - 1), 0)),
    ]
    out_shape = [jax.ShapeDtypeStruct((LEN // 2, d), bf16)] * 2
    scratch = [
        pltpu.VMEM((heads, LEN, HD), bf16),
        pltpu.VMEM((heads, LEN, HD), bf16),
        pltpu.VMEM((width, LEN), f32),
        pltpu.VMEM((width, LEN), f32),
        pltpu.VMEM((width, LEN), f32),
    ]
    if pieces:
        cut = (pieces, 4 * width // (2 * pieces), d)
        out_specs += [whole(8, d), whole(*cut), whole(*cut)]
        out_shape += [hbm((8, d), f32), hbm(cut, bf16), hbm(cut, bf16)]
        scratch = [pltpu.VMEM((3 * width, d), f32)] + scratch + [pltpu.VMEM(s, f32) for s in sums]
    else:
        out_specs += [whole(*s) for s in sums]
        out_shape += [hbm(s, f32) for s in sums]
    return pl.pallas_call(
        ignoring(len(wait), functools.partial(attend_back_kernel, first, pieces)),
        grid_spec=pltpu.PrefetchScalarGridSpec(
            num_scalar_prefetch=1, grid=(2 * steps,), in_specs=in_specs, out_specs=out_specs, scratch_shapes=scratch
        ),
        out_shape=out_shape,
        compiler_params=params(28),
        cost_estimate=cost(
            20 * LEN * LEN * width + 20 * LEN * d * width, 2 * LEN * (6 * width + 3 * d) + 16 * d * width,
            heads * LEN * LEN,
        ),
        name="attend_back",
    )(*args)


def norm_one_back_kernel(m_ref, mine_ref, theirs_ref, x_ref, rg0_ref, rg1_ref, gain_ref, out_ref):
    f = (mine_ref[...].astype(f32) + theirs_ref[...].astype(f32)) * gain_ref[...]
    xhat, inverse = standardize(x_ref[...].astype(f32))
    back = inverse * (
        f - jnp.mean(f, axis=-1, keepdims=True) - xhat * jnp.mean(f * xhat, axis=-1, keepdims=True)
    )
    rgrad = jnp.where(m_ref[0] < 2, rg0_ref[...], rg1_ref[...])
    out_ref[...] = (rgrad + back).astype(bf16)


def norm_one_back(place, mine, theirs, patches, rg0, rg1, gain):
    rows, d = mine.shape
    steps = rows // RB
    blk = pl.BlockSpec((RB, d), lambda i, m: (i, 0))
    return pl.pallas_call(
        norm_one_back_kernel,
        grid_spec=pltpu.PrefetchScalarGridSpec(
            num_scalar_prefetch=1,
            grid=(steps,),
            in_specs=[
                blk, blk, pl.BlockSpec((RB, d), lambda i, m: (m[0] * steps + i, 0)), blk, blk,
                pl.BlockSpec((1, d), lambda i, m: (0, 0)),
            ],
            out_specs=blk,
        ),
        out_shape=jax.ShapeDtypeStruct((rows, d), bf16),
        compiler_params=params(12),
        cost_estimate=cost(20 * rows * d, 16 * rows * d),
        name="norm_one_back",
    )(place, mine, theirs, *stay(patches, rg0, rg1), gain)


CORE_SWAP = [(i, i ^ 1) for i in range(4)]
CHIP_SWAP = [(i, i ^ 2) for i in range(4)]


def core_swap(value):
    return lax.ppermute(value, "mp", CORE_SWAP)


def chip_swap(value):
    return lax.ppermute(value, "mp", CHIP_SWAP)


def after(value, *events):
    return lax.optimization_barrier((value, *events))[0]


def add_low(a, b):
    return (a.astype(f32) + b.astype(f32)).astype(bf16)


def add_kernel(c_ref, a_ref, b_ref, out_ref):
    out_ref[...] = (a_ref[...].astype(f32) + b_ref[...].astype(f32)).astype(bf16)


def full(shape):
    return pl.BlockSpec(shape, lambda i, c: (0,) * len(shape))


def add_parts(core, a, b, wait=()):
    return pl.pallas_call(
        ignoring(len(wait), add_kernel),
        grid_spec=pltpu.PrefetchScalarGridSpec(
            num_scalar_prefetch=1, grid=(1,), in_specs=[ANY] * len(wait) + [full(a.shape)] * 2, out_specs=full(a.shape),
        ),
        out_shape=jax.ShapeDtypeStruct(a.shape, bf16),
        compiler_params=params(12),
        cost_estimate=cost(a.size, 6 * a.size),
        name="add_parts",
    )(core, *wait, a, b)


def sum_parts_kernel(c_ref, parts_ref, *refs):
    out_ref = refs[-1]
    total = parts_ref[0].astype(f32)
    for k in range(1, parts_ref.shape[0]):
        total = total + parts_ref[k].astype(f32)
    rows = total.shape[0]
    total = total.astype(bf16)
    for k in range(out_ref.shape[0]):
        out_ref[k, 0:rows, :] = total
    if len(refs) > 1:
        small = refs[0][...]
        high = small.astype(bf16)
        low = (small - high.astype(f32)).astype(bf16)
        for k in range(out_ref.shape[0]):
            out_ref[k, rows : rows + 8, :] = high
            out_ref[k, rows + 8 : rows + 16, :] = low


def sum_parts(core, parts, small=None, copies=None, wait=()):
    count, rows, d = parts.shape
    extra = () if small is None else (small,)
    out = (copies or count, rows + 16 * len(extra), d)
    return pl.pallas_call(
        ignoring(len(wait), sum_parts_kernel),
        grid_spec=pltpu.PrefetchScalarGridSpec(
            num_scalar_prefetch=1, grid=(1,),
            in_specs=[ANY] * len(wait) + [full(parts.shape)] + [full(e.shape) for e in extra],
            out_specs=full(out),
        ),
        out_shape=jax.ShapeDtypeStruct(out, bf16),
        compiler_params=params(12),
        cost_estimate=cost(count * rows * d, 4 * count * rows * d),
        name="sum_parts",
    )(core, *wait, parts, *extra)


def place_parts_kernel(with_small, c_ref, mine_ref, theirs_ref, *refs):
    outs = refs[: len(refs) - with_small]
    count = mine_ref.shape[0]
    small = None
    for ref, half in ((mine_ref, c_ref[1]), (theirs_ref, 1 - c_ref[1])):
        for k in range(count):
            at = 0
            for out in outs:
                rows = out.shape[0] // (2 * count)
                spot = pl.ds(pl.multiple_of((half * count + k) * rows, 8), rows)
                out[spot, :] = ref[k, at : at + rows, :].astype(f32)
                at += rows
            if with_small:
                part = ref[k, at : at + 8, :].astype(f32) + ref[k, at + 8 : at + 16, :].astype(f32)
                small = part if small is None else small + part
    if with_small:
        refs[-1][...] = small


def place_parts(core, mine, theirs, splits, with_small=False):
    d = mine.shape[2]
    shapes = [(rows, d) for rows in splits] + [(8, d)] * with_small
    return pl.pallas_call(
        functools.partial(place_parts_kernel, with_small),
        grid_spec=pltpu.PrefetchScalarGridSpec(
            num_scalar_prefetch=1, grid=(1,), in_specs=[full(mine.shape)] * 2, out_specs=[full(t) for t in shapes],
        ),
        out_shape=[jax.ShapeDtypeStruct(t, f32) for t in shapes],
        compiler_params=params(20),
        cost_estimate=cost(sum(splits) * d, 6 * sum(splits) * d),
        name="place_parts",
    )(core, mine, theirs)


def place_all_kernel(parts_ref, *outs):
    count = parts_ref.shape[0]
    for k in range(count):
        piece = (k % 2) * (count // 2) + k // 2
        at = 0
        for out in outs:
            rows = out.shape[0] // count
            out[piece * rows : (piece + 1) * rows, :] = parts_ref[k, at : at + rows, :].astype(f32)
            at += rows


def place_all(parts, splits):
    d = parts.shape[2]
    return pl.pallas_call(
        place_all_kernel,
        out_shape=[jax.ShapeDtypeStruct((rows, d), f32) for rows in splits],
        compiler_params=pltpu.CompilerParams(vmem_limit_bytes=20 * 1024 * 1024),
        cost_estimate=cost(sum(splits) * d, 6 * sum(splits) * d),
        name="place_all",
    )(parts)


def half_swap(value):
    return lax.ppermute(value, "dp", [(i, i ^ 1) for i in range(lax.axis_size("dp"))])


def quarter_trade(parts):
    return lax.all_to_all(parts, "dp", 0, 0, axis_index_groups=[[0, 2, 4, 6], [1, 3, 5, 7]])


def hold(values, *events):
    return list(lax.optimization_barrier((*values, *events))[: len(values)])


def local(patches, image_ids, patch_grid, first_norm_gain, first_norm_bias, qkv_weight, qkv_bias, rope_freq,
          out_weight, out_bias, second_norm_gain, second_norm_bias, up_weight, up_bias, down_weight, down_bias,
          out_grad):
    all_rows, d = patches.shape
    seqs = all_rows // LEN
    assert lax.axis_size("mp") == 4 and seqs == 2
    devices = lax.axis_size("dp")
    tree = devices == 8
    pieces = 4 if tree else 1
    heads = rope_freq.shape[0]
    width = heads * HD
    units = up_weight.shape[1]
    place = lax.axis_index("mp").astype(jnp.int32)
    half = lax.axis_index("dp").astype(jnp.int32) % 2 if tree else jnp.int32(0)
    core = jnp.stack([place % 2, half])
    place_arr = place.reshape(1)
    far = place >= 2
    row = lambda v: v.reshape(1, -1)

    tab, bias_cols = prepare(rope_freq, qkv_bias)
    wt = qkv_weight.transpose(1, 2, 0).reshape(3 * width, d)
    ids_rows = image_ids.reshape(seqs, 1, LEN)
    ids_cols = jnp.broadcast_to(image_ids[:, None], (all_rows, 128))
    gain1, beta1 = row(first_norm_gain), row(first_norm_bias)
    gain2, beta2 = row(second_norm_gain), row(second_norm_bias)

    wo_core = core_swap(out_weight)
    proj_args = (patches, patch_grid, tab, wt, bias_cols, gain1, beta1)
    made0 = project(0, core, *proj_args)
    send0, keep0, ctx0, lse0 = attend(0, core, *made0[1:], ids_rows, ids_cols)
    core0, far_keep0 = core_swap(send0), chip_swap(keep0)
    made1 = project(1, core, *proj_args, wait=[keep0, wo_core])
    far_core0, wo_far = chip_swap(core0), chip_swap(out_weight)
    send1, keep1, ctx1, lse1 = attend(1, core, *made1[1:], ids_rows, ids_cols, wait=[core0, far_keep0])
    core1, far_keep1 = core_swap(send1), chip_swap(keep1)
    wos = [out_weight, wo_core, wo_far, core_swap(wo_far)]
    norm_args = (row(out_bias), gain2, beta2)
    resid0, normed0 = norm_two(
        0, core, patches, [keep0, core0, far_keep0, far_core0], wos, *norm_args, wait=[keep1]
    )
    far_core1 = chip_swap(core1)
    feed_args = (out_grad, up_weight, row(up_bias), down_weight)
    mlp_send0, mlp_keep0, n2_send0, n2_keep0, *sums = feed(
        0, core, normed0, core_swap(normed0), *feed_args, wait=[core1, far_keep1]
    )
    n20 = add_low(n2_keep0, core_swap(n2_send0))
    resid1, normed1 = norm_two(
        1, core, patches, [keep1, core1, far_keep1, far_core1], wos, *norm_args, wait=[n2_keep0]
    )
    n2_far0 = chip_swap(n20)
    mlp_send1, mlp_keep1, n2_send1, n2_keep1, small_feed, feed_send, feed_keep = feed(
        1, core, normed1, core_swap(normed1), *feed_args, before=sums, last=pieces, wait=[n20]
    )
    if tree:
        feed_got = half_swap(feed_send)
    n21 = add_low(n2_keep1, core_swap(n2_send1))
    mlp0 = add_low(mlp_keep0, core_swap(mlp_send0))
    mlp1 = add_low(mlp_keep1, core_swap(mlp_send1))
    mlp_away, mlp_mine = jnp.where(far, mlp0, mlp1), jnp.where(far, mlp1, mlp0)
    rgrad0, branch0, small_two = norm_two_back(
        0, core, n20, n2_far0, resid0, out_grad, gain2, wait=[n2_keep1]
    )
    n2_far1 = chip_swap(n21)
    shared_args = (ids_rows, ids_cols, out_weight, wt, tab, patch_grid)
    n1_send0, n1_keep0, *sums = attend_back(
        0, core, branch0, core_swap(branch0), *made0[1:], ctx0, lse0, *shared_args, made0[0], gain1, beta1,
        wait=[n21],
    )
    n1_core0 = core_swap(n1_send0)
    after_first = [n1_keep0]
    if tree:
        feed_part = add_parts(core, feed_keep, feed_got, wait=[n1_keep0])
        after_first = [feed_part]
        feed_got = quarter_trade(feed_part)
    rgrad1, branch1, small_two = norm_two_back(
        1, core, n21, n2_far1, resid1, out_grad, gain2, before=small_two, wait=after_first
    )
    mlp_theirs = chip_swap(mlp_away)
    n1_send1, n1_keep1, *sums = attend_back(
        1, core, branch1, core_swap(branch1), *made1[1:], ctx1, lse1, *shared_args, made1[0], gain1, beta1,
        before=sums, pieces=pieces, small_two=small_two, small_feed=small_feed, wait=[n1_core0, mlp_away],
    )
    small, grad_send, grad_keep = hold(sums, mlp_theirs)
    halves = [add_low(n1_keep0, n1_core0), add_low(n1_keep1, core_swap(n1_send1))]
    shared = lax.broadcasted_iota(jnp.int32, small.shape, 0) < 5
    for swap in (core_swap, chip_swap):
        small = small + jnp.where(shared, swap(small), 0.0)
    away = after(jnp.where(far, halves[0], halves[1]), small)
    mine = jnp.where(far, halves[1], halves[0])
    theirs = chip_swap(away)
    if tree:
        grad_got = half_swap(grad_send)
        feed_all = lax.all_gather(sum_parts(core, feed_got, copies=1, wait=[grad_keep]), "dp", axis=0, tiled=True)
        grad_got = quarter_trade(add_parts(core, grad_keep, grad_got))
        grad_sum = quarter_trade(sum_parts(core, grad_got, small))
        grad_other = half_swap(grad_sum)
    else:
        small, grad_send, grad_keep, feed_send, feed_keep = lax.psum(
            (small, grad_send, grad_keep, feed_send, feed_keep), "dp"
        )
        feed_all = jnp.concatenate([feed_keep, feed_send])
        grad_sum = sum_parts(core, grad_keep, small)
        grad_other = sum_parts(core, grad_send, jnp.zeros_like(small))

    out_rows = (
        jnp.where(far, resid1, resid0)
        + (mlp_mine.astype(f32) + mlp_theirs.astype(f32))
        + row(down_bias)
    ).astype(bf16)
    grad_rows = norm_one_back(place_arr, mine, theirs, patches, rgrad0, rgrad1, gain1)
    up_grad, down_grad = place_all(feed_all, (d, units))
    (grad_other,) = hold([grad_other], grad_rows)
    qkv_grad, out_grad_w, small = place_parts(core, grad_sum, grad_other, (3 * width, width), True)
    turns = heads * HALF
    by_col = small[7, 3 * width : 3 * width + turns].reshape(heads, HALF)
    by_row = small[7, 3 * width + turns : 3 * width + 2 * turns].reshape(heads, HALF)
    return (
        out_rows,
        grad_rows,
        small[0],
        small[1],
        qkv_grad.reshape(3, width, d).transpose(2, 0, 1),
        small[7, : 3 * width].reshape(3, width),
        jnp.concatenate([by_col, by_row], axis=-1),
        out_grad_w,
        small[4],
        small[2],
        small[3],
        up_grad,
        small[5],
        down_grad,
        small[6],
    )


def solution(mesh):
    placed = (
        P("dp", None),
        P("dp"),
        P(None, "dp"),
        P(),
        P(),
        P(None, None, "mp"),
        P(None, "mp"),
        P("mp", None),
        P("mp", None),
        P(),
        P(),
        P(),
        P(None, "mp"),
        P("mp"),
        P("mp", None),
        P(),
        P("dp", None),
    )
    return jax.shard_map(
        local,
        mesh=mesh,
        in_specs=placed,
        out_specs=(
            P(("dp", "mp"), None),
            P(("dp", "mp"), None),
            P(),
            P(),
            P(None, None, "mp"),
            P(None, "mp"),
            P("mp", None),
            P("mp", None),
            P(),
            P(),
            P(),
            P(None, "mp"),
            P("mp"),
            P("mp", None),
            P(),
        ),
        check_vma=False,
    )
```

```python
import functools
import math

import jax
import jax.numpy as jnp
from jax import lax
from jax.experimental import pallas as pl
from jax.experimental.pallas import tpu as pltpu
from jax.sharding import PartitionSpec as P

LEN = 1024
HD = 64
HALF = HD // 2
RB = 256
KB = 256
FB = 512

masked_score = -1e30
epsilon = 1e-06
SCALE = HD ** (-0.5)
SCALE2 = SCALE * math.log2(math.e)
SQRT_HALF = math.sqrt(0.5)
INV_SQRT_2PI = 1.0 / math.sqrt(2.0 * math.pi)

f32 = jnp.float32
bf16 = jnp.bfloat16

NN = (((1,), (0,)), ((), ()))
NT = (((1,), (1,)), ((), ()))
TN = (((0,), (0,)), ((), ()))


def mm(a, b, dims=NN):
    return lax.dot_general(a, b, dims, preferred_element_type=f32)


ANY = pl.BlockSpec(memory_space=pl.ANY)


def ignoring(count, kernel):
    return lambda c_ref, *refs: kernel(c_ref, *refs[count:])


def params(mib):
    return pltpu.CompilerParams(
        dimension_semantics=("arbitrary",), vmem_limit_bytes=mib * 1024 * 1024
    )


def hbm(shape, dtype):
    return pltpu.HBM(shape, dtype)


def stay(*arrays):
    return [pltpu.with_memory_space_constraint(a, pltpu.HBM) for a in arrays]


def cost(flops, nbytes, trans=0):
    return pl.CostEstimate(flops=int(flops) // 4, bytes_accessed=int(nbytes) // 4, transcendentals=int(trans) // 4)


def standardize(values):
    center = jnp.mean(values, axis=-1, keepdims=True)
    centered = values - center
    spread = jnp.mean(centered * centered, axis=-1, keepdims=True)
    inverse = lax.rsqrt(spread + epsilon)
    return centered * inverse, inverse


def column(row):
    n = row.shape[1]
    here = lax.broadcasted_iota(jnp.int32, (n, n), 0) == lax.broadcasted_iota(jnp.int32, (n, n), 1)
    return jnp.sum(jnp.where(here, row, 0.0), axis=1, keepdims=True)


def prepare_kernel(freq_ref, bias_ref, tab_ref, cols_ref):
    heads = freq_ref.shape[0]
    n = heads * HALF
    lane = lax.broadcasted_iota(jnp.int32, (HALF, 128), 1)
    spot = (lane & 31).astype(f32)
    part = lane >> 5
    for h in range(heads):
        freq = column(freq_ref[h : h + 1, :])
        for axis in range(2):
            angle = spot * freq[axis * HALF : (axis + 1) * HALF]
            for k, val in enumerate((jnp.cos(angle), jnp.sin(angle))):
                high = val.astype(bf16).astype(f32)
                rest = val - high
                mid = rest.astype(bf16).astype(f32)
                low = (rest - mid).astype(bf16).astype(f32)
                out = jnp.where(part == 0, high, jnp.where(part == 1, mid, jnp.where(part == 2, low, 0.0)))
                at = (axis * 2 + k) * n + h * HALF
                tab_ref[at : at + HALF, :] = out.astype(bf16)
    width = bias_ref.shape[1]
    for k in range(3):
        for h in range(heads):
            col = column(bias_ref[k : k + 1, h * HD : (h + 1) * HD])
            cols_ref[k * width + h * HD : k * width + (h + 1) * HD, :] = jnp.broadcast_to(col, (HD, 128))


def prepare(freq, bias):
    heads = freq.shape[0]
    return pl.pallas_call(
        prepare_kernel,
        out_shape=[
            jax.ShapeDtypeStruct((4 * heads * HALF, 128), bf16),
            jax.ShapeDtypeStruct((bias.shape[0] * bias.shape[1], 128), f32),
        ],
        name="prepare",
    )(freq, bias)


def lookup(tab_ref, grid_blk):
    n = tab_ref.shape[0] // 4
    rows = grid_blk.shape[1]
    spot = lax.broadcasted_iota(jnp.int32, (128, rows), 0) & 31
    one_r = jnp.where(spot == grid_blk[0:1, :], 1.0, 0.0).astype(bf16)
    one_c = jnp.where(spot == grid_blk[1:2, :], 1.0, 0.0).astype(bf16)
    by_c = mm(tab_ref[0 : 2 * n, :], one_c)
    by_r = mm(tab_ref[2 * n : 4 * n, :], one_r)
    cc, sc = by_c[:n], by_c[n:]
    cr, sr = by_r[:n], by_r[n:]
    return cc * cr - sc * sr, sc * cr + cc * sr


def proj_kernel(c_ref, x_ref, grid_ref, tab_ref, wt_ref, bias_ref, gain_ref, beta_ref, xhat_ref, q_ref, k_ref, v_ref):
    width = q_ref.shape[0]
    xhat, _ = standardize(x_ref[...].astype(f32))
    xhat_ref[...] = xhat.astype(bf16)
    normed = (xhat * gain_ref[...] + beta_ref[...]).astype(bf16)
    mixed = mm(wt_ref[...], normed, NT) + bias_ref[:, 0:1]
    cosine, sine = lookup(tab_ref, grid_ref[...])
    for which, ref in ((0, q_ref), (1, k_ref)):
        for h in range(width // HD):
            at = which * width + h * HD
            a1 = mixed[at : at + HALF]
            a2 = mixed[at + HALF : at + HD]
            c = cosine[h * HALF : (h + 1) * HALF]
            s = sine[h * HALF : (h + 1) * HALF]
            ref[h * HD : h * HD + HALF, :] = (a1 * c - a2 * s).astype(bf16)
            ref[h * HD + HALF : (h + 1) * HD, :] = (a1 * s + a2 * c).astype(bf16)
    v_ref[...] = mixed[2 * width : 3 * width].astype(bf16)


def project(seq, core, patches, grid, tab, wt, bias_cols, gain, beta, wait=()):
    d = patches.shape[1]
    wide = wt.shape[0]
    width = wide // 3
    steps = LEN // FB
    whole = lambda *shape: pl.BlockSpec(shape, lambda i, c: (0,) * len(shape), pipeline_mode=pl.Buffered(1))
    tall = pl.BlockSpec((width, FB), lambda i, c: (0, i))
    return pl.pallas_call(
        ignoring(len(wait), proj_kernel),
        grid_spec=pltpu.PrefetchScalarGridSpec(
            num_scalar_prefetch=1,
            grid=(steps,),
            in_specs=[ANY] * len(wait)
            + [
                pl.BlockSpec((FB, d), lambda i, c: (seq * steps + i, 0)),
                pl.BlockSpec((2, FB), lambda i, c: (0, seq * steps + i)),
                whole(*tab.shape),
                whole(*wt.shape),
                whole(*bias_cols.shape),
                whole(1, d),
                whole(1, d),
            ],
            out_specs=[pl.BlockSpec((FB, d), lambda i, c: (i, 0)), tall, tall, tall],
        ),
        out_shape=[hbm((LEN, d), bf16)] + [jax.ShapeDtypeStruct((width, LEN), bf16)] * 3,
        compiler_params=params(20),
        cost_estimate=cost(2 * LEN * d * wide, 2 * (2 * LEN * d + wide * (d + LEN))),
        name="project",
    )(core, *stay(*wait), *stay(patches, grid, tab, wt, bias_cols), gain, beta)


def key_range(ids_all, ids_blk):
    first = jnp.min(ids_blk)
    last = jnp.max(ids_blk)
    start = jnp.sum((ids_all < first).astype(jnp.int32))
    stop = jnp.sum((ids_all <= last).astype(jnp.int32))
    return start // KB, (stop + KB - 1) // KB


def same_image(idc_ref, at, ids_blk):
    ids_k = idc_ref[pl.ds(at, KB), :]
    ids_k = jnp.concatenate([ids_k] * (ids_blk.shape[1] // 128), axis=1)
    return ids_k == ids_blk


def rows_of(ref, h):
    return ref[h * HD : (h + 1) * HD, :]


def attend_kernel(c_ref, q_ref, k_ref, v_ref, idr_ref, idq_ref, idc_ref,
                  send_ref, keep_ref, ctx_ref, lse_ref, keys, scores, acc):
    step = pl.program_id(0)
    heads = q_ref.shape[0] // HD
    half = pl.num_programs(0) // 2

    @pl.when(step == 0)
    def _():
        for h in range(heads):
            keys[h] = jnp.transpose(rows_of(k_ref, h))

    ids_q = idq_ref[...]
    lo, hi = key_range(idr_ref[...], ids_q)

    def first_pass(kb, tops):
        at = pl.multiple_of(kb * KB, KB)
        same = same_image(idc_ref, at, ids_q)
        new = []
        for h in range(heads):
            s = mm(keys[h, pl.ds(at, KB), :], rows_of(q_ref, h))
            s = jnp.where(same, s, masked_score)
            scores[h, pl.ds(at, KB), :] = s
            new.append(jnp.maximum(tops[h], jnp.max(s, axis=0, keepdims=True)))
        return tuple(new)

    tops = lax.fori_loop(lo, hi, first_pass, tuple(jnp.full((1, RB), masked_score, f32) for _ in range(heads)))
    tops = tuple(top * SCALE2 for top in tops)
    acc[...] = jnp.zeros_like(acc)

    def second_pass(kb, totals):
        at = pl.multiple_of(kb * KB, KB)
        new = []
        for h in range(heads):
            p = jnp.exp2(scores[h, pl.ds(at, KB), :] * SCALE2 - tops[h])
            new.append(totals[h] + jnp.sum(p, axis=0, keepdims=True))
            acc[h * HD : (h + 1) * HD, :] += mm(v_ref[h * HD : (h + 1) * HD, pl.ds(at, KB)], p.astype(bf16))
        return tuple(new)

    totals = lax.fori_loop(lo, hi, second_pass, tuple(jnp.zeros((1, RB), f32) for _ in range(heads)))
    lse = jnp.zeros((8, RB), f32)
    row = lax.broadcasted_iota(jnp.int32, (8, RB), 0)
    for h in range(heads):
        ctx_ref[h * HD : (h + 1) * HD, :] = acc[h * HD : (h + 1) * HD, :] * (1.0 / totals[h])
        lse = jnp.where(row == h, tops[h] + jnp.log2(totals[h]), lse)
    lse_ref[...] = lse
    partial = ctx_ref[...].astype(bf16)

    @pl.when(step < half)
    def _():
        send_ref[...] = partial

    @pl.when(step >= half)
    def _():
        keep_ref[...] = partial


def attend(seq, core, q, k, v, ids_rows, ids_cols, wait=()):
    width = q.shape[0]
    steps = LEN // RB
    half = steps // 2
    heads = width // HD
    blk = lambda i, c: lax.rem(i + half * (1 - c[0]), steps)
    whole = lambda *shape: pl.BlockSpec(shape, lambda i, c: (0,) * len(shape), pipeline_mode=pl.Buffered(1))
    return pl.pallas_call(
        ignoring(len(wait), attend_kernel),
        grid_spec=pltpu.PrefetchScalarGridSpec(
            num_scalar_prefetch=1,
            grid=(steps,),
            in_specs=[ANY] * len(wait)
            + [
                pl.BlockSpec((width, RB), lambda i, c: (0, blk(i, c))),
                whole(width, LEN),
                whole(width, LEN),
                pl.BlockSpec((None, 1, LEN), lambda i, c: (seq, 0, 0)),
                pl.BlockSpec((None, 1, RB), lambda i, c: (seq, 0, blk(i, c))),
                pl.BlockSpec((LEN, 128), lambda i, c: (seq, 0)),
            ],
            out_specs=[
                pl.BlockSpec((width, RB), lambda i, c: (0, jnp.minimum(i, half - 1))),
                pl.BlockSpec((width, RB), lambda i, c: (0, jnp.maximum(i - half, 0))),
                pl.BlockSpec((width, RB), lambda i, c: (0, blk(i, c))),
                pl.BlockSpec((8, RB), lambda i, c: (0, blk(i, c))),
            ],
            scratch_shapes=[
                pltpu.VMEM((heads, LEN, HD), bf16),
                pltpu.VMEM((heads, LEN, RB), f32),
                pltpu.VMEM((width, RB), f32),
            ],
        ),
        out_shape=[
            jax.ShapeDtypeStruct((width, LEN // 2), bf16),
            jax.ShapeDtypeStruct((width, LEN // 2), bf16),
            hbm((width, LEN), f32),
            hbm((8, LEN), f32),
        ],
        compiler_params=params(10),
        cost_estimate=cost(8 * LEN * LEN * width, 12 * LEN * width, heads * LEN * LEN),
        name="attend",
    )(core, *stay(*wait), q, k, v, ids_rows, ids_rows, ids_cols)


def norm_two_kernel(c_ref, x_ref, *refs):
    groups = (len(refs) - 5) // 2
    ctx_refs, wo_refs = refs[:groups], refs[groups : 2 * groups]
    bias_ref, gain_ref, beta_ref, resid_ref, normed_ref = refs[2 * groups :]
    attn = bias_ref[...]
    for ctx_ref, wo_ref in zip(ctx_refs, wo_refs):
        attn = attn + mm(ctx_ref[...], wo_ref[...], TN).astype(bf16).astype(f32)
    resid = x_ref[...].astype(f32) + attn
    resid_ref[...] = resid
    xhat, _ = standardize(resid)
    normed_ref[...] = (xhat * gain_ref[...] + beta_ref[...]).astype(bf16)


def norm_two(seq, core, patches, ctxs, wos, bias, gain, beta, wait=()):
    width, rows = ctxs[0].shape
    d = patches.shape[1]
    steps = rows // RB
    blk = pl.BlockSpec((RB, d), lambda i, c: (i, 0))
    whole = lambda *shape: pl.BlockSpec(shape, lambda i, c: (0,) * len(shape), pipeline_mode=pl.Buffered(1))
    return pl.pallas_call(
        ignoring(len(wait), norm_two_kernel),
        grid_spec=pltpu.PrefetchScalarGridSpec(
            num_scalar_prefetch=1,
            grid=(steps,),
            in_specs=[ANY] * len(wait)
            + [pl.BlockSpec((RB, d), lambda i, c: ((2 * seq + c[0]) * steps + i, 0))]
            + [pl.BlockSpec((width, RB), lambda i, c: (0, i))] * len(ctxs)
            + [whole(width, d)] * len(wos)
            + [whole(1, d)] * 3,
            out_specs=[blk, blk],
        ),
        out_shape=[hbm((rows, d), f32), hbm((rows, d), bf16)],
        compiler_params=params(10),
        cost_estimate=cost(2 * len(ctxs) * rows * d * width, 12 * rows * d),
        name="norm_two",
    )(core, *stay(*wait), *stay(patches), *ctxs, *wos, bias, gain, beta)


def store_halves(mine, outs, sums):
    count = outs[0].shape[0]
    for out, half in zip(outs, (1 - mine, mine)):
        for k in range(count):
            at = 0
            for acc in sums:
                rows = acc.shape[0] // (2 * count)
                spot = pl.ds(pl.multiple_of((half * count + k) * rows, 8), rows)
                out[k, at : at + rows, :] = acc[spot, :].astype(bf16)
                at += rows


def feed_kernel(first, last, c_ref, *refs):
    refs = list(refs)
    own_ref, other_ref, og_ref, up_ref, upb_ref, down_ref = refs[:6]
    refs = refs[6:]
    if not first:
        small0_ref, up0_ref, down0_ref = refs[:3]
        refs = refs[3:]
    mlp_send, mlp_keep, n2_send, n2_keep, small_out = refs[:5]
    outs = refs[5:-4]
    up_acc, down_acc, up_sum, down_sum = refs[-4:]
    step = pl.program_id(0)
    steps = pl.num_programs(0)
    half = steps // 2

    @pl.when(step == 0)
    def _():
        if first:
            up_acc[...] = jnp.zeros_like(up_acc)
            down_acc[...] = jnp.zeros_like(down_acc)
            up_sum[...] = jnp.zeros_like(up_sum)
            down_sum[...] = jnp.zeros_like(down_sum)
        else:
            up_acc[...] = up0_ref[...]
            down_acc[...] = down0_ref[...]
            up_sum[...] = small0_ref[0:1, :]
            down_sum[...] = small0_ref[1:2, :]

    normed = jnp.where(step < half, other_ref[...], own_ref[...])
    og = og_ref[...]
    pre = mm(normed, up_ref[...]) + upb_ref[...]
    phi_cap = 0.5 * (1.0 + lax.erf(pre * SQRT_HALF))
    hidden = (pre * phi_cap).astype(bf16)
    mlp = mm(hidden, down_ref[...]).astype(bf16)
    slope = phi_cap + pre * (jnp.exp(-0.5 * pre * pre) * INV_SQRT_2PI)
    grad = mm(og, down_ref[...], NT)
    pre_grad = (grad * slope).astype(bf16)
    n2 = mm(pre_grad, up_ref[...], NT).astype(bf16)
    down_acc[...] += mm(hidden, og, TN)
    up_acc[...] += mm(normed, pre_grad, TN)
    up_sum[...] += jnp.sum(pre_grad.astype(f32), axis=0, keepdims=True)
    down_sum[...] += jnp.sum(og.astype(f32), axis=0, keepdims=True)

    @pl.when(step < half)
    def _():
        mlp_send[...] = mlp
        n2_send[...] = n2

    @pl.when(step >= half)
    def _():
        mlp_keep[...] = mlp
        n2_keep[...] = n2

    @pl.when(step == steps - 1)
    def _():
        if last:
            store_halves(c_ref[1], outs, (up_acc, down_acc))
        else:
            outs[0][...] = up_acc[...]
            outs[1][...] = down_acc[...]
        small_out[0:1, :] = up_sum[...]
        small_out[1:2, :] = down_sum[...]
        small_out[2:8, :] = jnp.zeros((6, up_sum.shape[1]), f32)


def feed(seq, core, own, other, out_grad, up, up_bias, down, before=None, last=0, wait=()):
    d, units = up.shape
    steps = LEN // FB
    half = steps // 2
    first = before is None
    whole = lambda *shape: pl.BlockSpec(shape, lambda i, c: (0,) * len(shape), pipeline_mode=pl.Buffered(1))
    low = pl.BlockSpec((FB, d), lambda i, c: (jnp.minimum(i, half - 1), 0))
    high = pl.BlockSpec((FB, d), lambda i, c: (jnp.maximum(i - half, 0), 0))
    blk = lambda i, c: seq * steps + lax.rem(i + half * (1 - c[0]), steps)
    in_specs = [ANY] * len(wait) + [
        high, low,
        pl.BlockSpec((FB, d), lambda i, c: (blk(i, c), 0)),
        whole(d, units), whole(1, units), whole(units, d),
    ]
    args = [core, *stay(*wait), *stay(own), other, *stay(out_grad), up, up_bias, down]
    if not first:
        in_specs += [whole(8, d), whole(d, units), whole(units, d)]
        args += list(before)
    if last:
        grads = [(last, (d + units) // (2 * last), d)] * 2
        kind = bf16
    else:
        grads = [(d, units), (units, d)]
        kind = f32
    rows = jax.ShapeDtypeStruct((LEN // 2, d), bf16)
    return pl.pallas_call(
        ignoring(len(wait), functools.partial(feed_kernel, first, last)),
        grid_spec=pltpu.PrefetchScalarGridSpec(
            num_scalar_prefetch=1,
            grid=(steps,),
            in_specs=in_specs,
            out_specs=[low, high, low, high, whole(8, d)] + [whole(*g) for g in grads],
            scratch_shapes=[
                pltpu.VMEM((d, units), f32),
                pltpu.VMEM((units, d), f32),
                pltpu.VMEM((1, units), f32),
                pltpu.VMEM((1, d), f32),
            ],
        ),
        out_shape=[hbm(rows.shape, bf16), hbm(rows.shape, bf16), hbm(rows.shape, bf16), rows, hbm((8, d), f32)]
        + [(hbm if last else jax.ShapeDtypeStruct)(g, kind) for g in grads],
        compiler_params=params(50),
        cost_estimate=cost(12 * LEN * d * units, 2 * LEN * d * 4 + 12 * d * units, 2 * LEN * units),
        name="feed",
    )(*args)


def norm_two_back_kernel(first, c_ref, *refs):
    refs = list(refs)
    mine_ref, theirs_ref, resid_ref, og_ref, gain_ref = refs[:5]
    refs = refs[5:]
    if not first:
        small0_ref = refs[0]
        refs = refs[1:]
    rgrad_ref, branch_ref, small_ref = refs
    step = pl.program_id(0)

    @pl.when(step == 0)
    def _():
        if first:
            small_ref[...] = jnp.zeros_like(small_ref)
        else:
            small_ref[...] = small0_ref[...]

    grad = mine_ref[...].astype(f32) + theirs_ref[...].astype(f32)
    xhat, inverse = standardize(resid_ref[...])
    e = grad * gain_ref[...]
    back = inverse * (
        e - jnp.mean(e, axis=-1, keepdims=True) - xhat * jnp.mean(e * xhat, axis=-1, keepdims=True)
    )
    rgrad = og_ref[...].astype(f32) + back
    rgrad_ref[...] = rgrad
    branch = rgrad.astype(bf16)
    branch_ref[...] = branch
    small_ref[0:1, :] += jnp.sum(grad * xhat, axis=0, keepdims=True)
    small_ref[1:2, :] += jnp.sum(grad, axis=0, keepdims=True)
    small_ref[2:3, :] += jnp.sum(branch.astype(f32), axis=0, keepdims=True)


def norm_two_back(seq, core, mine, theirs, resid, out_grad, gain, before=None, wait=()):
    rows, d = mine.shape
    steps = rows // RB
    first = before is None
    blk = pl.BlockSpec((RB, d), lambda i, c: (i, 0))
    vec = pl.BlockSpec((1, d), lambda i, c: (0, 0))
    small = pl.BlockSpec((8, d), lambda i, c: (0, 0))
    in_specs = [ANY] * len(wait) + [blk, blk, blk, pl.BlockSpec((RB, d), lambda i, c: ((2 * seq + c[0]) * steps + i, 0)), vec]
    args = [core, *stay(*wait), mine, theirs, *stay(resid, out_grad), gain]
    if not first:
        in_specs.append(small)
        args += stay(before)
    return pl.pallas_call(
        ignoring(len(wait), functools.partial(norm_two_back_kernel, first)),
        grid_spec=pltpu.PrefetchScalarGridSpec(
            num_scalar_prefetch=1, grid=(steps,), in_specs=in_specs, out_specs=[blk, blk, small]
        ),
        out_shape=[
            hbm((rows, d), f32),
            jax.ShapeDtypeStruct((rows, d), bf16),
            hbm((8, d), f32),
        ],
        compiler_params=params(12),
        cost_estimate=cost(20 * rows * d, 16 * rows * d),
        name="norm_two_back",
    )(*args)


def attend_back_kernel(first, c_ref, *refs):
    refs = list(refs)
    own_ref, other_ref, q_ref, k_ref, v_ref, ctx_ref, lse_ref, idr_ref, idq_ref, idc_ref, wo_ref = refs[:11]
    refs = refs[11:]
    dwo0_ref = None if first else refs.pop(0)
    grads_ref, dwo_ref, keys, vals = refs
    step = pl.program_id(0)
    steps = pl.num_programs(0)
    half = steps // 2
    width = q_ref.shape[0]
    heads = width // HD
    blk = lax.rem(step + half * (1 - c_ref[0]), steps)
    here = pl.ds(pl.multiple_of(blk * RB, RB), RB)

    @pl.when(step == 0)
    def _():
        for h in range(heads):
            keys[h] = jnp.transpose(rows_of(k_ref, h))
            vals[h] = jnp.transpose(rows_of(v_ref, h))
        grads_ref[...] = jnp.zeros_like(grads_ref)
        dwo_ref[...] = jnp.zeros_like(dwo_ref) if first else dwo0_ref[...]

    branch = jnp.where(step < half, other_ref[...], own_ref[...])
    ctx = ctx_ref[:, here]
    dctx = mm(wo_ref[...], branch, NT).astype(bf16)
    dwo_ref[...] += mm(ctx.astype(bf16), branch)
    prod = dctx.astype(f32) * ctx
    lse = lse_ref[:, here]
    ids_q = idq_ref[...]
    lo, hi = key_range(idr_ref[...], ids_q)
    parts = []
    for h in range(heads):
        sl = slice(h * HD, (h + 1) * HD)
        parts.append((q_ref[sl, here], dctx[sl], jnp.sum(prod[sl], axis=0, keepdims=True), lse[h : h + 1]))

    def body(kb, carry):
        at = pl.multiple_of(kb * KB, KB)
        there = pl.ds(at, KB)
        same = same_image(idc_ref, at, ids_q)
        for h in range(heads):
            q_h, do_h, delta, lse_h = parts[h]
            s = mm(keys[h, there, :], q_h)
            p = jnp.exp2(jnp.where(same, s * SCALE2 - lse_h, masked_score))
            dp = mm(vals[h, there, :], do_h)
            ds = (p * (dp - delta)).astype(bf16)
            at_q, at_k, at_v = (slice(k * width + h * HD, k * width + (h + 1) * HD) for k in range(3))
            grads_ref[at_q, here] += mm(k_ref[h * HD : (h + 1) * HD, there], ds)
            grads_ref[at_k, there] += mm(q_h, ds, NT)
            grads_ref[at_v, there] += mm(do_h, p.astype(bf16), NT)
        return carry

    lax.fori_loop(lo, hi, body, 0)


def attend_back(seq, core, own, other, q, k, v, ctx, lse, ids_rows, ids_cols, wo, before=None, wait=()):
    width, d = wo.shape
    heads = width // HD
    steps = LEN // RB
    half = steps // 2
    first = before is None
    whole = lambda *shape: pl.BlockSpec(shape, lambda i, c: (0,) * len(shape), pipeline_mode=pl.Buffered(1))
    blk = lambda i, c: lax.rem(i + half * (1 - c[0]), steps)
    in_specs = [ANY] * len(wait) + [
        pl.BlockSpec((RB, d), lambda i, c: (jnp.maximum(i - half, 0), 0)),
        pl.BlockSpec((RB, d), lambda i, c: (jnp.minimum(i, half - 1), 0)),
        whole(width, LEN), whole(width, LEN), whole(width, LEN), whole(width, LEN), whole(8, LEN),
        pl.BlockSpec((None, 1, LEN), lambda i, c: (seq, 0, 0)),
        pl.BlockSpec((None, 1, RB), lambda i, c: (seq, 0, blk(i, c))),
        pl.BlockSpec((LEN, 128), lambda i, c: (seq, 0)),
        whole(width, d),
    ]
    q, k, v, ctx, lse, ids_cols = stay(q, k, v, ctx, lse, ids_cols)
    args = [core, *stay(*wait), own, other, q, k, v, ctx, lse, ids_rows, ids_rows, ids_cols, wo]
    if not first:
        in_specs.append(whole(width, d))
        args += stay(before)
    return pl.pallas_call(
        ignoring(len(wait), functools.partial(attend_back_kernel, first)),
        grid_spec=pltpu.PrefetchScalarGridSpec(
            num_scalar_prefetch=1, grid=(steps,), in_specs=in_specs,
            out_specs=[whole(3 * width, LEN), whole(width, d)],
            scratch_shapes=[pltpu.VMEM((heads, LEN, HD), bf16), pltpu.VMEM((heads, LEN, HD), bf16)],
        ),
        out_shape=[hbm((3 * width, LEN), f32), hbm((width, d), f32)],
        compiler_params=params(20),
        cost_estimate=cost(
            20 * LEN * LEN * width + 8 * LEN * d * width, 2 * LEN * (10 * width + d) + 8 * d * width, heads * LEN * LEN,
        ),
        name="attend_back",
    )(*args)


def project_back_kernel(c_ref, *refs):
    seqs = (refs[:4], refs[4:8])
    (wt_ref, tab_ref, grid_ref, gain_ref, beta_ref, dwo_ref, small_two_ref, small_feed_ref) = refs[8:16]
    send_away, keep_away, send_mine, keep_mine, small_ref = refs[16:21]
    outs = refs[21:23]
    dwt_acc, row_acc, col_acc, rope_acc = refs[23:]
    step = pl.program_id(0)
    steps = pl.num_programs(0) // 2
    half = steps // 2
    width = seqs[0][0].shape[0]
    heads = width // HD
    second = (step < steps) != (c_ref[2] > 0)

    def pick(k):
        return jnp.where(second, seqs[1][k][...], seqs[0][k][...])

    @pl.when(step == 0)
    def _():
        for acc in (dwt_acc, row_acc, col_acc, rope_acc):
            acc[...] = jnp.zeros_like(acc)

    place = grid_ref[...]
    cosine, sine = lookup(tab_ref, place)
    grads = pick(2)
    pieces = []
    angle = [None] * heads
    for k in range(2):
        turned = pick(k)
        for h in range(heads):
            b = grads[k * width + h * HD : k * width + (h + 1) * HD] * SCALE
            a = turned[h * HD : (h + 1) * HD].astype(f32)
            b1, b2 = b[:HALF], b[HALF:]
            co = cosine[h * HALF : (h + 1) * HALF]
            si = sine[h * HALF : (h + 1) * HALF]
            pieces.append((b1 * co + b2 * si).astype(bf16))
            pieces.append((b2 * co - b1 * si).astype(bf16))
            term = b2 * a[:HALF] - b1 * a[HALF:]
            angle[h] = term if angle[h] is None else angle[h] + term
    pieces.append(grads[2 * width :].astype(bf16))
    mixed_grad = jnp.concatenate(pieces, axis=0)
    angle = jnp.concatenate(angle, axis=0)
    rope_acc[...] += lax.dot_general(
        place.astype(f32), angle, NT, precision=lax.Precision.HIGHEST, preferred_element_type=f32
    )
    row_acc[...] += mm(jnp.ones((8, RB), bf16), mixed_grad, NT)
    col_acc[...] += mm(mixed_grad, jnp.ones((RB, 128), bf16))
    dwt_acc[...] += mm(mixed_grad, pick(3))
    partial = mm(mixed_grad, wt_ref[...], TN).astype(bf16)
    for k, out in enumerate((send_away, keep_away, send_mine, keep_mine)):
        @pl.when(step // half == k)
        def _():
            out[...] = partial

    @pl.when(step == 2 * steps - 1)
    def _():
        raw = dwt_acc[...]
        col = col_acc[:, 0:1]
        wt = wt_ref[...].astype(f32)
        small_ref[0:1, :] = jnp.sum(wt * raw, axis=0, keepdims=True)
        small_ref[1:2, :] = jnp.sum(wt * col, axis=0, keepdims=True)
        small_ref[2:5, :] = 0.5 * small_two_ref[0:3, :]
        small_ref[5:7, :] = small_feed_ref[0:2, :]
        small_ref[7:8, :] = jnp.concatenate([row_acc[0:1, :], rope_acc[1:2, :], rope_acc[0:1, :]], axis=1)
        dwt_acc[...] = raw * gain_ref[...] + col * beta_ref[...]
        store_halves(c_ref[1], outs, (dwt_acc, dwo_ref))


def project_back(core, seqs, wt, tab, grid, gain, beta, dwo, small_two, small_feed, pieces, wait=()):
    d = wt.shape[1]
    width = wt.shape[0] // 3
    heads = width // HD
    steps = LEN // RB
    half = steps // 2
    whole = lambda *shape: pl.BlockSpec(shape, lambda i, c: (0,) * len(shape), pipeline_mode=pl.Buffered(1))
    blk = lambda i, c: lax.rem(lax.rem(i, steps) + half * (1 - c[0]), steps)
    now = lambda i, c: jnp.where(i < steps, 1 - c[2], c[2])

    def turn(s, i, c):
        early = s == jnp.where(c[2] > 0, 0, 1)
        rest = jnp.where(early, blk(steps - 1, c), blk(0, c))
        return jnp.where(now(i, c) == s, blk(i, c), rest)

    in_specs = [ANY] * len(wait)
    args = [core, *stay(*wait)]
    for s in range(2):
        tall = lambda i, c, s=s: (0, turn(s, i, c))
        flat = lambda i, c, s=s: (turn(s, i, c), 0)
        in_specs += [
            pl.BlockSpec((width, RB), tall), pl.BlockSpec((width, RB), tall), pl.BlockSpec((3 * width, RB), tall),
            pl.BlockSpec((RB, d), flat),
        ]
        args += stay(*seqs[s])
    in_specs += [
        whole(3 * width, d), whole(*tab.shape),
        pl.BlockSpec((2, RB), lambda i, c: (0, now(i, c) * steps + blk(i, c))),
        whole(1, d), whole(1, d), whole(width, d), whole(8, d), whole(8, d),
    ]
    args += [wt, *stay(tab, grid), gain, beta, *stay(dwo, small_two, small_feed)]
    part = lambda k: pl.BlockSpec((RB, d), lambda i, c: (jnp.clip(i - k * half, 0, half - 1), 0))
    cut = (pieces, 4 * width // (2 * pieces), d)
    rows = hbm((LEN // 2, d), bf16)
    return pl.pallas_call(
        ignoring(len(wait), project_back_kernel),
        grid_spec=pltpu.PrefetchScalarGridSpec(
            num_scalar_prefetch=1, grid=(2 * steps,), in_specs=in_specs,
            out_specs=[part(0), part(1), part(2), part(3), whole(8, d), whole(*cut), whole(*cut)],
            scratch_shapes=[
                pltpu.VMEM((3 * width, d), f32),
                pltpu.VMEM((8, 3 * width), f32),
                pltpu.VMEM((3 * width, 128), f32),
                pltpu.VMEM((2, heads * HALF), f32),
            ],
        ),
        out_shape=[rows, rows, rows, rows, hbm((8, d), f32), hbm(cut, bf16), hbm(cut, bf16)],
        compiler_params=params(28),
        cost_estimate=cost(24 * LEN * d * width, 4 * LEN * (12 * width + 3 * d), LEN * width),
        name="project_back",
    )(*args)


def norm_one_back_kernel(m_ref, mine_ref, got_ref, theirs_ref, x_ref, rg0_ref, rg1_ref, gain_ref, out_ref):
    f = (mine_ref[...].astype(f32) + got_ref[...].astype(f32) + theirs_ref[...].astype(f32)) * gain_ref[...]
    xhat, inverse = standardize(x_ref[...].astype(f32))
    back = inverse * (
        f - jnp.mean(f, axis=-1, keepdims=True) - xhat * jnp.mean(f * xhat, axis=-1, keepdims=True)
    )
    rgrad = jnp.where(m_ref[0] < 2, rg0_ref[...], rg1_ref[...])
    out_ref[...] = (rgrad + back).astype(bf16)


def norm_one_back(place, mine, got, theirs, patches, rg0, rg1, gain):
    rows, d = mine.shape
    steps = rows // RB
    blk = pl.BlockSpec((RB, d), lambda i, m: (i, 0))
    return pl.pallas_call(
        norm_one_back_kernel,
        grid_spec=pltpu.PrefetchScalarGridSpec(
            num_scalar_prefetch=1,
            grid=(steps,),
            in_specs=[
                blk, blk, blk, pl.BlockSpec((RB, d), lambda i, m: (m[0] * steps + i, 0)), blk, blk,
                pl.BlockSpec((1, d), lambda i, m: (0, 0)),
            ],
            out_specs=blk,
        ),
        out_shape=jax.ShapeDtypeStruct((rows, d), bf16),
        compiler_params=params(12),
        cost_estimate=cost(20 * rows * d, 16 * rows * d),
        name="norm_one_back",
    )(place, mine, got, theirs, *stay(patches, rg0, rg1), gain)


CORE_SWAP = [(i, i ^ 1) for i in range(4)]
CHIP_SWAP = [(i, i ^ 2) for i in range(4)]


def core_swap(value):
    return lax.ppermute(value, "mp", CORE_SWAP)


def chip_swap(value):
    return lax.ppermute(value, "mp", CHIP_SWAP)


def after(value, *events):
    return lax.optimization_barrier((value, *events))[0]


def add_low(a, b):
    return (a.astype(f32) + b.astype(f32)).astype(bf16)


def add_kernel(c_ref, a_ref, b_ref, out_ref):
    out_ref[...] = (a_ref[...].astype(f32) + b_ref[...].astype(f32)).astype(bf16)


def full(shape):
    return pl.BlockSpec(shape, lambda i, c: (0,) * len(shape))


def add_parts(core, a, b, wait=()):
    return pl.pallas_call(
        ignoring(len(wait), add_kernel),
        grid_spec=pltpu.PrefetchScalarGridSpec(
            num_scalar_prefetch=1, grid=(1,), in_specs=[ANY] * len(wait) + [full(a.shape)] * 2, out_specs=full(a.shape),
        ),
        out_shape=hbm(a.shape, bf16),
        compiler_params=params(12),
        cost_estimate=cost(a.size, 6 * a.size),
        name="add_parts",
    )(core, *stay(*wait), *stay(a), b)


def sum_parts_kernel(c_ref, parts_ref, *refs):
    out_ref = refs[-1]
    total = parts_ref[0].astype(f32)
    for k in range(1, parts_ref.shape[0]):
        total = total + parts_ref[k].astype(f32)
    rows = total.shape[0]
    total = total.astype(bf16)
    for k in range(out_ref.shape[0]):
        out_ref[k, 0:rows, :] = total
    if len(refs) > 1:
        small = refs[0][...]
        high = small.astype(bf16)
        low = (small - high.astype(f32)).astype(bf16)
        for k in range(out_ref.shape[0]):
            out_ref[k, rows : rows + 8, :] = high
            out_ref[k, rows + 8 : rows + 16, :] = low


def sum_parts(core, parts, small=None, copies=None, wait=()):
    count, rows, d = parts.shape
    extra = () if small is None else (small,)
    out = (copies or count, rows + 16 * len(extra), d)
    return pl.pallas_call(
        ignoring(len(wait), sum_parts_kernel),
        grid_spec=pltpu.PrefetchScalarGridSpec(
            num_scalar_prefetch=1, grid=(1,),
            in_specs=[ANY] * len(wait) + [full(parts.shape)] + [full(e.shape) for e in extra],
            out_specs=full(out),
        ),
        out_shape=jax.ShapeDtypeStruct(out, bf16),
        compiler_params=params(12),
        cost_estimate=cost(count * rows * d, 4 * count * rows * d),
        name="sum_parts",
    )(core, *stay(*wait), parts, *extra)


def place_parts_kernel(with_small, c_ref, mine_ref, theirs_ref, *refs):
    outs = refs[: len(refs) - with_small]
    count = mine_ref.shape[0]
    small = None
    for ref, half in ((mine_ref, c_ref[1]), (theirs_ref, 1 - c_ref[1])):
        for k in range(count):
            at = 0
            for out in outs:
                rows = out.shape[0] // (2 * count)
                spot = pl.ds(pl.multiple_of((half * count + k) * rows, 8), rows)
                out[spot, :] = ref[k, at : at + rows, :].astype(f32)
                at += rows
            if with_small:
                part = ref[k, at : at + 8, :].astype(f32) + ref[k, at + 8 : at + 16, :].astype(f32)
                small = part if small is None else small + part
    if with_small:
        refs[-1][...] = small


def place_parts(core, mine, theirs, splits, with_small=False):
    d = mine.shape[2]
    shapes = [(rows, d) for rows in splits] + [(8, d)] * with_small
    return pl.pallas_call(
        functools.partial(place_parts_kernel, with_small),
        grid_spec=pltpu.PrefetchScalarGridSpec(
            num_scalar_prefetch=1, grid=(1,), in_specs=[full(mine.shape)] * 2, out_specs=[full(t) for t in shapes],
        ),
        out_shape=[jax.ShapeDtypeStruct(t, f32) for t in shapes],
        compiler_params=params(20),
        cost_estimate=cost(sum(splits) * d, 6 * sum(splits) * d),
        name="place_parts",
    )(core, mine, theirs)


def half_swap(value):
    return lax.ppermute(value, "dp", [(i, i ^ 1) for i in range(lax.axis_size("dp"))])


def quarter_trade(parts):
    return lax.all_to_all(parts, "dp", 0, 0, axis_index_groups=[[0, 2, 4, 6], [1, 3, 5, 7]])


def hold(values, *events):
    return list(lax.optimization_barrier((*values, *events))[: len(values)])


def local(patches, image_ids, patch_grid, first_norm_gain, first_norm_bias, qkv_weight, qkv_bias, rope_freq,
          out_weight, out_bias, second_norm_gain, second_norm_bias, up_weight, up_bias, down_weight, down_bias,
          out_grad):
    all_rows, d = patches.shape
    seqs = all_rows // LEN
    assert lax.axis_size("mp") == 4 and seqs == 2
    devices = lax.axis_size("dp")
    tree = devices == 8
    pieces = 4 if tree else 1
    heads = rope_freq.shape[0]
    width = heads * HD
    units = up_weight.shape[1]
    place = lax.axis_index("mp").astype(jnp.int32)
    half = lax.axis_index("dp").astype(jnp.int32) % 2 if tree else jnp.int32(0)
    core = jnp.stack([place % 2, half, place // 2])
    place_arr = place.reshape(1)
    far = place >= 2
    row = lambda v: v.reshape(1, -1)

    tab, bias_cols = prepare(rope_freq, qkv_bias)
    wt = qkv_weight.transpose(1, 2, 0).reshape(3 * width, d)
    ids_rows = image_ids.reshape(seqs, 1, LEN)
    ids_cols = jnp.broadcast_to(image_ids[:, None], (all_rows, 128))
    gain1, beta1 = row(first_norm_gain), row(first_norm_bias)
    gain2, beta2 = row(second_norm_gain), row(second_norm_bias)

    wo_core = core_swap(out_weight)
    proj_args = (patches, patch_grid, tab, wt, bias_cols, gain1, beta1)
    made0 = project(0, core, *proj_args)
    send0, keep0, ctx0, lse0 = attend(0, core, *made0[1:], ids_rows, ids_cols)
    core0, far_keep0 = core_swap(send0), chip_swap(keep0)
    made1 = project(1, core, *proj_args, wait=[lse0, wo_core])
    far_core0, wo_far = chip_swap(core0), chip_swap(out_weight)
    send1, keep1, ctx1, lse1 = attend(1, core, *made1[1:], ids_rows, ids_cols, wait=[made1[0]])
    core1, far_keep1 = core_swap(send1), chip_swap(keep1)
    wos = [out_weight, wo_core, wo_far, core_swap(wo_far)]
    norm_args = (row(out_bias), gain2, beta2)
    resid0, normed0 = norm_two(
        0, core, patches, [keep0, core0, far_keep0, far_core0], wos, *norm_args, wait=[lse1]
    )
    normed0, core1, far_keep1 = hold([normed0, core1, far_keep1])
    far_core1 = chip_swap(core1)
    feed_args = (out_grad, up_weight, row(up_bias), down_weight)
    mlp_send0, mlp_keep0, n2_send0, n2_keep0, *sums = feed(
        0, core, normed0, core_swap(normed0), *feed_args
    )
    n2_send0, far_core1 = hold([n2_send0, far_core1])
    n20 = add_low(n2_keep0, core_swap(n2_send0))
    resid1, normed1 = norm_two(
        1, core, patches, [keep1, core1, far_keep1, far_core1], wos, *norm_args, wait=[sums[0]]
    )
    n2_far0 = chip_swap(n20)
    mlp_send1, mlp_keep1, n2_send1, n2_keep1, small_feed, feed_send, feed_keep = feed(
        1, core, normed1, core_swap(normed1), *feed_args, before=sums, last=pieces, wait=[n20]
    )
    if tree:
        feed_got = half_swap(feed_send)
    n21 = add_low(n2_keep1, core_swap(n2_send1))
    mlp0 = add_low(mlp_keep0, core_swap(mlp_send0))
    mlp1 = add_low(mlp_keep1, core_swap(mlp_send1))
    mlp_away, mlp_mine = jnp.where(far, mlp0, mlp1), jnp.where(far, mlp1, mlp0)
    rgrad0, branch0, small_two = norm_two_back(
        0, core, n20, n2_far0, resid0, out_grad, gain2, wait=[small_feed]
    )
    n2_far1 = chip_swap(n21)
    grads0, dwo = attend_back(
        0, core, branch0, core_swap(branch0), *made0[1:], ctx0, lse0, ids_rows, ids_cols, out_weight, wait=[n21]
    )
    event = dwo
    if tree:
        feed_part = add_parts(core, feed_keep, feed_got, wait=[dwo, n2_far1])
        event = feed_part
        feed_got = quarter_trade(feed_part)
    rgrad1, branch1, small_two = norm_two_back(
        1, core, n21, n2_far1, resid1, out_grad, gain2, before=small_two, wait=[event]
    )
    grads1, dwo = attend_back(
        1, core, branch1, core_swap(branch1), *made1[1:], ctx1, lse1, ids_rows, ids_cols, out_weight, before=dwo,
        wait=[mlp_away],
    )
    event = dwo
    if tree:
        feed_sum = sum_parts(core, feed_got, wait=[dwo])
        event = feed_sum
        feed_all = quarter_trade(feed_sum)
    mlp_theirs = chip_swap(mlp_away)
    n1_send_away, n1_away, n1_send, n1_keep, small, grad_send, grad_keep = project_back(
        core, [(*made[1:3], grads, made[0]) for made, grads in ((made0, grads0), (made1, grads1))],
        wt, tab, patch_grid, gain1, beta1, dwo, small_two, small_feed, pieces, wait=[event],
    )
    n1_send_away, small, grad_send, mlp_theirs = hold([n1_send_away, small, grad_send, mlp_theirs])
    n1_away = add_low(n1_away, core_swap(n1_send_away))
    n1_got = core_swap(n1_send)
    shared = lax.broadcasted_iota(jnp.int32, small.shape, 0) < 5
    for swap in (core_swap, chip_swap):
        small = small + jnp.where(shared, swap(small), 0.0)
    theirs = chip_swap(after(n1_away, small))
    if tree:
        grad_got = half_swap(grad_send)
        grad_got = quarter_trade(add_parts(core, grad_keep, grad_got, wait=[feed_all]))
        feed_other = half_swap(feed_all)
        grad_sum = quarter_trade(sum_parts(core, grad_got, small))
        grad_other = half_swap(grad_sum)
    else:
        small, grad_send, grad_keep, feed_send, feed_keep = lax.psum(
            (small, grad_send, grad_keep, feed_send, feed_keep), "dp"
        )
        feed_all, feed_other = feed_keep, feed_send
        grad_sum = sum_parts(core, grad_keep, small)
        grad_other = sum_parts(core, grad_send, jnp.zeros_like(small))

    out_rows = (
        jnp.where(far, resid1, resid0)
        + (mlp_mine.astype(f32) + mlp_theirs.astype(f32))
        + row(down_bias)
    ).astype(bf16)
    grad_rows = norm_one_back(place_arr, n1_keep, n1_got, theirs, patches, rgrad0, rgrad1, gain1)
    up_grad, down_grad = place_parts(core, feed_all, feed_other, (d, units))
    (grad_other,) = hold([grad_other], grad_rows)
    qkv_grad, out_grad_w, small = place_parts(core, grad_sum, grad_other, (3 * width, width), True)
    turns = heads * HALF
    by_col = small[7, 3 * width : 3 * width + turns].reshape(heads, HALF)
    by_row = small[7, 3 * width + turns : 3 * width + 2 * turns].reshape(heads, HALF)
    return (
        out_rows,
        grad_rows,
        small[0],
        small[1],
        qkv_grad.reshape(3, width, d).transpose(2, 0, 1),
        small[7, : 3 * width].reshape(3, width),
        jnp.concatenate([by_col, by_row], axis=-1),
        out_grad_w,
        small[4],
        small[2],
        small[3],
        up_grad,
        small[5],
        down_grad,
        small[6],
    )


def solution(mesh):
    placed = (
        P("dp", None),
        P("dp"),
        P(None, "dp"),
        P(),
        P(),
        P(None, None, "mp"),
        P(None, "mp"),
        P("mp", None),
        P("mp", None),
        P(),
        P(),
        P(),
        P(None, "mp"),
        P("mp"),
        P("mp", None),
        P(),
        P("dp", None),
    )
    return jax.shard_map(
        local,
        mesh=mesh,
        in_specs=placed,
        out_specs=(
            P(("dp", "mp"), None),
            P(("dp", "mp"), None),
            P(),
            P(),
            P(None, None, "mp"),
            P(None, "mp"),
            P("mp", None),
            P("mp", None),
            P(),
            P(),
            P(),
            P(None, "mp"),
            P("mp"),
            P("mp", None),
            P(),
        ),
        check_vma=False,
    )
```

```python
import functools
import math

import jax
import jax.numpy as jnp
from jax import lax
from jax.experimental import pallas as pl
from jax.experimental.pallas import tpu as pltpu
from jax.sharding import PartitionSpec as P

LEN = 1024
HD = 64
HALF = HD // 2
RB = 256
KB = 512
FB = 512

masked_score = -1e30
epsilon = 1e-06
SCALE = HD ** (-0.5)
SCALE2 = SCALE * math.log2(math.e)
SQRT_HALF = math.sqrt(0.5)
INV_SQRT_2PI = 1.0 / math.sqrt(2.0 * math.pi)

f32 = jnp.float32
bf16 = jnp.bfloat16

NN = (((1,), (0,)), ((), ()))
NT = (((1,), (1,)), ((), ()))
TN = (((0,), (0,)), ((), ()))


def mm(a, b, dims=NN):
    return lax.dot_general(a, b, dims, preferred_element_type=f32)


ANY = pl.BlockSpec(memory_space=pl.ANY)


def ignoring(count, kernel):
    return lambda c_ref, *refs: kernel(c_ref, *refs[count:])


def params(mib):
    return pltpu.CompilerParams(
        dimension_semantics=("arbitrary",), vmem_limit_bytes=mib * 1024 * 1024
    )


def hbm(shape, dtype):
    return pltpu.HBM(shape, dtype)


def stay(*arrays):
    return [pltpu.with_memory_space_constraint(a, pltpu.HBM) for a in arrays]


def cost(flops, nbytes, trans=0):
    return pl.CostEstimate(flops=int(flops) // 4, bytes_accessed=int(nbytes) // 4, transcendentals=int(trans) // 4)


def standardize(values):
    center = jnp.mean(values, axis=-1, keepdims=True)
    centered = values - center
    spread = jnp.mean(centered * centered, axis=-1, keepdims=True)
    inverse = lax.rsqrt(spread + epsilon)
    return centered * inverse, inverse


def column(row):
    n = row.shape[1]
    here = lax.broadcasted_iota(jnp.int32, (n, n), 0) == lax.broadcasted_iota(jnp.int32, (n, n), 1)
    return jnp.sum(jnp.where(here, row, 0.0), axis=1, keepdims=True)


def prepare_kernel(freq_ref, bias_ref, tab_ref, cols_ref):
    heads = freq_ref.shape[0]
    n = heads * HALF
    lane = lax.broadcasted_iota(jnp.int32, (HALF, 128), 1)
    spot = (lane & 31).astype(f32)
    part = lane >> 5
    for h in range(heads):
        freq = column(freq_ref[h : h + 1, :])
        for axis in range(2):
            angle = spot * freq[axis * HALF : (axis + 1) * HALF]
            for k, val in enumerate((jnp.cos(angle), jnp.sin(angle))):
                high = val.astype(bf16).astype(f32)
                rest = val - high
                mid = rest.astype(bf16).astype(f32)
                low = (rest - mid).astype(bf16).astype(f32)
                out = jnp.where(part == 0, high, jnp.where(part == 1, mid, jnp.where(part == 2, low, 0.0)))
                at = (axis * 2 + k) * n + h * HALF
                tab_ref[at : at + HALF, :] = out.astype(bf16)
    width = bias_ref.shape[1]
    for k in range(3):
        for h in range(heads):
            col = column(bias_ref[k : k + 1, h * HD : (h + 1) * HD])
            cols_ref[k * width + h * HD : k * width + (h + 1) * HD, :] = jnp.broadcast_to(col, (HD, 128))


def prepare(freq, bias):
    heads = freq.shape[0]
    return pl.pallas_call(
        prepare_kernel,
        out_shape=[
            jax.ShapeDtypeStruct((4 * heads * HALF, 128), bf16),
            jax.ShapeDtypeStruct((bias.shape[0] * bias.shape[1], 128), f32),
        ],
        name="prepare",
    )(freq, bias)


def lookup(tab_ref, grid_blk):
    n = tab_ref.shape[0] // 4
    rows = grid_blk.shape[1]
    spot = lax.broadcasted_iota(jnp.int32, (128, rows), 0) & 31
    one_r = jnp.where(spot == grid_blk[0:1, :], 1.0, 0.0).astype(bf16)
    one_c = jnp.where(spot == grid_blk[1:2, :], 1.0, 0.0).astype(bf16)
    by_c = mm(tab_ref[0 : 2 * n, :], one_c)
    by_r = mm(tab_ref[2 * n : 4 * n, :], one_r)
    cc, sc = by_c[:n], by_c[n:]
    cr, sr = by_r[:n], by_r[n:]
    return cc * cr - sc * sr, sc * cr + cc * sr


def proj_kernel(c_ref, x_ref, grid_ref, tab_ref, wt_ref, bias_ref, gain_ref, beta_ref, xhat_ref, q_ref, k_ref, v_ref):
    width = q_ref.shape[0]
    xhat, _ = standardize(x_ref[...].astype(f32))
    xhat_ref[...] = xhat.astype(bf16)
    normed = (xhat * gain_ref[...] + beta_ref[...]).astype(bf16)
    mixed = mm(wt_ref[...], normed, NT) + bias_ref[:, 0:1]
    cosine, sine = lookup(tab_ref, grid_ref[...])
    for which, ref in ((0, q_ref), (1, k_ref)):
        for h in range(width // HD):
            at = which * width + h * HD
            a1 = mixed[at : at + HALF]
            a2 = mixed[at + HALF : at + HD]
            c = cosine[h * HALF : (h + 1) * HALF]
            s = sine[h * HALF : (h + 1) * HALF]
            ref[h * HD : h * HD + HALF, :] = (a1 * c - a2 * s).astype(bf16)
            ref[h * HD + HALF : (h + 1) * HD, :] = (a1 * s + a2 * c).astype(bf16)
    v_ref[...] = mixed[2 * width : 3 * width].astype(bf16)


def project(seq, core, patches, grid, tab, wt, bias_cols, gain, beta, wait=()):
    d = patches.shape[1]
    wide = wt.shape[0]
    width = wide // 3
    steps = LEN // FB
    whole = lambda *shape: pl.BlockSpec(shape, lambda i, c: (0,) * len(shape), pipeline_mode=pl.Buffered(1))
    tall = pl.BlockSpec((width, FB), lambda i, c: (0, i))
    return pl.pallas_call(
        ignoring(len(wait), proj_kernel),
        grid_spec=pltpu.PrefetchScalarGridSpec(
            num_scalar_prefetch=1,
            grid=(steps,),
            in_specs=[ANY] * len(wait)
            + [
                pl.BlockSpec((FB, d), lambda i, c: (seq * steps + i, 0)),
                pl.BlockSpec((2, FB), lambda i, c: (0, seq * steps + i)),
                whole(*tab.shape),
                whole(*wt.shape),
                whole(*bias_cols.shape),
                whole(1, d),
                whole(1, d),
            ],
            out_specs=[pl.BlockSpec((FB, d), lambda i, c: (i, 0)), tall, tall, tall],
        ),
        out_shape=[hbm((LEN, d), bf16)] + [jax.ShapeDtypeStruct((width, LEN), bf16)] * 3,
        compiler_params=params(16),
        cost_estimate=cost(2 * LEN * d * wide, 2 * (2 * LEN * d + wide * (d + LEN))),
        name="project",
    )(core, *stay(*wait), *stay(patches, grid, tab, wt, bias_cols), gain, beta)


def key_range(ids_all, ids_blk):
    first = jnp.min(ids_blk)
    last = jnp.max(ids_blk)
    start = jnp.sum((ids_all < first).astype(jnp.int32))
    stop = jnp.sum((ids_all <= last).astype(jnp.int32))
    return start // KB, (stop + KB - 1) // KB


def same_image(idc_ref, at, ids_blk):
    ids_k = idc_ref[pl.ds(at, KB), :]
    ids_k = jnp.concatenate([ids_k] * (ids_blk.shape[1] // 128), axis=1)
    return ids_k == ids_blk


def rows_of(ref, h):
    return ref[h * HD : (h + 1) * HD, :]


def attend_kernel(c_ref, q_ref, k_ref, v_ref, idr_ref, idq_ref, idc_ref,
                  send_ref, keep_ref, ctx_ref, lse_ref, keys, scores, acc):
    step = pl.program_id(0)
    heads = q_ref.shape[0] // HD
    half = pl.num_programs(0) // 2

    @pl.when(step == 0)
    def _():
        for h in range(heads):
            keys[h] = jnp.transpose(rows_of(k_ref, h))

    ids_q = idq_ref[...]
    lo, hi = key_range(idr_ref[...], ids_q)

    def first_pass(kb, tops):
        at = pl.multiple_of(kb * KB, KB)
        same = same_image(idc_ref, at, ids_q)
        new = []
        for h in range(heads):
            s = mm(keys[h, pl.ds(at, KB), :], rows_of(q_ref, h))
            s = jnp.where(same, s, masked_score)
            scores[h, pl.ds(at, KB), :] = s
            new.append(jnp.maximum(tops[h], jnp.max(s, axis=0, keepdims=True)))
        return tuple(new)

    tops = lax.fori_loop(lo, hi, first_pass, tuple(jnp.full((1, FB), masked_score, f32) for _ in range(heads)))
    tops = tuple(top * SCALE2 for top in tops)
    acc[...] = jnp.zeros_like(acc)

    def second_pass(kb, totals):
        at = pl.multiple_of(kb * KB, KB)
        new = []
        for h in range(heads):
            p = jnp.exp2(scores[h, pl.ds(at, KB), :] * SCALE2 - tops[h])
            new.append(totals[h] + jnp.sum(p, axis=0, keepdims=True))
            acc[h * HD : (h + 1) * HD, :] += mm(v_ref[h * HD : (h + 1) * HD, pl.ds(at, KB)], p.astype(bf16))
        return tuple(new)

    totals = lax.fori_loop(lo, hi, second_pass, tuple(jnp.zeros((1, FB), f32) for _ in range(heads)))
    lse = jnp.zeros((8, FB), f32)
    row = lax.broadcasted_iota(jnp.int32, (8, FB), 0)
    for h in range(heads):
        ctx_ref[h * HD : (h + 1) * HD, :] = acc[h * HD : (h + 1) * HD, :] * (1.0 / totals[h])
        lse = jnp.where(row == h, tops[h] + jnp.log2(totals[h]), lse)
    lse_ref[...] = lse
    partial = ctx_ref[...].astype(bf16)

    @pl.when(step < half)
    def _():
        send_ref[...] = partial

    @pl.when(step >= half)
    def _():
        keep_ref[...] = partial


def attend(seq, core, q, k, v, ids_rows, ids_cols, wait=()):
    width = q.shape[0]
    steps = LEN // FB
    half = steps // 2
    heads = width // HD
    blk = lambda i, c: lax.rem(i + half * (1 - c[0]), steps)
    whole = lambda *shape: pl.BlockSpec(shape, lambda i, c: (0,) * len(shape), pipeline_mode=pl.Buffered(1))
    return pl.pallas_call(
        ignoring(len(wait), attend_kernel),
        grid_spec=pltpu.PrefetchScalarGridSpec(
            num_scalar_prefetch=1,
            grid=(steps,),
            in_specs=[ANY] * len(wait)
            + [
                pl.BlockSpec((width, FB), lambda i, c: (0, blk(i, c))),
                whole(width, LEN),
                whole(width, LEN),
                pl.BlockSpec((None, 1, LEN), lambda i, c: (seq, 0, 0)),
                pl.BlockSpec((None, 1, FB), lambda i, c: (seq, 0, blk(i, c))),
                pl.BlockSpec((LEN, 128), lambda i, c: (seq, 0)),
            ],
            out_specs=[
                pl.BlockSpec((width, FB), lambda i, c: (0, jnp.minimum(i, half - 1))),
                pl.BlockSpec((width, FB), lambda i, c: (0, jnp.maximum(i - half, 0))),
                pl.BlockSpec((width, FB), lambda i, c: (0, blk(i, c))),
                pl.BlockSpec((8, FB), lambda i, c: (0, blk(i, c))),
            ],
            scratch_shapes=[
                pltpu.VMEM((heads, LEN, HD), bf16),
                pltpu.VMEM((heads, LEN, FB), f32),
                pltpu.VMEM((width, FB), f32),
            ],
        ),
        out_shape=[
            jax.ShapeDtypeStruct((width, LEN // 2), bf16),
            jax.ShapeDtypeStruct((width, LEN // 2), bf16),
            hbm((width, LEN), f32),
            hbm((8, LEN), f32),
        ],
        compiler_params=params(16),
        cost_estimate=cost(8 * LEN * LEN * width, 12 * LEN * width, heads * LEN * LEN),
        name="attend",
    )(core, *stay(*wait), q, k, v, ids_rows, ids_rows, ids_cols)


def norm_two_kernel(c_ref, x_ref, *refs):
    groups = (len(refs) - 5) // 2
    ctx_refs, wo_refs = refs[:groups], refs[groups : 2 * groups]
    bias_ref, gain_ref, beta_ref, resid_ref, normed_ref = refs[2 * groups :]
    attn = bias_ref[...]
    for ctx_ref, wo_ref in zip(ctx_refs, wo_refs):
        attn = attn + mm(ctx_ref[...], wo_ref[...], TN).astype(bf16).astype(f32)
    resid = x_ref[...].astype(f32) + attn
    resid_ref[...] = resid
    xhat, _ = standardize(resid)
    normed_ref[...] = (xhat * gain_ref[...] + beta_ref[...]).astype(bf16)


def norm_two(seq, core, patches, ctxs, wos, bias, gain, beta, wait=()):
    width, rows = ctxs[0].shape
    d = patches.shape[1]
    steps = rows // RB
    blk = pl.BlockSpec((RB, d), lambda i, c: (i, 0))
    whole = lambda *shape: pl.BlockSpec(shape, lambda i, c: (0,) * len(shape), pipeline_mode=pl.Buffered(1))
    return pl.pallas_call(
        ignoring(len(wait), norm_two_kernel),
        grid_spec=pltpu.PrefetchScalarGridSpec(
            num_scalar_prefetch=1,
            grid=(steps,),
            in_specs=[ANY] * len(wait)
            + [pl.BlockSpec((RB, d), lambda i, c: ((2 * seq + c[0]) * steps + i, 0))]
            + [pl.BlockSpec((width, RB), lambda i, c: (0, i))] * len(ctxs)
            + [whole(width, d)] * len(wos)
            + [whole(1, d)] * 3,
            out_specs=[blk, blk],
        ),
        out_shape=[hbm((rows, d), f32), hbm((rows, d), bf16)],
        compiler_params=params(8),
        cost_estimate=cost(2 * len(ctxs) * rows * d * width, 12 * rows * d),
        name="norm_two",
    )(core, *stay(*wait), *stay(patches), *ctxs, *wos, bias, gain, beta)


def store_halves(mine, outs, sums):
    count = outs[0].shape[0]
    for out, half in zip(outs, (1 - mine, mine)):
        for k in range(count):
            at = 0
            for acc in sums:
                rows = acc.shape[0] // (2 * count)
                spot = pl.ds(pl.multiple_of((half * count + k) * rows, 8), rows)
                out[k, at : at + rows, :] = acc[spot, :].astype(bf16)
                at += rows


def feed_kernel(first, last, c_ref, *refs):
    refs = list(refs)
    own_ref, other_ref, og_ref, up_ref, upb_ref, down_ref = refs[:6]
    refs = refs[6:]
    if not first:
        small0_ref, up0_ref, down0_ref = refs[:3]
        refs = refs[3:]
    mlp_send, mlp_keep, n2_send, n2_keep, small_out = refs[:5]
    outs = refs[5:-4]
    up_acc, down_acc, up_sum, down_sum = refs[-4:]
    step = pl.program_id(0)
    steps = pl.num_programs(0)
    half = steps // 2

    @pl.when(step == 0)
    def _():
        if first:
            up_acc[...] = jnp.zeros_like(up_acc)
            down_acc[...] = jnp.zeros_like(down_acc)
            up_sum[...] = jnp.zeros_like(up_sum)
            down_sum[...] = jnp.zeros_like(down_sum)
        else:
            up_acc[...] = up0_ref[...]
            down_acc[...] = down0_ref[...]
            up_sum[...] = small0_ref[0:1, :]
            down_sum[...] = small0_ref[1:2, :]

    normed = jnp.where(step < half, other_ref[...], own_ref[...])
    og = og_ref[...]
    pre = mm(normed, up_ref[...]) + upb_ref[...]
    phi_cap = 0.5 * (1.0 + lax.erf(pre * SQRT_HALF))
    hidden = (pre * phi_cap).astype(bf16)
    mlp = mm(hidden, down_ref[...]).astype(bf16)
    slope = phi_cap + pre * (jnp.exp(-0.5 * pre * pre) * INV_SQRT_2PI)
    grad = mm(og, down_ref[...], NT)
    pre_grad = (grad * slope).astype(bf16)
    n2 = mm(pre_grad, up_ref[...], NT).astype(bf16)
    down_acc[...] += mm(hidden, og, TN)
    up_acc[...] += mm(normed, pre_grad, TN)
    up_sum[...] += jnp.sum(pre_grad.astype(f32), axis=0, keepdims=True)
    down_sum[...] += jnp.sum(og.astype(f32), axis=0, keepdims=True)

    @pl.when(step < half)
    def _():
        mlp_send[...] = mlp
        n2_send[...] = n2

    @pl.when(step >= half)
    def _():
        mlp_keep[...] = mlp
        n2_keep[...] = n2

    @pl.when(step == steps - 1)
    def _():
        if last:
            store_halves(c_ref[1], outs, (up_acc, down_acc))
        else:
            outs[0][...] = up_acc[...]
            outs[1][...] = down_acc[...]
        small_out[0:1, :] = up_sum[...]
        small_out[1:2, :] = down_sum[...]
        small_out[2:8, :] = jnp.zeros((6, up_sum.shape[1]), f32)


def feed(seq, core, own, other, out_grad, up, up_bias, down, before=None, last=0, wait=()):
    d, units = up.shape
    steps = LEN // FB
    half = steps // 2
    first = before is None
    whole = lambda *shape: pl.BlockSpec(shape, lambda i, c: (0,) * len(shape), pipeline_mode=pl.Buffered(1))
    low = pl.BlockSpec((FB, d), lambda i, c: (jnp.minimum(i, half - 1), 0))
    high = pl.BlockSpec((FB, d), lambda i, c: (jnp.maximum(i - half, 0), 0))
    blk = lambda i, c: seq * steps + lax.rem(i + half * (1 - c[0]), steps)
    in_specs = [ANY] * len(wait) + [
        high, low,
        pl.BlockSpec((FB, d), lambda i, c: (blk(i, c), 0)),
        whole(d, units), whole(1, units), whole(units, d),
    ]
    args = [core, *stay(*wait), *stay(own), other, *stay(out_grad), up, up_bias, down]
    if not first:
        in_specs += [whole(8, d), whole(d, units), whole(units, d)]
        args += list(before)
    if last:
        grads = [(last, (d + units) // (2 * last), d)] * 2
        kind = bf16
    else:
        grads = [(d, units), (units, d)]
        kind = f32
    rows = jax.ShapeDtypeStruct((LEN // 2, d), bf16)
    return pl.pallas_call(
        ignoring(len(wait), functools.partial(feed_kernel, first, last)),
        grid_spec=pltpu.PrefetchScalarGridSpec(
            num_scalar_prefetch=1,
            grid=(steps,),
            in_specs=in_specs,
            out_specs=[low, high, low, high, whole(8, d)] + [whole(*g) for g in grads],
            scratch_shapes=[
                pltpu.VMEM((d, units), f32),
                pltpu.VMEM((units, d), f32),
                pltpu.VMEM((1, units), f32),
                pltpu.VMEM((1, d), f32),
            ],
        ),
        out_shape=[hbm(rows.shape, bf16), hbm(rows.shape, bf16), hbm(rows.shape, bf16), rows, hbm((8, d), f32)]
        + [(hbm if last else jax.ShapeDtypeStruct)(g, kind) for g in grads],
        compiler_params=params(24),
        cost_estimate=cost(12 * LEN * d * units, 2 * LEN * d * 4 + 12 * d * units, 2 * LEN * units),
        name="feed",
    )(*args)


def norm_two_back_kernel(first, c_ref, *refs):
    refs = list(refs)
    mine_ref, theirs_ref, resid_ref, og_ref, gain_ref = refs[:5]
    refs = refs[5:]
    if not first:
        small0_ref = refs[0]
        refs = refs[1:]
    rgrad_ref, branch_ref, small_ref = refs
    step = pl.program_id(0)

    @pl.when(step == 0)
    def _():
        if first:
            small_ref[...] = jnp.zeros_like(small_ref)
        else:
            small_ref[...] = small0_ref[...]

    grad = mine_ref[...].astype(f32) + theirs_ref[...].astype(f32)
    xhat, inverse = standardize(resid_ref[...])
    e = grad * gain_ref[...]
    back = inverse * (
        e - jnp.mean(e, axis=-1, keepdims=True) - xhat * jnp.mean(e * xhat, axis=-1, keepdims=True)
    )
    rgrad = og_ref[...].astype(f32) + back
    rgrad_ref[...] = rgrad
    branch = rgrad.astype(bf16)
    branch_ref[...] = branch
    small_ref[0:1, :] += jnp.sum(grad * xhat, axis=0, keepdims=True)
    small_ref[1:2, :] += jnp.sum(grad, axis=0, keepdims=True)
    small_ref[2:3, :] += jnp.sum(branch.astype(f32), axis=0, keepdims=True)


def norm_two_back(seq, core, mine, theirs, resid, out_grad, gain, before=None, wait=()):
    rows, d = mine.shape
    steps = rows // RB
    first = before is None
    blk = pl.BlockSpec((RB, d), lambda i, c: (i, 0))
    vec = pl.BlockSpec((1, d), lambda i, c: (0, 0))
    small = pl.BlockSpec((8, d), lambda i, c: (0, 0))
    in_specs = [ANY] * len(wait) + [blk, blk, blk, pl.BlockSpec((RB, d), lambda i, c: ((2 * seq + c[0]) * steps + i, 0)), vec]
    args = [core, *stay(*wait), mine, theirs, *stay(resid, out_grad), gain]
    if not first:
        in_specs.append(small)
        args += stay(before)
    return pl.pallas_call(
        ignoring(len(wait), functools.partial(norm_two_back_kernel, first)),
        grid_spec=pltpu.PrefetchScalarGridSpec(
            num_scalar_prefetch=1, grid=(steps,), in_specs=in_specs, out_specs=[blk, blk, small]
        ),
        out_shape=[
            hbm((rows, d), f32),
            jax.ShapeDtypeStruct((rows, d), bf16),
            hbm((8, d), f32),
        ],
        compiler_params=params(8),
        cost_estimate=cost(20 * rows * d, 16 * rows * d),
        name="norm_two_back",
    )(*args)


def attend_back_kernel(first, c_ref, *refs):
    refs = list(refs)
    own_ref, other_ref, q_ref, k_ref, v_ref, ctx_ref, lse_ref, idr_ref, idq_ref, idc_ref, wo_ref = refs[:11]
    refs = refs[11:]
    dwo0_ref = None if first else refs.pop(0)
    low_ref, dwo_ref, keys, vals, grads_ref = refs
    step = pl.program_id(0)
    steps = pl.num_programs(0)
    half = steps // 2
    width = q_ref.shape[0]
    heads = width // HD
    blk = lax.rem(step + half * (1 - c_ref[0]), steps)
    here = pl.ds(pl.multiple_of(blk * RB, RB), RB)

    @pl.when(step == 0)
    def _():
        for h in range(heads):
            keys[h] = jnp.transpose(rows_of(k_ref, h))
            vals[h] = jnp.transpose(rows_of(v_ref, h))
        grads_ref[...] = jnp.zeros_like(grads_ref)
        dwo_ref[...] = jnp.zeros_like(dwo_ref) if first else dwo0_ref[...]

    branch = jnp.where(step < half, other_ref[...], own_ref[...])
    ctx = ctx_ref[:, here]
    dctx = mm(wo_ref[...], branch, NT).astype(bf16)
    dwo_ref[...] += mm(ctx.astype(bf16), branch)
    prod = dctx.astype(f32) * ctx
    lse = lse_ref[:, here]
    ids_q = idq_ref[...]
    lo, hi = key_range(idr_ref[...], ids_q)
    parts = []
    for h in range(heads):
        sl = slice(h * HD, (h + 1) * HD)
        parts.append((q_ref[sl, here], dctx[sl], jnp.sum(prod[sl], axis=0, keepdims=True), lse[h : h + 1]))

    def body(kb, carry):
        at = pl.multiple_of(kb * KB, KB)
        there = pl.ds(at, KB)
        same = same_image(idc_ref, at, ids_q)
        for h in range(heads):
            q_h, do_h, delta, lse_h = parts[h]
            s = mm(keys[h, there, :], q_h)
            p = jnp.exp2(jnp.where(same, s * SCALE2 - lse_h, masked_score))
            dp = mm(vals[h, there, :], do_h)
            ds = (p * (dp - delta)).astype(bf16)
            at_q, at_k, at_v = (slice(k * width + h * HD, k * width + (h + 1) * HD) for k in range(3))
            grads_ref[at_q, here] += mm(k_ref[h * HD : (h + 1) * HD, there], ds)
            grads_ref[at_k, there] += mm(q_h, ds, NT)
            grads_ref[at_v, there] += mm(do_h, p.astype(bf16), NT)
        return carry

    lax.fori_loop(lo, hi, body, 0)

    @pl.when(step == steps - 1)
    def _():
        low_ref[...] = grads_ref[...].astype(bf16)


def attend_back(seq, core, own, other, q, k, v, ctx, lse, ids_rows, ids_cols, wo, before=None, wait=()):
    width, d = wo.shape
    heads = width // HD
    steps = LEN // RB
    half = steps // 2
    first = before is None
    whole = lambda *shape: pl.BlockSpec(shape, lambda i, c: (0,) * len(shape), pipeline_mode=pl.Buffered(1))
    blk = lambda i, c: lax.rem(i + half * (1 - c[0]), steps)
    in_specs = [ANY] * len(wait) + [
        pl.BlockSpec((RB, d), lambda i, c: (jnp.maximum(i - half, 0), 0)),
        pl.BlockSpec((RB, d), lambda i, c: (jnp.minimum(i, half - 1), 0)),
        whole(width, LEN), whole(width, LEN), whole(width, LEN), whole(width, LEN), whole(8, LEN),
        pl.BlockSpec((None, 1, LEN), lambda i, c: (seq, 0, 0)),
        pl.BlockSpec((None, 1, RB), lambda i, c: (seq, 0, blk(i, c))),
        pl.BlockSpec((LEN, 128), lambda i, c: (seq, 0)),
        whole(width, d),
    ]
    q, k, v, ctx, lse, ids_cols = stay(q, k, v, ctx, lse, ids_cols)
    args = [core, *stay(*wait), own, other, q, k, v, ctx, lse, ids_rows, ids_rows, ids_cols, wo]
    if not first:
        in_specs.append(whole(width, d))
        args += stay(before)
    return pl.pallas_call(
        ignoring(len(wait), functools.partial(attend_back_kernel, first)),
        grid_spec=pltpu.PrefetchScalarGridSpec(
            num_scalar_prefetch=1, grid=(steps,), in_specs=in_specs,
            out_specs=[whole(3 * width, LEN), whole(width, d)],
            scratch_shapes=[
                pltpu.VMEM((heads, LEN, HD), bf16), pltpu.VMEM((heads, LEN, HD), bf16), pltpu.VMEM((3 * width, LEN), f32)
            ],
        ),
        out_shape=[hbm((3 * width, LEN), bf16), hbm((width, d), f32)],
        compiler_params=params(18),
        cost_estimate=cost(
            20 * LEN * LEN * width + 8 * LEN * d * width, 2 * LEN * (10 * width + d) + 8 * d * width, heads * LEN * LEN,
        ),
        name="attend_back",
    )(*args)


def project_back_kernel(c_ref, *refs):
    seqs = (refs[:4], refs[4:8])
    (wt_ref, tab_ref, grid_ref, gain_ref, beta_ref, dwo_ref, small_two_ref, small_feed_ref) = refs[8:16]
    send_away, keep_away, send_mine, keep_mine, small_ref = refs[16:21]
    outs = refs[21:23]
    dwt_acc, col_acc, rope_acc = refs[23:]
    step = pl.program_id(0)
    steps = pl.num_programs(0) // 2
    half = steps // 2
    width = seqs[0][0].shape[0]
    heads = width // HD
    second = (step < steps) != (c_ref[2] > 0)

    def pick(k):
        return jnp.where(second, seqs[1][k][...], seqs[0][k][...])

    @pl.when(step == 0)
    def _():
        for acc in (dwt_acc, col_acc, rope_acc):
            acc[...] = jnp.zeros_like(acc)

    place = grid_ref[...]
    cosine, sine = lookup(tab_ref, place)
    grads = pick(2)
    pieces = []
    angle = [None] * heads
    for k in range(2):
        turned = pick(k)
        for h in range(heads):
            b = grads[k * width + h * HD : k * width + (h + 1) * HD].astype(f32) * SCALE
            a = turned[h * HD : (h + 1) * HD].astype(f32)
            b1, b2 = b[:HALF], b[HALF:]
            co = cosine[h * HALF : (h + 1) * HALF]
            si = sine[h * HALF : (h + 1) * HALF]
            pieces.append((b1 * co + b2 * si).astype(bf16))
            pieces.append((b2 * co - b1 * si).astype(bf16))
            term = b2 * a[:HALF] - b1 * a[HALF:]
            angle[h] = term if angle[h] is None else angle[h] + term
    pieces.append(grads[2 * width :].astype(bf16))
    mixed_grad = jnp.concatenate(pieces, axis=0)
    angle = jnp.concatenate(angle, axis=0)
    rope_acc[...] += lax.dot_general(
        place.astype(f32), angle, NT, precision=lax.Precision.HIGHEST, preferred_element_type=f32
    )
    exact = mixed_grad.astype(f32)
    folded = exact[:, 0:128]
    for at in range(128, FB, 128):
        folded = folded + exact[:, at : at + 128]
    col_acc[...] += folded
    dwt_acc[...] += mm(mixed_grad, pick(3))
    partial = mm(mixed_grad, wt_ref[...], TN).astype(bf16)
    for k, out in enumerate((send_away, keep_away, send_mine, keep_mine)):
        @pl.when(step // half == k)
        def _():
            out[...] = partial

    @pl.when(step == 2 * steps - 1)
    def _():
        raw = dwt_acc[...]
        col = jnp.sum(col_acc[...], axis=1, keepdims=True)
        row_sum = jnp.sum(jnp.transpose(col_acc[...]), axis=0, keepdims=True)
        wt = wt_ref[...].astype(f32)
        small_ref[0:1, :] = jnp.sum(wt * raw, axis=0, keepdims=True)
        small_ref[1:2, :] = jnp.sum(wt * col, axis=0, keepdims=True)
        small_ref[2:5, :] = 0.5 * small_two_ref[0:3, :]
        small_ref[5:7, :] = small_feed_ref[0:2, :]
        small_ref[7:8, :] = jnp.concatenate([row_sum, rope_acc[1:2, :], rope_acc[0:1, :]], axis=1)
        dwt_acc[...] = raw * gain_ref[...] + col * beta_ref[...]
        store_halves(c_ref[1], outs, (dwt_acc, dwo_ref))


def project_back(core, seqs, wt, tab, grid, gain, beta, dwo, small_two, small_feed, pieces, wait=()):
    d = wt.shape[1]
    width = wt.shape[0] // 3
    heads = width // HD
    steps = LEN // FB
    half = steps // 2
    whole = lambda *shape: pl.BlockSpec(shape, lambda i, c: (0,) * len(shape), pipeline_mode=pl.Buffered(1))
    blk = lambda i, c: lax.rem(lax.rem(i, steps) + half * (1 - c[0]), steps)
    now = lambda i, c: jnp.where(i < steps, 1 - c[2], c[2])

    def turn(s, i, c):
        early = s == jnp.where(c[2] > 0, 0, 1)
        rest = jnp.where(early, blk(steps - 1, c), blk(0, c))
        return jnp.where(now(i, c) == s, blk(i, c), rest)

    in_specs = [ANY] * len(wait)
    args = [core, *stay(*wait)]
    for s in range(2):
        tall = lambda i, c, s=s: (0, turn(s, i, c))
        flat = lambda i, c, s=s: (turn(s, i, c), 0)
        in_specs += [
            pl.BlockSpec((width, FB), tall), pl.BlockSpec((width, FB), tall), pl.BlockSpec((3 * width, FB), tall),
            pl.BlockSpec((FB, d), flat),
        ]
        args += stay(*seqs[s])
    in_specs += [
        whole(3 * width, d), whole(*tab.shape),
        pl.BlockSpec((2, FB), lambda i, c: (0, now(i, c) * steps + blk(i, c))),
        whole(1, d), whole(1, d), whole(width, d), whole(8, d), whole(8, d),
    ]
    args += [wt, *stay(tab, grid), gain, beta, *stay(dwo, small_two, small_feed)]
    part = lambda k: pl.BlockSpec((FB, d), lambda i, c: (jnp.clip(i - k * half, 0, half - 1), 0))
    cut = (pieces, 4 * width // (2 * pieces), d)
    rows = hbm((LEN // 2, d), bf16)
    return pl.pallas_call(
        ignoring(len(wait), project_back_kernel),
        grid_spec=pltpu.PrefetchScalarGridSpec(
            num_scalar_prefetch=1, grid=(2 * steps,), in_specs=in_specs,
            out_specs=[part(0), part(1), part(2), part(3), whole(8, d), whole(*cut), whole(*cut)],
            scratch_shapes=[
                pltpu.VMEM((3 * width, d), f32),
                pltpu.VMEM((3 * width, 128), f32),
                pltpu.VMEM((2, heads * HALF), f32),
            ],
        ),
        out_shape=[rows, rows, rows, rows, hbm((8, d), f32), hbm(cut, bf16), hbm(cut, bf16)],
        compiler_params=params(30),
        cost_estimate=cost(24 * LEN * d * width, 4 * LEN * (12 * width + 3 * d), LEN * width),
        name="project_back",
    )(*args)


def norm_one_back_kernel(m_ref, mine_ref, got_ref, theirs_ref, x_ref, rg0_ref, rg1_ref, gain_ref, out_ref):
    f = (mine_ref[...].astype(f32) + got_ref[...].astype(f32) + theirs_ref[...].astype(f32)) * gain_ref[...]
    xhat, inverse = standardize(x_ref[...].astype(f32))
    back = inverse * (
        f - jnp.mean(f, axis=-1, keepdims=True) - xhat * jnp.mean(f * xhat, axis=-1, keepdims=True)
    )
    rgrad = jnp.where(m_ref[0] < 2, rg0_ref[...], rg1_ref[...])
    out_ref[...] = (rgrad + back).astype(bf16)


def norm_one_back(place, mine, got, theirs, patches, rg0, rg1, gain):
    rows, d = mine.shape
    steps = rows // RB
    blk = pl.BlockSpec((RB, d), lambda i, m: (i, 0))
    return pl.pallas_call(
        norm_one_back_kernel,
        grid_spec=pltpu.PrefetchScalarGridSpec(
            num_scalar_prefetch=1,
            grid=(steps,),
            in_specs=[
                blk, blk, blk, pl.BlockSpec((RB, d), lambda i, m: (m[0] * steps + i, 0)), blk, blk,
                pl.BlockSpec((1, d), lambda i, m: (0, 0)),
            ],
            out_specs=blk,
        ),
        out_shape=jax.ShapeDtypeStruct((rows, d), bf16),
        compiler_params=params(10),
        cost_estimate=cost(20 * rows * d, 16 * rows * d),
        name="norm_one_back",
    )(place, mine, got, theirs, *stay(patches, rg0, rg1), gain)


CORE_SWAP = [(i, i ^ 1) for i in range(4)]
CHIP_SWAP = [(i, i ^ 2) for i in range(4)]


def core_swap(value):
    return lax.ppermute(value, "mp", CORE_SWAP)


def chip_swap(value):
    return lax.ppermute(value, "mp", CHIP_SWAP)


def after(value, *events):
    return lax.optimization_barrier((value, *events))[0]


def add_low(a, b):
    return (a.astype(f32) + b.astype(f32)).astype(bf16)


def add_kernel(c_ref, a_ref, b_ref, out_ref):
    out_ref[...] = (a_ref[...].astype(f32) + b_ref[...].astype(f32)).astype(bf16)


def full(shape):
    return pl.BlockSpec(shape, lambda i, c: (0,) * len(shape))


def add_parts(core, a, b, wait=()):
    return pl.pallas_call(
        ignoring(len(wait), add_kernel),
        grid_spec=pltpu.PrefetchScalarGridSpec(
            num_scalar_prefetch=1, grid=(1,), in_specs=[ANY] * len(wait) + [full(a.shape)] * 2, out_specs=full(a.shape),
        ),
        out_shape=hbm(a.shape, bf16),
        compiler_params=params(10),
        cost_estimate=cost(a.size, 6 * a.size),
        name="add_parts",
    )(core, *stay(*wait), *stay(a), b)


def sum_parts_kernel(c_ref, parts_ref, *refs):
    out_ref = refs[-1]
    total = parts_ref[0].astype(f32)
    for k in range(1, parts_ref.shape[0]):
        total = total + parts_ref[k].astype(f32)
    rows = total.shape[0]
    total = total.astype(bf16)
    for k in range(out_ref.shape[0]):
        out_ref[k, 0:rows, :] = total
    if len(refs) > 1:
        small = refs[0][...]
        high = small.astype(bf16)
        low = (small - high.astype(f32)).astype(bf16)
        for k in range(out_ref.shape[0]):
            out_ref[k, rows : rows + 8, :] = high
            out_ref[k, rows + 8 : rows + 16, :] = low


def sum_parts(core, parts, small=None, copies=None, wait=()):
    count, rows, d = parts.shape
    extra = () if small is None else (small,)
    out = (copies or count, rows + 16 * len(extra), d)
    return pl.pallas_call(
        ignoring(len(wait), sum_parts_kernel),
        grid_spec=pltpu.PrefetchScalarGridSpec(
            num_scalar_prefetch=1, grid=(1,),
            in_specs=[ANY] * len(wait) + [full(parts.shape)] + [full(e.shape) for e in extra],
            out_specs=full(out),
        ),
        out_shape=jax.ShapeDtypeStruct(out, bf16),
        compiler_params=params(10),
        cost_estimate=cost(count * rows * d, 4 * count * rows * d),
        name="sum_parts",
    )(core, *stay(*wait), parts, *extra)


def place_parts_kernel(with_small, c_ref, mine_ref, theirs_ref, *refs):
    outs = refs[: len(refs) - with_small]
    count = mine_ref.shape[0]
    small = None
    for ref, half in ((mine_ref, c_ref[1]), (theirs_ref, 1 - c_ref[1])):
        for k in range(count):
            at = 0
            for out in outs:
                rows = out.shape[0] // (2 * count)
                spot = pl.ds(pl.multiple_of((half * count + k) * rows, 8), rows)
                out[spot, :] = ref[k, at : at + rows, :].astype(f32)
                at += rows
            if with_small:
                part = ref[k, at : at + 8, :].astype(f32) + ref[k, at + 8 : at + 16, :].astype(f32)
                small = part if small is None else small + part
    if with_small:
        refs[-1][...] = small


def place_parts(core, mine, theirs, splits, with_small=False):
    d = mine.shape[2]
    shapes = [(rows, d) for rows in splits] + [(8, d)] * with_small
    return pl.pallas_call(
        functools.partial(place_parts_kernel, with_small),
        grid_spec=pltpu.PrefetchScalarGridSpec(
            num_scalar_prefetch=1, grid=(1,), in_specs=[full(mine.shape)] * 2, out_specs=[full(t) for t in shapes],
        ),
        out_shape=[jax.ShapeDtypeStruct(t, f32) for t in shapes],
        compiler_params=params(18),
        cost_estimate=cost(sum(splits) * d, 6 * sum(splits) * d),
        name="place_parts",
    )(core, mine, theirs)


def half_swap(value):
    return lax.ppermute(value, "dp", [(i, i ^ 1) for i in range(lax.axis_size("dp"))])


def quarter_trade(parts):
    return lax.all_to_all(parts, "dp", 0, 0, axis_index_groups=[[0, 2, 4, 6], [1, 3, 5, 7]])


def hold(values, *events):
    return list(lax.optimization_barrier((*values, *events))[: len(values)])


def local(patches, image_ids, patch_grid, first_norm_gain, first_norm_bias, qkv_weight, qkv_bias, rope_freq,
          out_weight, out_bias, second_norm_gain, second_norm_bias, up_weight, up_bias, down_weight, down_bias,
          out_grad):
    all_rows, d = patches.shape
    seqs = all_rows // LEN
    assert lax.axis_size("mp") == 4 and seqs == 2
    devices = lax.axis_size("dp")
    tree = devices == 8
    pieces = 4 if tree else 1
    heads = rope_freq.shape[0]
    width = heads * HD
    units = up_weight.shape[1]
    place = lax.axis_index("mp").astype(jnp.int32)
    half = lax.axis_index("dp").astype(jnp.int32) % 2 if tree else jnp.int32(0)
    core = jnp.stack([place % 2, half, place // 2])
    place_arr = place.reshape(1)
    far = place >= 2
    row = lambda v: v.reshape(1, -1)

    tab, bias_cols = prepare(rope_freq, qkv_bias)
    wt = qkv_weight.transpose(1, 2, 0).reshape(3 * width, d)
    ids_rows = image_ids.reshape(seqs, 1, LEN)
    ids_cols = jnp.broadcast_to(image_ids[:, None], (all_rows, 128))
    gain1, beta1 = row(first_norm_gain), row(first_norm_bias)
    gain2, beta2 = row(second_norm_gain), row(second_norm_bias)

    wo_core = core_swap(out_weight)
    proj_args = (patches, patch_grid, tab, wt, bias_cols, gain1, beta1)
    made0 = project(0, core, *proj_args)
    send0, keep0, ctx0, lse0 = attend(0, core, *made0[1:], ids_rows, ids_cols)
    core0, far_keep0 = core_swap(send0), chip_swap(keep0)
    made1 = project(1, core, *proj_args, wait=[lse0, wo_core])
    far_core0, wo_far = chip_swap(core0), chip_swap(out_weight)
    send1, keep1, ctx1, lse1 = attend(1, core, *made1[1:], ids_rows, ids_cols, wait=[made1[0]])
    core1, far_keep1 = core_swap(send1), chip_swap(keep1)
    wos = [out_weight, wo_core, wo_far, core_swap(wo_far)]
    norm_args = (row(out_bias), gain2, beta2)
    resid0, normed0 = norm_two(
        0, core, patches, [keep0, core0, far_keep0, far_core0], wos, *norm_args, wait=[lse1]
    )
    normed0, core1, far_keep1 = hold([normed0, core1, far_keep1])
    far_core1 = chip_swap(core1)
    feed_args = (out_grad, up_weight, row(up_bias), down_weight)
    mlp_send0, mlp_keep0, n2_send0, n2_keep0, *sums = feed(
        0, core, normed0, core_swap(normed0), *feed_args
    )
    n2_send0, far_core1 = hold([n2_send0, far_core1])
    n20 = add_low(n2_keep0, core_swap(n2_send0))
    resid1, normed1 = norm_two(
        1, core, patches, [keep1, core1, far_keep1, far_core1], wos, *norm_args, wait=[sums[0]]
    )
    n2_far0 = chip_swap(n20)
    mlp_send1, mlp_keep1, n2_send1, n2_keep1, small_feed, feed_send, feed_keep = feed(
        1, core, normed1, core_swap(normed1), *feed_args, before=sums, last=pieces, wait=[n20]
    )
    if tree:
        feed_got = half_swap(feed_send)
    n21 = add_low(n2_keep1, core_swap(n2_send1))
    mlp0 = add_low(mlp_keep0, core_swap(mlp_send0))
    mlp1 = add_low(mlp_keep1, core_swap(mlp_send1))
    mlp_away, mlp_mine = jnp.where(far, mlp0, mlp1), jnp.where(far, mlp1, mlp0)
    rgrad0, branch0, small_two = norm_two_back(
        0, core, n20, n2_far0, resid0, out_grad, gain2, wait=[small_feed]
    )
    n2_far1 = chip_swap(n21)
    grads0, dwo = attend_back(
        0, core, branch0, core_swap(branch0), *made0[1:], ctx0, lse0, ids_rows, ids_cols, out_weight, wait=[n21]
    )
    event = dwo
    if tree:
        feed_part = add_parts(core, feed_keep, feed_got, wait=[dwo, n2_far1])
        event = feed_part
        feed_got = quarter_trade(feed_part)
    rgrad1, branch1, small_two = norm_two_back(
        1, core, n21, n2_far1, resid1, out_grad, gain2, before=small_two, wait=[event]
    )
    mlp_theirs = chip_swap(mlp_away)
    grads1, dwo = attend_back(
        1, core, branch1, core_swap(branch1), *made1[1:], ctx1, lse1, ids_rows, ids_cols, out_weight, before=dwo,
        wait=[mlp_away],
    )
    event = dwo
    if tree:
        feed_sum = sum_parts(core, feed_got, wait=[dwo, mlp_theirs])
        event = feed_sum
        feed_all = quarter_trade(feed_sum)
    n1_send_away, n1_away, n1_send, n1_keep, small, grad_send, grad_keep = project_back(
        core, [(*made[1:3], grads, made[0]) for made, grads in ((made0, grads0), (made1, grads1))],
        wt, tab, patch_grid, gain1, beta1, dwo, small_two, small_feed, pieces, wait=[event],
    )
    n1_away = add_low(n1_away, core_swap(n1_send_away))
    n1_got = core_swap(n1_send)
    shared = lax.broadcasted_iota(jnp.int32, small.shape, 0) < 5
    for swap in (core_swap, chip_swap):
        small = small + jnp.where(shared, swap(small), 0.0)
    theirs = chip_swap(after(n1_away, small))
    if tree:
        grad_got = half_swap(grad_send)
        grad_got = quarter_trade(add_parts(core, grad_keep, grad_got, wait=[feed_all]))
        feed_other = half_swap(feed_all)
        grad_sum = quarter_trade(sum_parts(core, grad_got, small, wait=[feed_other]))
        grad_other = half_swap(grad_sum)
    else:
        small, grad_send, grad_keep, feed_send, feed_keep = lax.psum(
            (small, grad_send, grad_keep, feed_send, feed_keep), "dp"
        )
        feed_all, feed_other = feed_keep, feed_send
        grad_sum = sum_parts(core, grad_keep, small)
        grad_other = sum_parts(core, grad_send, jnp.zeros_like(small))

    out_rows = (
        jnp.where(far, resid1, resid0)
        + (mlp_mine.astype(f32) + mlp_theirs.astype(f32))
        + row(down_bias)
    ).astype(bf16)
    grad_rows = norm_one_back(place_arr, n1_keep, n1_got, theirs, patches, rgrad0, rgrad1, gain1)
    up_grad, down_grad = place_parts(core, feed_all, feed_other, (d, units))
    (grad_other,) = hold([grad_other], grad_rows)
    qkv_grad, out_grad_w, small = place_parts(core, grad_sum, grad_other, (3 * width, width), True)
    turns = heads * HALF
    by_col = small[7, 3 * width : 3 * width + turns].reshape(heads, HALF)
    by_row = small[7, 3 * width + turns : 3 * width + 2 * turns].reshape(heads, HALF)
    return (
        out_rows,
        grad_rows,
        small[0],
        small[1],
        qkv_grad.reshape(3, width, d).transpose(2, 0, 1),
        small[7, : 3 * width].reshape(3, width),
        jnp.concatenate([by_col, by_row], axis=-1),
        out_grad_w,
        small[4],
        small[2],
        small[3],
        up_grad,
        small[5],
        down_grad,
        small[6],
    )


def solution(mesh):
    placed = (
        P("dp", None),
        P("dp"),
        P(None, "dp"),
        P(),
        P(),
        P(None, None, "mp"),
        P(None, "mp"),
        P("mp", None),
        P("mp", None),
        P(),
        P(),
        P(),
        P(None, "mp"),
        P("mp"),
        P("mp", None),
        P(),
        P("dp", None),
    )
    return jax.shard_map(
        local,
        mesh=mesh,
        in_specs=placed,
        out_specs=(
            P(("dp", "mp"), None),
            P(("dp", "mp"), None),
            P(),
            P(),
            P(None, None, "mp"),
            P(None, "mp"),
            P("mp", None),
            P("mp", None),
            P(),
            P(),
            P(),
            P(None, "mp"),
            P("mp"),
            P("mp", None),
            P(),
        ),
        check_vma=False,
    )
```

```python
import functools
import math

import jax
import jax.numpy as jnp
from jax import lax
from jax.experimental import pallas as pl
from jax.experimental.pallas import tpu as pltpu
from jax.sharding import PartitionSpec as P

LEN = 1024
HD = 64
HALF = HD // 2
RB = 256
KB = 512
FB = 512

masked_score = -1e30
epsilon = 1e-06
SCALE = HD ** (-0.5)
SCALE2 = SCALE * math.log2(math.e)
SQRT_HALF = math.sqrt(0.5)
INV_SQRT_2PI = 1.0 / math.sqrt(2.0 * math.pi)

f32 = jnp.float32
bf16 = jnp.bfloat16

NN = (((1,), (0,)), ((), ()))
NT = (((1,), (1,)), ((), ()))
TN = (((0,), (0,)), ((), ()))


def mm(a, b, dims=NN):
    return lax.dot_general(a, b, dims, preferred_element_type=f32)


ANY = pl.BlockSpec(memory_space=pl.ANY)


def ignoring(count, kernel):
    return lambda c_ref, *refs: kernel(c_ref, *refs[count:])


def params(mib):
    return pltpu.CompilerParams(
        dimension_semantics=("arbitrary",), vmem_limit_bytes=mib * 1024 * 1024
    )


def hbm(shape, dtype):
    return pltpu.HBM(shape, dtype)


def stay(*arrays):
    return [pltpu.with_memory_space_constraint(a, pltpu.HBM) for a in arrays]


def cost(flops, nbytes, trans=0):
    return pl.CostEstimate(flops=int(flops) // 4, bytes_accessed=int(nbytes) // 4, transcendentals=int(trans) // 4)


def standardize(values):
    center = jnp.mean(values, axis=-1, keepdims=True)
    centered = values - center
    spread = jnp.mean(centered * centered, axis=-1, keepdims=True)
    inverse = lax.rsqrt(spread + epsilon)
    return centered * inverse, inverse


def column(row):
    n = row.shape[1]
    here = lax.broadcasted_iota(jnp.int32, (n, n), 0) == lax.broadcasted_iota(jnp.int32, (n, n), 1)
    return jnp.sum(jnp.where(here, row, 0.0), axis=1, keepdims=True)


def prepare_kernel(freq_ref, bias_ref, tab_ref, cols_ref):
    heads = freq_ref.shape[0]
    n = heads * HALF
    lane = lax.broadcasted_iota(jnp.int32, (HALF, 128), 1)
    spot = (lane & 31).astype(f32)
    part = lane >> 5
    for h in range(heads):
        freq = column(freq_ref[h : h + 1, :])
        for axis in range(2):
            angle = spot * freq[axis * HALF : (axis + 1) * HALF]
            for k, val in enumerate((jnp.cos(angle), jnp.sin(angle))):
                high = val.astype(bf16).astype(f32)
                rest = val - high
                mid = rest.astype(bf16).astype(f32)
                low = (rest - mid).astype(bf16).astype(f32)
                out = jnp.where(part == 0, high, jnp.where(part == 1, mid, jnp.where(part == 2, low, 0.0)))
                at = (axis * 2 + k) * n + h * HALF
                tab_ref[at : at + HALF, :] = out.astype(bf16)
    width = bias_ref.shape[1]
    for k in range(3):
        for h in range(heads):
            col = column(bias_ref[k : k + 1, h * HD : (h + 1) * HD])
            cols_ref[k * width + h * HD : k * width + (h + 1) * HD, :] = jnp.broadcast_to(col, (HD, 128))


def prepare(freq, bias):
    heads = freq.shape[0]
    return pl.pallas_call(
        prepare_kernel,
        out_shape=[
            jax.ShapeDtypeStruct((4 * heads * HALF, 128), bf16),
            jax.ShapeDtypeStruct((bias.shape[0] * bias.shape[1], 128), f32),
        ],
        name="prepare",
    )(freq, bias)


def lookup(tab_ref, grid_blk):
    n = tab_ref.shape[0] // 4
    rows = grid_blk.shape[1]
    spot = lax.broadcasted_iota(jnp.int32, (128, rows), 0) & 31
    one_r = jnp.where(spot == grid_blk[0:1, :], 1.0, 0.0).astype(bf16)
    one_c = jnp.where(spot == grid_blk[1:2, :], 1.0, 0.0).astype(bf16)
    by_c = mm(tab_ref[0 : 2 * n, :], one_c)
    by_r = mm(tab_ref[2 * n : 4 * n, :], one_r)
    cc, sc = by_c[:n], by_c[n:]
    cr, sr = by_r[:n], by_r[n:]
    return cc * cr - sc * sr, sc * cr + cc * sr


def proj_kernel(c_ref, x_ref, grid_ref, tab_ref, wt_ref, bias_ref, gain_ref, beta_ref, xhat_ref, q_ref, k_ref, v_ref):
    width = q_ref.shape[0]
    xhat, _ = standardize(x_ref[...].astype(f32))
    xhat_ref[...] = xhat.astype(bf16)
    normed = (xhat * gain_ref[...] + beta_ref[...]).astype(bf16)
    mixed = mm(wt_ref[...], normed, NT) + bias_ref[:, 0:1]
    cosine, sine = lookup(tab_ref, grid_ref[...])
    for which, ref in ((0, q_ref), (1, k_ref)):
        for h in range(width // HD):
            at = which * width + h * HD
            a1 = mixed[at : at + HALF]
            a2 = mixed[at + HALF : at + HD]
            c = cosine[h * HALF : (h + 1) * HALF]
            s = sine[h * HALF : (h + 1) * HALF]
            ref[h * HD : h * HD + HALF, :] = (a1 * c - a2 * s).astype(bf16)
            ref[h * HD + HALF : (h + 1) * HD, :] = (a1 * s + a2 * c).astype(bf16)
    v_ref[...] = mixed[2 * width : 3 * width].astype(bf16)


def project(seq, core, patches, grid, tab, wt, bias_cols, gain, beta, wait=()):
    d = patches.shape[1]
    wide = wt.shape[0]
    width = wide // 3
    steps = LEN // FB
    whole = lambda *shape: pl.BlockSpec(shape, lambda i, c: (0,) * len(shape), pipeline_mode=pl.Buffered(1))
    tall = pl.BlockSpec((width, FB), lambda i, c: (0, i))
    return pl.pallas_call(
        ignoring(len(wait), proj_kernel),
        grid_spec=pltpu.PrefetchScalarGridSpec(
            num_scalar_prefetch=1,
            grid=(steps,),
            in_specs=[ANY] * len(wait)
            + [
                pl.BlockSpec((FB, d), lambda i, c: (seq * steps + i, 0)),
                pl.BlockSpec((2, FB), lambda i, c: (0, seq * steps + i)),
                whole(*tab.shape),
                whole(*wt.shape),
                whole(*bias_cols.shape),
                whole(1, d),
                whole(1, d),
            ],
            out_specs=[pl.BlockSpec((FB, d), lambda i, c: (i, 0)), tall, tall, tall],
        ),
        out_shape=[hbm((LEN, d), bf16)] + [jax.ShapeDtypeStruct((width, LEN), bf16)] * 3,
        compiler_params=params(16),
        cost_estimate=cost(2 * LEN * d * wide, 2 * (2 * LEN * d + wide * (d + LEN))),
        name="project",
    )(core, *stay(*wait), *stay(patches, grid, tab, wt, bias_cols), gain, beta)


def key_range(ids_all, ids_blk):
    first = jnp.min(ids_blk)
    last = jnp.max(ids_blk)
    start = jnp.sum((ids_all < first).astype(jnp.int32))
    stop = jnp.sum((ids_all <= last).astype(jnp.int32))
    return start // KB, (stop + KB - 1) // KB


def same_image(idc_ref, at, ids_blk):
    ids_k = idc_ref[pl.ds(at, KB), :]
    ids_k = jnp.concatenate([ids_k] * (ids_blk.shape[1] // 128), axis=1)
    return ids_k == ids_blk


def rows_of(ref, h):
    return ref[h * HD : (h + 1) * HD, :]


def attend_kernel(c_ref, q_ref, k_ref, v_ref, idr_ref, idq_ref, idc_ref,
                  send_ref, keep_ref, ctx_ref, lse_ref, keys, scores, acc):
    step = pl.program_id(0)
    heads = q_ref.shape[0] // HD
    half = pl.num_programs(0) // 2

    @pl.when(step == 0)
    def _():
        for h in range(heads):
            keys[h] = jnp.transpose(rows_of(k_ref, h))

    ids_q = idq_ref[...]
    lo, hi = key_range(idr_ref[...], ids_q)

    def first_pass(kb, tops):
        at = pl.multiple_of(kb * KB, KB)
        same = same_image(idc_ref, at, ids_q)
        new = []
        for h in range(heads):
            s = mm(keys[h, pl.ds(at, KB), :], rows_of(q_ref, h))
            s = jnp.where(same, s, masked_score)
            scores[h, pl.ds(at, KB), :] = s
            new.append(jnp.maximum(tops[h], jnp.max(s, axis=0, keepdims=True)))
        return tuple(new)

    tops = lax.fori_loop(lo, hi, first_pass, tuple(jnp.full((1, FB), masked_score, f32) for _ in range(heads)))
    tops = tuple(top * SCALE2 for top in tops)
    acc[...] = jnp.zeros_like(acc)

    def second_pass(kb, totals):
        at = pl.multiple_of(kb * KB, KB)
        new = []
        for h in range(heads):
            p = jnp.exp2(scores[h, pl.ds(at, KB), :] * SCALE2 - tops[h])
            new.append(totals[h] + jnp.sum(p, axis=0, keepdims=True))
            acc[h * HD : (h + 1) * HD, :] += mm(v_ref[h * HD : (h + 1) * HD, pl.ds(at, KB)], p.astype(bf16))
        return tuple(new)

    totals = lax.fori_loop(lo, hi, second_pass, tuple(jnp.zeros((1, FB), f32) for _ in range(heads)))
    lse = jnp.zeros((8, FB), f32)
    row = lax.broadcasted_iota(jnp.int32, (8, FB), 0)
    for h in range(heads):
        ctx_ref[h * HD : (h + 1) * HD, :] = acc[h * HD : (h + 1) * HD, :] * (1.0 / totals[h])
        lse = jnp.where(row == h, tops[h] + jnp.log2(totals[h]), lse)
    lse_ref[...] = lse
    partial = ctx_ref[...].astype(bf16)

    @pl.when(step < half)
    def _():
        send_ref[...] = partial

    @pl.when(step >= half)
    def _():
        keep_ref[...] = partial


def attend(seq, core, q, k, v, ids_rows, ids_cols, wait=()):
    width = q.shape[0]
    steps = LEN // FB
    half = steps // 2
    heads = width // HD
    blk = lambda i, c: lax.rem(i + half * (1 - c[0]), steps)
    whole = lambda *shape: pl.BlockSpec(shape, lambda i, c: (0,) * len(shape), pipeline_mode=pl.Buffered(1))
    return pl.pallas_call(
        ignoring(len(wait), attend_kernel),
        grid_spec=pltpu.PrefetchScalarGridSpec(
            num_scalar_prefetch=1,
            grid=(steps,),
            in_specs=[ANY] * len(wait)
            + [
                pl.BlockSpec((width, FB), lambda i, c: (0, blk(i, c))),
                whole(width, LEN),
                whole(width, LEN),
                pl.BlockSpec((None, 1, LEN), lambda i, c: (seq, 0, 0)),
                pl.BlockSpec((None, 1, FB), lambda i, c: (seq, 0, blk(i, c))),
                pl.BlockSpec((LEN, 128), lambda i, c: (seq, 0)),
            ],
            out_specs=[
                pl.BlockSpec((width, FB), lambda i, c: (0, jnp.minimum(i, half - 1))),
                pl.BlockSpec((width, FB), lambda i, c: (0, jnp.maximum(i - half, 0))),
                pl.BlockSpec((width, FB), lambda i, c: (0, blk(i, c))),
                pl.BlockSpec((8, FB), lambda i, c: (0, blk(i, c))),
            ],
            scratch_shapes=[
                pltpu.VMEM((heads, LEN, HD), bf16),
                pltpu.VMEM((heads, LEN, FB), f32),
                pltpu.VMEM((width, FB), f32),
            ],
        ),
        out_shape=[
            jax.ShapeDtypeStruct((width, LEN // 2), bf16),
            jax.ShapeDtypeStruct((width, LEN // 2), bf16),
            hbm((width, LEN), f32),
            hbm((8, LEN), f32),
        ],
        compiler_params=params(16),
        cost_estimate=cost(8 * LEN * LEN * width, 12 * LEN * width, heads * LEN * LEN),
        name="attend",
    )(core, *stay(*wait), q, k, v, ids_rows, ids_rows, ids_cols)


def norm_two_kernel(c_ref, x_ref, *refs):
    groups = (len(refs) - 5) // 2
    ctx_refs, wo_refs = refs[:groups], refs[groups : 2 * groups]
    bias_ref, gain_ref, beta_ref, resid_ref, normed_ref = refs[2 * groups :]
    attn = bias_ref[...]
    for ctx_ref, wo_ref in zip(ctx_refs, wo_refs):
        attn = attn + mm(ctx_ref[...], wo_ref[...], TN).astype(bf16).astype(f32)
    resid = x_ref[...].astype(f32) + attn
    resid_ref[...] = resid
    xhat, _ = standardize(resid)
    normed_ref[...] = (xhat * gain_ref[...] + beta_ref[...]).astype(bf16)


def norm_two(seq, core, patches, ctxs, wos, bias, gain, beta, wait=()):
    width, rows = ctxs[0].shape
    d = patches.shape[1]
    steps = rows // RB
    blk = pl.BlockSpec((RB, d), lambda i, c: (i, 0))
    whole = lambda *shape: pl.BlockSpec(shape, lambda i, c: (0,) * len(shape), pipeline_mode=pl.Buffered(1))
    return pl.pallas_call(
        ignoring(len(wait), norm_two_kernel),
        grid_spec=pltpu.PrefetchScalarGridSpec(
            num_scalar_prefetch=1,
            grid=(steps,),
            in_specs=[ANY] * len(wait)
            + [pl.BlockSpec((RB, d), lambda i, c: ((2 * seq + c[0]) * steps + i, 0))]
            + [pl.BlockSpec((width, RB), lambda i, c: (0, i))] * len(ctxs)
            + [whole(width, d)] * len(wos)
            + [whole(1, d)] * 3,
            out_specs=[blk, blk],
        ),
        out_shape=[hbm((rows, d), f32), hbm((rows, d), bf16)],
        compiler_params=params(8),
        cost_estimate=cost(2 * len(ctxs) * rows * d * width, 12 * rows * d),
        name="norm_two",
    )(core, *stay(*wait), *stay(patches), *ctxs, *wos, bias, gain, beta)


def store_halves(mine, outs, sums):
    count = outs[0].shape[0]
    for out, half in zip(outs, (1 - mine, mine)):
        for k in range(count):
            at = 0
            for acc in sums:
                rows = acc.shape[0] // (2 * count)
                spot = pl.ds(pl.multiple_of((half * count + k) * rows, 8), rows)
                out[k, at : at + rows, :] = acc[spot, :].astype(bf16)
                at += rows


def feed_kernel(first, last, c_ref, *refs):
    refs = list(refs)
    own_ref, other_ref, og_ref, up_ref, upb_ref, down_ref = refs[:6]
    refs = refs[6:]
    if not first:
        small0_ref, up0_ref, down0_ref = refs[:3]
        refs = refs[3:]
    mlp_send, mlp_keep, n2_send, n2_keep, small_out = refs[:5]
    outs = refs[5:-4]
    up_acc, down_acc, up_sum, down_sum = refs[-4:]
    step = pl.program_id(0)
    steps = pl.num_programs(0)
    half = steps // 2

    @pl.when(step == 0)
    def _():
        if first:
            up_acc[...] = jnp.zeros_like(up_acc)
            down_acc[...] = jnp.zeros_like(down_acc)
            up_sum[...] = jnp.zeros_like(up_sum)
            down_sum[...] = jnp.zeros_like(down_sum)
        else:
            up_acc[...] = up0_ref[...]
            down_acc[...] = down0_ref[...]
            up_sum[...] = small0_ref[0:1, :]
            down_sum[...] = small0_ref[1:2, :]

    normed = jnp.where(step < half, other_ref[...], own_ref[...])
    og = og_ref[...]
    pre = mm(normed, up_ref[...]) + upb_ref[...]
    phi_cap = 0.5 * (1.0 + lax.erf(pre * SQRT_HALF))
    hidden = (pre * phi_cap).astype(bf16)
    mlp = mm(hidden, down_ref[...]).astype(bf16)
    slope = phi_cap + pre * (jnp.exp(-0.5 * pre * pre) * INV_SQRT_2PI)
    grad = mm(og, down_ref[...], NT)
    pre_grad = (grad * slope).astype(bf16)
    n2 = mm(pre_grad, up_ref[...], NT).astype(bf16)
    down_acc[...] += mm(hidden, og, TN)
    up_acc[...] += mm(normed, pre_grad, TN)
    up_sum[...] += jnp.sum(pre_grad.astype(f32), axis=0, keepdims=True)
    down_sum[...] += jnp.sum(og.astype(f32), axis=0, keepdims=True)

    @pl.when(step < half)
    def _():
        mlp_send[...] = mlp
        n2_send[...] = n2

    @pl.when(step >= half)
    def _():
        mlp_keep[...] = mlp
        n2_keep[...] = n2

    @pl.when(step == steps - 1)
    def _():
        if last:
            store_halves(c_ref[1], outs, (up_acc, down_acc))
        else:
            outs[0][...] = up_acc[...]
            outs[1][...] = down_acc[...]
        small_out[0:1, :] = up_sum[...]
        small_out[1:2, :] = down_sum[...]
        small_out[2:8, :] = jnp.zeros((6, up_sum.shape[1]), f32)


def feed(seq, core, own, other, out_grad, up, up_bias, down, before=None, last=0, wait=()):
    d, units = up.shape
    steps = LEN // FB
    half = steps // 2
    first = before is None
    whole = lambda *shape: pl.BlockSpec(shape, lambda i, c: (0,) * len(shape), pipeline_mode=pl.Buffered(1))
    low = pl.BlockSpec((FB, d), lambda i, c: (jnp.minimum(i, half - 1), 0))
    high = pl.BlockSpec((FB, d), lambda i, c: (jnp.maximum(i - half, 0), 0))
    blk = lambda i, c: seq * steps + lax.rem(i + half * (1 - c[0]), steps)
    in_specs = [ANY] * len(wait) + [
        high, low,
        pl.BlockSpec((FB, d), lambda i, c: (blk(i, c), 0)),
        whole(d, units), whole(1, units), whole(units, d),
    ]
    args = [core, *stay(*wait), *stay(own), other, *stay(out_grad), up, up_bias, down]
    if not first:
        in_specs += [whole(8, d), whole(d, units), whole(units, d)]
        args += list(before)
    if last:
        grads = [(last, (d + units) // (2 * last), d)] * 2
        kind = bf16
    else:
        grads = [(d, units), (units, d)]
        kind = f32
    rows = jax.ShapeDtypeStruct((LEN // 2, d), bf16)
    return pl.pallas_call(
        ignoring(len(wait), functools.partial(feed_kernel, first, last)),
        grid_spec=pltpu.PrefetchScalarGridSpec(
            num_scalar_prefetch=1,
            grid=(steps,),
            in_specs=in_specs,
            out_specs=[low, high, low, high, whole(8, d)] + [whole(*g) for g in grads],
            scratch_shapes=[
                pltpu.VMEM((d, units), f32),
                pltpu.VMEM((units, d), f32),
                pltpu.VMEM((1, units), f32),
                pltpu.VMEM((1, d), f32),
            ],
        ),
        out_shape=[hbm(rows.shape, bf16), hbm(rows.shape, bf16), hbm(rows.shape, bf16), rows, hbm((8, d), f32)]
        + [(hbm if last else jax.ShapeDtypeStruct)(g, kind) for g in grads],
        compiler_params=params(24),
        cost_estimate=cost(12 * LEN * d * units, 2 * LEN * d * 4 + 12 * d * units, 2 * LEN * units),
        name="feed",
    )(*args)


def norm_two_back_kernel(first, c_ref, *refs):
    refs = list(refs)
    mine_ref, theirs_ref, resid_ref, og_ref, gain_ref = refs[:5]
    refs = refs[5:]
    if not first:
        small0_ref = refs[0]
        refs = refs[1:]
    rgrad_ref, branch_ref, small_ref = refs
    step = pl.program_id(0)

    @pl.when(step == 0)
    def _():
        if first:
            small_ref[...] = jnp.zeros_like(small_ref)
        else:
            small_ref[...] = small0_ref[...]

    grad = mine_ref[...].astype(f32) + theirs_ref[...].astype(f32)
    xhat, inverse = standardize(resid_ref[...])
    e = grad * gain_ref[...]
    back = inverse * (
        e - jnp.mean(e, axis=-1, keepdims=True) - xhat * jnp.mean(e * xhat, axis=-1, keepdims=True)
    )
    rgrad = og_ref[...].astype(f32) + back
    rgrad_ref[...] = rgrad
    branch = rgrad.astype(bf16)
    branch_ref[...] = branch
    small_ref[0:1, :] += jnp.sum(grad * xhat, axis=0, keepdims=True)
    small_ref[1:2, :] += jnp.sum(grad, axis=0, keepdims=True)
    small_ref[2:3, :] += jnp.sum(branch.astype(f32), axis=0, keepdims=True)


def norm_two_back(seq, core, mine, theirs, resid, out_grad, gain, before=None, wait=()):
    rows, d = mine.shape
    steps = rows // RB
    first = before is None
    blk = pl.BlockSpec((RB, d), lambda i, c: (i, 0))
    vec = pl.BlockSpec((1, d), lambda i, c: (0, 0))
    small = pl.BlockSpec((8, d), lambda i, c: (0, 0))
    in_specs = [ANY] * len(wait) + [blk, blk, blk, pl.BlockSpec((RB, d), lambda i, c: ((2 * seq + c[0]) * steps + i, 0)), vec]
    args = [core, *stay(*wait), mine, theirs, *stay(resid, out_grad), gain]
    if not first:
        in_specs.append(small)
        args += stay(before)
    return pl.pallas_call(
        ignoring(len(wait), functools.partial(norm_two_back_kernel, first)),
        grid_spec=pltpu.PrefetchScalarGridSpec(
            num_scalar_prefetch=1, grid=(steps,), in_specs=in_specs, out_specs=[blk, blk, small]
        ),
        out_shape=[
            hbm((rows, d), f32),
            jax.ShapeDtypeStruct((rows, d), bf16),
            hbm((8, d), f32),
        ],
        compiler_params=params(8),
        cost_estimate=cost(20 * rows * d, 16 * rows * d),
        name="norm_two_back",
    )(*args)


def attend_back_kernel(first, c_ref, *refs):
    refs = list(refs)
    own_ref, other_ref, q_ref, k_ref, v_ref, ctx_ref, lse_ref, idr_ref, idq_ref, idc_ref, wo_ref = refs[:11]
    refs = refs[11:]
    dwo0_ref = None if first else refs.pop(0)
    low_ref, dwo_ref, keys, vals, grads_ref = refs
    step = pl.program_id(0)
    steps = pl.num_programs(0)
    half = steps // 2
    width = q_ref.shape[0]
    heads = width // HD
    blk = lax.rem(step + half * (1 - c_ref[0]), steps)
    here = pl.ds(pl.multiple_of(blk * RB, RB), RB)

    @pl.when(step == 0)
    def _():
        for h in range(heads):
            keys[h] = jnp.transpose(rows_of(k_ref, h))
            vals[h] = jnp.transpose(rows_of(v_ref, h))
        grads_ref[...] = jnp.zeros_like(grads_ref)
        dwo_ref[...] = jnp.zeros_like(dwo_ref) if first else dwo0_ref[...]

    branch = jnp.where(step < half, other_ref[...], own_ref[...])
    ctx = ctx_ref[:, here]
    dctx = mm(wo_ref[...], branch, NT).astype(bf16)
    dwo_ref[...] += mm(ctx.astype(bf16), branch)
    prod = dctx.astype(f32) * ctx
    lse = lse_ref[:, here]
    ids_q = idq_ref[...]
    lo, hi = key_range(idr_ref[...], ids_q)
    parts = []
    for h in range(heads):
        sl = slice(h * HD, (h + 1) * HD)
        parts.append((q_ref[sl, here], dctx[sl], jnp.sum(prod[sl], axis=0, keepdims=True), lse[h : h + 1]))

    def body(kb, carry):
        at = pl.multiple_of(kb * KB, KB)
        there = pl.ds(at, KB)
        same = same_image(idc_ref, at, ids_q)
        for h in range(heads):
            q_h, do_h, delta, lse_h = parts[h]
            s = mm(keys[h, there, :], q_h)
            p = jnp.exp2(jnp.where(same, s * SCALE2 - lse_h, masked_score))
            dp = mm(vals[h, there, :], do_h)
            ds = (p * (dp - delta)).astype(bf16)
            at_q, at_k, at_v = (slice(k * width + h * HD, k * width + (h + 1) * HD) for k in range(3))
            grads_ref[at_q, here] += mm(k_ref[h * HD : (h + 1) * HD, there], ds)
            grads_ref[at_k, there] += mm(q_h, ds, NT)
            grads_ref[at_v, there] += mm(do_h, p.astype(bf16), NT)
        return carry

    lax.fori_loop(lo, hi, body, 0)

    @pl.when(step == steps - 1)
    def _():
        low_ref[...] = grads_ref[...].astype(bf16)


def attend_back(seq, core, own, other, q, k, v, ctx, lse, ids_rows, ids_cols, wo, before=None, wait=()):
    width, d = wo.shape
    heads = width // HD
    steps = LEN // RB
    half = steps // 2
    first = before is None
    whole = lambda *shape: pl.BlockSpec(shape, lambda i, c: (0,) * len(shape), pipeline_mode=pl.Buffered(1))
    blk = lambda i, c: lax.rem(i + half * (1 - c[0]), steps)
    in_specs = [ANY] * len(wait) + [
        pl.BlockSpec((RB, d), lambda i, c: (jnp.maximum(i - half, 0), 0)),
        pl.BlockSpec((RB, d), lambda i, c: (jnp.minimum(i, half - 1), 0)),
        whole(width, LEN), whole(width, LEN), whole(width, LEN), whole(width, LEN), whole(8, LEN),
        pl.BlockSpec((None, 1, LEN), lambda i, c: (seq, 0, 0)),
        pl.BlockSpec((None, 1, RB), lambda i, c: (seq, 0, blk(i, c))),
        pl.BlockSpec((LEN, 128), lambda i, c: (seq, 0)),
        whole(width, d),
    ]
    q, k, v, ctx, lse, ids_cols = stay(q, k, v, ctx, lse, ids_cols)
    args = [core, *stay(*wait), own, other, q, k, v, ctx, lse, ids_rows, ids_rows, ids_cols, wo]
    if not first:
        in_specs.append(whole(width, d))
        args += stay(before)
    return pl.pallas_call(
        ignoring(len(wait), functools.partial(attend_back_kernel, first)),
        grid_spec=pltpu.PrefetchScalarGridSpec(
            num_scalar_prefetch=1, grid=(steps,), in_specs=in_specs,
            out_specs=[whole(3 * width, LEN), whole(width, d)],
            scratch_shapes=[
                pltpu.VMEM((heads, LEN, HD), bf16), pltpu.VMEM((heads, LEN, HD), bf16), pltpu.VMEM((3 * width, LEN), f32)
            ],
        ),
        out_shape=[hbm((3 * width, LEN), bf16), hbm((width, d), f32)],
        compiler_params=params(18),
        cost_estimate=cost(
            20 * LEN * LEN * width + 8 * LEN * d * width, 2 * LEN * (10 * width + d) + 8 * d * width, heads * LEN * LEN,
        ),
        name="attend_back",
    )(*args)


def project_back_kernel(c_ref, *refs):
    seqs = (refs[:4], refs[4:8])
    (wt_ref, tab_ref, grid_ref, gain_ref, beta_ref, dwo_ref, small_two_ref, small_feed_ref) = refs[8:16]
    send_away, keep_away, send_mine, keep_mine, small_ref = refs[16:21]
    outs = refs[21:23]
    dwt_acc, col_acc, rope_acc = refs[23:]
    step = pl.program_id(0)
    steps = pl.num_programs(0) // 2
    half = steps // 2
    width = seqs[0][0].shape[0]
    heads = width // HD
    second = (step < steps) != (c_ref[2] > 0)

    def pick(k):
        return jnp.where(second, seqs[1][k][...], seqs[0][k][...])

    @pl.when(step == 0)
    def _():
        for acc in (dwt_acc, col_acc, rope_acc):
            acc[...] = jnp.zeros_like(acc)

    place = grid_ref[...]
    cosine, sine = lookup(tab_ref, place)
    grads = pick(2)
    pieces = []
    angle = [None] * heads
    for k in range(2):
        turned = pick(k)
        for h in range(heads):
            b = grads[k * width + h * HD : k * width + (h + 1) * HD].astype(f32) * SCALE
            a = turned[h * HD : (h + 1) * HD].astype(f32)
            b1, b2 = b[:HALF], b[HALF:]
            co = cosine[h * HALF : (h + 1) * HALF]
            si = sine[h * HALF : (h + 1) * HALF]
            pieces.append((b1 * co + b2 * si).astype(bf16))
            pieces.append((b2 * co - b1 * si).astype(bf16))
            term = b2 * a[:HALF] - b1 * a[HALF:]
            angle[h] = term if angle[h] is None else angle[h] + term
    pieces.append(grads[2 * width :].astype(bf16))
    mixed_grad = jnp.concatenate(pieces, axis=0)
    angle = jnp.concatenate(angle, axis=0)
    rope_acc[...] += lax.dot_general(
        place.astype(f32), angle, NT, precision=lax.Precision.HIGHEST, preferred_element_type=f32
    )
    exact = mixed_grad.astype(f32)
    folded = exact[:, 0:128]
    for at in range(128, FB, 128):
        folded = folded + exact[:, at : at + 128]
    col_acc[...] += folded
    dwt_acc[...] += mm(mixed_grad, pick(3))
    partial = mm(mixed_grad, wt_ref[...], TN).astype(bf16)
    for k, out in enumerate((send_away, keep_away, send_mine, keep_mine)):
        @pl.when(step // half == k)
        def _():
            out[...] = partial

    @pl.when(step == 2 * steps - 1)
    def _():
        raw = dwt_acc[...]
        col = jnp.sum(col_acc[...], axis=1, keepdims=True)
        row_sum = jnp.sum(jnp.transpose(col_acc[...]), axis=0, keepdims=True)
        wt = wt_ref[...].astype(f32)
        small_ref[0:1, :] = jnp.sum(wt * raw, axis=0, keepdims=True)
        small_ref[1:2, :] = jnp.sum(wt * col, axis=0, keepdims=True)
        small_ref[2:5, :] = 0.5 * small_two_ref[0:3, :]
        small_ref[5:7, :] = small_feed_ref[0:2, :]
        small_ref[7:8, :] = jnp.concatenate([row_sum, rope_acc[1:2, :], rope_acc[0:1, :]], axis=1)
        dwt_acc[...] = raw * gain_ref[...] + col * beta_ref[...]
        store_halves(c_ref[1], outs, (dwt_acc, dwo_ref))


def project_back(core, seqs, wt, tab, grid, gain, beta, dwo, small_two, small_feed, pieces, wait=()):
    d = wt.shape[1]
    width = wt.shape[0] // 3
    heads = width // HD
    steps = LEN // FB
    half = steps // 2
    whole = lambda *shape: pl.BlockSpec(shape, lambda i, c: (0,) * len(shape), pipeline_mode=pl.Buffered(1))
    blk = lambda i, c: lax.rem(lax.rem(i, steps) + half * (1 - c[0]), steps)
    now = lambda i, c: jnp.where(i < steps, 1 - c[2], c[2])

    def turn(s, i, c):
        early = s == jnp.where(c[2] > 0, 0, 1)
        rest = jnp.where(early, blk(steps - 1, c), blk(0, c))
        return jnp.where(now(i, c) == s, blk(i, c), rest)

    in_specs = [ANY] * len(wait)
    args = [core, *stay(*wait)]
    for s in range(2):
        tall = lambda i, c, s=s: (0, turn(s, i, c))
        flat = lambda i, c, s=s: (turn(s, i, c), 0)
        in_specs += [
            pl.BlockSpec((width, FB), tall), pl.BlockSpec((width, FB), tall), pl.BlockSpec((3 * width, FB), tall),
            pl.BlockSpec((FB, d), flat),
        ]
        args += stay(*seqs[s])
    in_specs += [
        whole(3 * width, d), whole(*tab.shape),
        pl.BlockSpec((2, FB), lambda i, c: (0, now(i, c) * steps + blk(i, c))),
        whole(1, d), whole(1, d), whole(width, d), whole(8, d), whole(8, d),
    ]
    args += [wt, *stay(tab, grid), gain, beta, *stay(dwo, small_two, small_feed)]
    part = lambda k: pl.BlockSpec((FB, d), lambda i, c: (jnp.clip(i - k * half, 0, half - 1), 0))
    cut = (pieces, 4 * width // (2 * pieces), d)
    rows = hbm((LEN // 2, d), bf16)
    return pl.pallas_call(
        ignoring(len(wait), project_back_kernel),
        grid_spec=pltpu.PrefetchScalarGridSpec(
            num_scalar_prefetch=1, grid=(2 * steps,), in_specs=in_specs,
            out_specs=[part(0), part(1), part(2), part(3), whole(8, d), whole(*cut), whole(*cut)],
            scratch_shapes=[
                pltpu.VMEM((3 * width, d), f32),
                pltpu.VMEM((3 * width, 128), f32),
                pltpu.VMEM((2, heads * HALF), f32),
            ],
        ),
        out_shape=[rows, rows, rows, rows, hbm((8, d), f32), hbm(cut, bf16), hbm(cut, bf16)],
        compiler_params=params(30),
        cost_estimate=cost(24 * LEN * d * width, 4 * LEN * (12 * width + 3 * d), LEN * width),
        name="project_back",
    )(*args)


def norm_one_back_kernel(m_ref, mine_ref, got_ref, theirs_ref, x_ref, rg0_ref, rg1_ref, gain_ref, out_ref):
    f = (mine_ref[...].astype(f32) + got_ref[...].astype(f32) + theirs_ref[...].astype(f32)) * gain_ref[...]
    xhat, inverse = standardize(x_ref[...].astype(f32))
    back = inverse * (
        f - jnp.mean(f, axis=-1, keepdims=True) - xhat * jnp.mean(f * xhat, axis=-1, keepdims=True)
    )
    rgrad = jnp.where(m_ref[0] < 2, rg0_ref[...], rg1_ref[...])
    out_ref[...] = (rgrad + back).astype(bf16)


def norm_one_back(place, mine, got, theirs, patches, rg0, rg1, gain):
    rows, d = mine.shape
    steps = rows // RB
    blk = pl.BlockSpec((RB, d), lambda i, m: (i, 0))
    return pl.pallas_call(
        norm_one_back_kernel,
        grid_spec=pltpu.PrefetchScalarGridSpec(
            num_scalar_prefetch=1,
            grid=(steps,),
            in_specs=[
                blk, blk, blk, pl.BlockSpec((RB, d), lambda i, m: (m[0] * steps + i, 0)), blk, blk,
                pl.BlockSpec((1, d), lambda i, m: (0, 0)),
            ],
            out_specs=blk,
        ),
        out_shape=jax.ShapeDtypeStruct((rows, d), bf16),
        compiler_params=params(10),
        cost_estimate=cost(20 * rows * d, 16 * rows * d),
        name="norm_one_back",
    )(place, mine, got, theirs, *stay(patches, rg0, rg1), gain)


CORE_SWAP = [(i, i ^ 1) for i in range(4)]
CHIP_SWAP = [(i, i ^ 2) for i in range(4)]


def core_swap(value):
    return lax.ppermute(value, "mp", CORE_SWAP)


def chip_swap(value):
    return lax.ppermute(value, "mp", CHIP_SWAP)


def after(value, *events):
    return lax.optimization_barrier((value, *events))[0]


def add_low(a, b):
    return (a.astype(f32) + b.astype(f32)).astype(bf16)


def add_kernel(c_ref, a_ref, b_ref, out_ref):
    out_ref[...] = (a_ref[...].astype(f32) + b_ref[...].astype(f32)).astype(bf16)


def full(shape):
    return pl.BlockSpec(shape, lambda i, c: (0,) * len(shape))


def add_parts(core, a, b, wait=()):
    return pl.pallas_call(
        ignoring(len(wait), add_kernel),
        grid_spec=pltpu.PrefetchScalarGridSpec(
            num_scalar_prefetch=1, grid=(1,), in_specs=[ANY] * len(wait) + [full(a.shape)] * 2, out_specs=full(a.shape),
        ),
        out_shape=hbm(a.shape, bf16),
        compiler_params=params(10),
        cost_estimate=cost(a.size, 6 * a.size),
        name="add_parts",
    )(core, *stay(*wait), *stay(a), b)


def sum_parts_kernel(c_ref, parts_ref, *refs):
    out_ref = refs[-1]
    total = parts_ref[0].astype(f32)
    for k in range(1, parts_ref.shape[0]):
        total = total + parts_ref[k].astype(f32)
    rows = total.shape[0]
    total = total.astype(bf16)
    for k in range(out_ref.shape[0]):
        out_ref[k, 0:rows, :] = total
    if len(refs) > 1:
        small = refs[0][...]
        high = small.astype(bf16)
        low = (small - high.astype(f32)).astype(bf16)
        for k in range(out_ref.shape[0]):
            out_ref[k, rows : rows + 8, :] = high
            out_ref[k, rows + 8 : rows + 16, :] = low


def sum_parts(core, parts, small=None, copies=None, wait=()):
    count, rows, d = parts.shape
    extra = () if small is None else (small,)
    out = (copies or count, rows + 16 * len(extra), d)
    return pl.pallas_call(
        ignoring(len(wait), sum_parts_kernel),
        grid_spec=pltpu.PrefetchScalarGridSpec(
            num_scalar_prefetch=1, grid=(1,),
            in_specs=[ANY] * len(wait) + [full(parts.shape)] + [full(e.shape) for e in extra],
            out_specs=full(out),
        ),
        out_shape=jax.ShapeDtypeStruct(out, bf16),
        compiler_params=params(10),
        cost_estimate=cost(count * rows * d, 4 * count * rows * d),
        name="sum_parts",
    )(core, *stay(*wait), parts, *extra)


def place_parts_kernel(with_small, c_ref, mine_ref, theirs_ref, *refs):
    outs = refs[: len(refs) - 3 * with_small]
    count = mine_ref.shape[0]
    small = None
    for ref, half in ((mine_ref, c_ref[1]), (theirs_ref, 1 - c_ref[1])):
        for k in range(count):
            at = 0
            for out in outs:
                rows = out.shape[0] // (2 * count)
                spot = pl.ds(pl.multiple_of((half * count + k) * rows, 8), rows)
                out[spot, :] = ref[k, at : at + rows, :].astype(f32)
                at += rows
            if with_small:
                part = ref[k, at : at + 8, :].astype(f32) + ref[k, at + 8 : at + 16, :].astype(f32)
                small = part if small is None else small + part
    if with_small:
        small_ref, bias_ref, rope_ref = refs[-3:]
        small_ref[...] = small
        width = bias_ref.shape[1]
        heads = rope_ref.shape[0]
        for k in range(3):
            bias_ref[k : k + 1, :] = small[7:8, k * width : (k + 1) * width]
        for h in range(heads):
            for k in range(2):
                at = 3 * width + (k * heads + h) * HALF
                rope_ref[h : h + 1, k * HALF : (k + 1) * HALF] = small[7:8, at : at + HALF]


def place_parts(core, mine, theirs, splits, with_small=()):
    d = mine.shape[2]
    shapes = [(rows, d) for rows in splits] + list(with_small)
    return pl.pallas_call(
        functools.partial(place_parts_kernel, bool(with_small)),
        grid_spec=pltpu.PrefetchScalarGridSpec(
            num_scalar_prefetch=1, grid=(1,), in_specs=[full(mine.shape)] * 2, out_specs=[full(t) for t in shapes],
        ),
        out_shape=[jax.ShapeDtypeStruct(t, f32) for t in shapes],
        compiler_params=params(18),
        cost_estimate=cost(sum(splits) * d, 6 * sum(splits) * d),
        name="place_parts",
    )(core, mine, theirs)


def half_swap(value):
    return lax.ppermute(value, "dp", [(i, i ^ 1) for i in range(lax.axis_size("dp"))])


def quarter_trade(parts):
    return lax.all_to_all(parts, "dp", 0, 0, axis_index_groups=[[0, 2, 4, 6], [1, 3, 5, 7]])


def hold(values, *events):
    return list(lax.optimization_barrier((*values, *events))[: len(values)])


def local(patches, image_ids, patch_grid, first_norm_gain, first_norm_bias, qkv_weight, qkv_bias, rope_freq,
          out_weight, out_bias, second_norm_gain, second_norm_bias, up_weight, up_bias, down_weight, down_bias,
          out_grad):
    all_rows, d = patches.shape
    seqs = all_rows // LEN
    assert lax.axis_size("mp") == 4 and seqs == 2
    devices = lax.axis_size("dp")
    tree = devices == 8
    pieces = 4 if tree else 1
    heads = rope_freq.shape[0]
    width = heads * HD
    units = up_weight.shape[1]
    place = lax.axis_index("mp").astype(jnp.int32)
    half = lax.axis_index("dp").astype(jnp.int32) % 2 if tree else jnp.int32(0)
    core = jnp.stack([place % 2, half, place // 2])
    place_arr = place.reshape(1)
    far = place >= 2
    row = lambda v: v.reshape(1, -1)

    tab, bias_cols = prepare(rope_freq, qkv_bias)
    wt = qkv_weight.transpose(1, 2, 0).reshape(3 * width, d)
    ids_rows = image_ids.reshape(seqs, 1, LEN)
    ids_cols = jnp.broadcast_to(image_ids[:, None], (all_rows, 128))
    gain1, beta1 = row(first_norm_gain), row(first_norm_bias)
    gain2, beta2 = row(second_norm_gain), row(second_norm_bias)

    wo_core = core_swap(out_weight)
    proj_args = (patches, patch_grid, tab, wt, bias_cols, gain1, beta1)
    made0 = project(0, core, *proj_args)
    send0, keep0, ctx0, lse0 = attend(0, core, *made0[1:], ids_rows, ids_cols)
    core0, far_keep0 = core_swap(send0), chip_swap(keep0)
    made1 = project(1, core, *proj_args, wait=[lse0, wo_core])
    far_core0, wo_far = chip_swap(core0), chip_swap(out_weight)
    send1, keep1, ctx1, lse1 = attend(1, core, *made1[1:], ids_rows, ids_cols, wait=[made1[0]])
    core1, far_keep1 = core_swap(send1), chip_swap(keep1)
    wos = [out_weight, wo_core, wo_far, core_swap(wo_far)]
    norm_args = (row(out_bias), gain2, beta2)
    resid0, normed0 = norm_two(
        0, core, patches, [keep0, core0, far_keep0, far_core0], wos, *norm_args, wait=[lse1]
    )
    normed0, core1, far_keep1 = hold([normed0, core1, far_keep1])
    far_core1 = chip_swap(core1)
    feed_args = (out_grad, up_weight, row(up_bias), down_weight)
    mlp_send0, mlp_keep0, n2_send0, n2_keep0, *sums = feed(
        0, core, normed0, core_swap(normed0), *feed_args
    )
    n2_send0, far_core1 = hold([n2_send0, far_core1])
    n20 = add_low(n2_keep0, core_swap(n2_send0))
    resid1, normed1 = norm_two(
        1, core, patches, [keep1, core1, far_keep1, far_core1], wos, *norm_args, wait=[sums[0]]
    )
    n2_far0 = chip_swap(n20)
    mlp_send1, mlp_keep1, n2_send1, n2_keep1, small_feed, feed_send, feed_keep = feed(
        1, core, normed1, core_swap(normed1), *feed_args, before=sums, last=pieces, wait=[n20]
    )
    if tree:
        feed_got = half_swap(feed_send)
    n21 = add_low(n2_keep1, core_swap(n2_send1))
    mlp0 = add_low(mlp_keep0, core_swap(mlp_send0))
    mlp1 = add_low(mlp_keep1, core_swap(mlp_send1))
    mlp_away, mlp_mine = jnp.where(far, mlp0, mlp1), jnp.where(far, mlp1, mlp0)
    rgrad0, branch0, small_two = norm_two_back(
        0, core, n20, n2_far0, resid0, out_grad, gain2, wait=[small_feed]
    )
    n2_far1 = chip_swap(n21)
    grads0, dwo = attend_back(
        0, core, branch0, core_swap(branch0), *made0[1:], ctx0, lse0, ids_rows, ids_cols, out_weight, wait=[n21]
    )
    event = dwo
    if tree:
        feed_part = add_low(feed_keep, after(feed_got, dwo, n2_far1))
        event = feed_part
        feed_got = quarter_trade(feed_part)
    rgrad1, branch1, small_two = norm_two_back(
        1, core, n21, n2_far1, resid1, out_grad, gain2, before=small_two, wait=[event]
    )
    mlp_theirs = chip_swap(mlp_away)
    grads1, dwo = attend_back(
        1, core, branch1, core_swap(branch1), *made1[1:], ctx1, lse1, ids_rows, ids_cols, out_weight, before=dwo,
        wait=[mlp_away],
    )
    event = dwo
    if tree:
        feed_sum = sum_parts(core, feed_got, wait=[dwo, mlp_theirs])
        event = feed_sum
        feed_all = quarter_trade(feed_sum)
    n1_send_away, n1_away, n1_send, n1_keep, small, grad_send, grad_keep = project_back(
        core, [(*made[1:3], grads, made[0]) for made, grads in ((made0, grads0), (made1, grads1))],
        wt, tab, patch_grid, gain1, beta1, dwo, small_two, small_feed, pieces, wait=[event],
    )
    n1_away = add_low(n1_away, core_swap(n1_send_away))
    n1_got = core_swap(n1_send)
    shared = lax.broadcasted_iota(jnp.int32, small.shape, 0) < 5
    for swap in (core_swap, chip_swap):
        small = small + jnp.where(shared, swap(small), 0.0)
    theirs = chip_swap(after(n1_away, small))
    if tree:
        grad_got = half_swap(grad_send)
        grad_got = quarter_trade(add_parts(core, grad_keep, grad_got, wait=[feed_all]))
        feed_other = half_swap(feed_all)
        grad_sum = quarter_trade(sum_parts(core, grad_got, small, wait=[feed_other]))
        grad_other = half_swap(grad_sum)
    else:
        small, grad_send, grad_keep, feed_send, feed_keep = lax.psum(
            (small, grad_send, grad_keep, feed_send, feed_keep), "dp"
        )
        feed_all, feed_other = feed_keep, feed_send
        grad_sum = sum_parts(core, grad_keep, small)
        grad_other = sum_parts(core, grad_send, jnp.zeros_like(small))

    out_rows = (
        jnp.where(far, resid1, resid0)
        + (mlp_mine.astype(f32) + mlp_theirs.astype(f32))
        + row(down_bias)
    ).astype(bf16)
    grad_rows = norm_one_back(place_arr, n1_keep, n1_got, theirs, patches, rgrad0, rgrad1, gain1)
    up_grad, down_grad = place_parts(core, feed_all, feed_other, (d, units))
    (grad_other,) = hold([grad_other], grad_rows)
    qkv_grad, out_grad_w, small, bias_grad, rope_grad = place_parts(
        core, grad_sum, grad_other, (3 * width, width), ((8, d), (3, width), (heads, HD))
    )
    return (
        out_rows,
        grad_rows,
        small[0],
        small[1],
        qkv_grad.reshape(3, width, d).transpose(2, 0, 1),
        bias_grad,
        rope_grad,
        out_grad_w,
        small[4],
        small[2],
        small[3],
        up_grad,
        small[5],
        down_grad,
        small[6],
    )


def solution(mesh):
    placed = (
        P("dp", None),
        P("dp"),
        P(None, "dp"),
        P(),
        P(),
        P(None, None, "mp"),
        P(None, "mp"),
        P("mp", None),
        P("mp", None),
        P(),
        P(),
        P(),
        P(None, "mp"),
        P("mp"),
        P("mp", None),
        P(),
        P("dp", None),
    )
    return jax.shard_map(
        local,
        mesh=mesh,
        in_specs=placed,
        out_specs=(
            P(("dp", "mp"), None),
            P(("dp", "mp"), None),
            P(),
            P(),
            P(None, None, "mp"),
            P(None, "mp"),
            P("mp", None),
            P("mp", None),
            P(),
            P(),
            P(),
            P(None, "mp"),
            P("mp"),
            P("mp", None),
            P(),
        ),
        check_vma=False,
    )
```

```python
import functools
import math

import jax
import jax.numpy as jnp
from jax import lax
from jax.experimental import pallas as pl
from jax.experimental.pallas import tpu as pltpu
from jax.sharding import PartitionSpec as P

LEN = 1024
HD = 64
HALF = HD // 2
RB = 256
KB = 512
FB = 512

masked_score = -1e30
epsilon = 1e-06
SCALE = HD ** (-0.5)
SCALE2 = SCALE * math.log2(math.e)
SQRT_HALF = math.sqrt(0.5)
INV_SQRT_2PI = 1.0 / math.sqrt(2.0 * math.pi)

f32 = jnp.float32
bf16 = jnp.bfloat16

NN = (((1,), (0,)), ((), ()))
NT = (((1,), (1,)), ((), ()))
TN = (((0,), (0,)), ((), ()))


def mm(a, b, dims=NN):
    return lax.dot_general(a, b, dims, preferred_element_type=f32)


ANY = pl.BlockSpec(memory_space=pl.ANY)


def ignoring(count, kernel):
    return lambda c_ref, *refs: kernel(c_ref, *refs[count:])


def params(mib):
    return pltpu.CompilerParams(
        dimension_semantics=("arbitrary",), vmem_limit_bytes=mib * 1024 * 1024
    )


def hbm(shape, dtype):
    return pltpu.HBM(shape, dtype)


def stay(*arrays):
    return [pltpu.with_memory_space_constraint(a, pltpu.HBM) for a in arrays]


def cost(flops, nbytes, trans=0):
    return pl.CostEstimate(flops=int(flops) // 4, bytes_accessed=int(nbytes) // 4, transcendentals=int(trans) // 4)


def standardize(values):
    center = jnp.mean(values, axis=-1, keepdims=True)
    centered = values - center
    spread = jnp.mean(centered * centered, axis=-1, keepdims=True)
    inverse = lax.rsqrt(spread + epsilon)
    return centered * inverse, inverse


def column(row):
    n = row.shape[1]
    here = lax.broadcasted_iota(jnp.int32, (n, n), 0) == lax.broadcasted_iota(jnp.int32, (n, n), 1)
    return jnp.sum(jnp.where(here, row, 0.0), axis=1, keepdims=True)


def prepare_kernel(freq_ref, bias_ref, tab_ref, cols_ref):
    heads = freq_ref.shape[0]
    n = heads * HALF
    lane = lax.broadcasted_iota(jnp.int32, (HALF, 128), 1)
    spot = (lane & 31).astype(f32)
    part = lane >> 5
    for h in range(heads):
        freq = column(freq_ref[h : h + 1, :])
        for axis in range(2):
            angle = spot * freq[axis * HALF : (axis + 1) * HALF]
            for k, val in enumerate((jnp.cos(angle), jnp.sin(angle))):
                high = val.astype(bf16).astype(f32)
                rest = val - high
                mid = rest.astype(bf16).astype(f32)
                low = (rest - mid).astype(bf16).astype(f32)
                out = jnp.where(part == 0, high, jnp.where(part == 1, mid, jnp.where(part == 2, low, 0.0)))
                at = (axis * 2 + k) * n + h * HALF
                tab_ref[at : at + HALF, :] = out.astype(bf16)
    width = bias_ref.shape[1]
    for k in range(3):
        for h in range(heads):
            col = column(bias_ref[k : k + 1, h * HD : (h + 1) * HD])
            cols_ref[k * width + h * HD : k * width + (h + 1) * HD, :] = jnp.broadcast_to(col, (HD, 128))


def prepare(freq, bias):
    heads = freq.shape[0]
    return pl.pallas_call(
        prepare_kernel,
        out_shape=[
            jax.ShapeDtypeStruct((4 * heads * HALF, 128), bf16),
            jax.ShapeDtypeStruct((bias.shape[0] * bias.shape[1], 128), f32),
        ],
        name="prepare",
    )(freq, bias)


def lookup(tab_ref, grid_blk):
    n = tab_ref.shape[0] // 4
    rows = grid_blk.shape[1]
    spot = lax.broadcasted_iota(jnp.int32, (128, rows), 0) & 31
    one_r = jnp.where(spot == grid_blk[0:1, :], 1.0, 0.0).astype(bf16)
    one_c = jnp.where(spot == grid_blk[1:2, :], 1.0, 0.0).astype(bf16)
    by_c = mm(tab_ref[0 : 2 * n, :], one_c)
    by_r = mm(tab_ref[2 * n : 4 * n, :], one_r)
    cc, sc = by_c[:n], by_c[n:]
    cr, sr = by_r[:n], by_r[n:]
    return cc * cr - sc * sr, sc * cr + cc * sr


def proj_kernel(c_ref, x_ref, grid_ref, tab_ref, wt_ref, bias_ref, gain_ref, beta_ref, xhat_ref, q_ref, k_ref, v_ref):
    width = q_ref.shape[0]
    xhat, _ = standardize(x_ref[...].astype(f32))
    xhat_ref[...] = xhat.astype(bf16)
    normed = (xhat * gain_ref[...] + beta_ref[...]).astype(bf16)
    mixed = mm(wt_ref[...], normed, NT) + bias_ref[:, 0:1]
    cosine, sine = lookup(tab_ref, grid_ref[...])
    for which, ref in ((0, q_ref), (1, k_ref)):
        for h in range(width // HD):
            at = which * width + h * HD
            a1 = mixed[at : at + HALF]
            a2 = mixed[at + HALF : at + HD]
            c = cosine[h * HALF : (h + 1) * HALF]
            s = sine[h * HALF : (h + 1) * HALF]
            ref[h * HD : h * HD + HALF, :] = (a1 * c - a2 * s).astype(bf16)
            ref[h * HD + HALF : (h + 1) * HD, :] = (a1 * s + a2 * c).astype(bf16)
    v_ref[...] = mixed[2 * width : 3 * width].astype(bf16)


def project(seq, core, patches, grid, tab, wt, bias_cols, gain, beta, wait=()):
    d = patches.shape[1]
    wide = wt.shape[0]
    width = wide // 3
    steps = LEN // FB
    whole = lambda *shape: pl.BlockSpec(shape, lambda i, c: (0,) * len(shape), pipeline_mode=pl.Buffered(1))
    tall = pl.BlockSpec((width, FB), lambda i, c: (0, i))
    return pl.pallas_call(
        ignoring(len(wait), proj_kernel),
        grid_spec=pltpu.PrefetchScalarGridSpec(
            num_scalar_prefetch=1,
            grid=(steps,),
            in_specs=[ANY] * len(wait)
            + [
                pl.BlockSpec((FB, d), lambda i, c: (seq * steps + i, 0)),
                pl.BlockSpec((2, FB), lambda i, c: (0, seq * steps + i)),
                whole(*tab.shape),
                whole(*wt.shape),
                whole(*bias_cols.shape),
                whole(1, d),
                whole(1, d),
            ],
            out_specs=[pl.BlockSpec((FB, d), lambda i, c: (i, 0)), tall, tall, tall],
        ),
        out_shape=[hbm((LEN, d), bf16)] + [jax.ShapeDtypeStruct((width, LEN), bf16)] * 3,
        compiler_params=params(16),
        cost_estimate=cost(2 * LEN * d * wide, 2 * (2 * LEN * d + wide * (d + LEN))),
        name="project",
    )(core, *stay(*wait), *stay(patches, grid, tab, wt, bias_cols), gain, beta)


def key_range(ids_all, ids_blk):
    first = jnp.min(ids_blk)
    last = jnp.max(ids_blk)
    start = jnp.sum((ids_all < first).astype(jnp.int32))
    stop = jnp.sum((ids_all <= last).astype(jnp.int32))
    return start // KB, (stop + KB - 1) // KB


def same_image(idc_ref, at, ids_blk):
    ids_k = idc_ref[pl.ds(at, KB), :]
    ids_k = jnp.concatenate([ids_k] * (ids_blk.shape[1] // 128), axis=1)
    return ids_k == ids_blk


def rows_of(ref, h):
    return ref[h * HD : (h + 1) * HD, :]


def attend_kernel(c_ref, q_ref, k_ref, v_ref, idr_ref, idq_ref, idc_ref,
                  send_ref, keep_ref, ctx_ref, lse_ref, keys, scores, acc):
    step = pl.program_id(0)
    heads = q_ref.shape[0] // HD
    half = pl.num_programs(0) // 2

    @pl.when(step == 0)
    def _():
        for h in range(heads):
            keys[h] = jnp.transpose(rows_of(k_ref, h))

    ids_q = idq_ref[...]
    lo, hi = key_range(idr_ref[...], ids_q)

    def first_pass(kb, tops):
        at = pl.multiple_of(kb * KB, KB)
        same = same_image(idc_ref, at, ids_q)
        new = []
        for h in range(heads):
            s = mm(keys[h, pl.ds(at, KB), :], rows_of(q_ref, h))
            s = jnp.where(same, s, masked_score)
            scores[h, pl.ds(at, KB), :] = s
            new.append(jnp.maximum(tops[h], jnp.max(s, axis=0, keepdims=True)))
        return tuple(new)

    tops = lax.fori_loop(lo, hi, first_pass, tuple(jnp.full((1, FB), masked_score, f32) for _ in range(heads)))
    tops = tuple(top * SCALE2 for top in tops)
    acc[...] = jnp.zeros_like(acc)

    def second_pass(kb, totals):
        at = pl.multiple_of(kb * KB, KB)
        new = []
        for h in range(heads):
            p = jnp.exp2(scores[h, pl.ds(at, KB), :] * SCALE2 - tops[h])
            new.append(totals[h] + jnp.sum(p, axis=0, keepdims=True))
            acc[h * HD : (h + 1) * HD, :] += mm(v_ref[h * HD : (h + 1) * HD, pl.ds(at, KB)], p.astype(bf16))
        return tuple(new)

    totals = lax.fori_loop(lo, hi, second_pass, tuple(jnp.zeros((1, FB), f32) for _ in range(heads)))
    lse = jnp.zeros((8, FB), f32)
    row = lax.broadcasted_iota(jnp.int32, (8, FB), 0)
    for h in range(heads):
        ctx_ref[h * HD : (h + 1) * HD, :] = acc[h * HD : (h + 1) * HD, :] * (1.0 / totals[h])
        lse = jnp.where(row == h, tops[h] + jnp.log2(totals[h]), lse)
    lse_ref[...] = lse
    partial = ctx_ref[...].astype(bf16)

    @pl.when(step < half)
    def _():
        send_ref[...] = partial

    @pl.when(step >= half)
    def _():
        keep_ref[...] = partial


def attend(seq, core, q, k, v, ids_rows, ids_cols, wait=()):
    width = q.shape[0]
    steps = LEN // FB
    half = steps // 2
    heads = width // HD
    blk = lambda i, c: lax.rem(i + half * (1 - c[0]), steps)
    whole = lambda *shape: pl.BlockSpec(shape, lambda i, c: (0,) * len(shape), pipeline_mode=pl.Buffered(1))
    return pl.pallas_call(
        ignoring(len(wait), attend_kernel),
        grid_spec=pltpu.PrefetchScalarGridSpec(
            num_scalar_prefetch=1,
            grid=(steps,),
            in_specs=[ANY] * len(wait)
            + [
                pl.BlockSpec((width, FB), lambda i, c: (0, blk(i, c))),
                whole(width, LEN),
                whole(width, LEN),
                pl.BlockSpec((None, 1, LEN), lambda i, c: (seq, 0, 0)),
                pl.BlockSpec((None, 1, FB), lambda i, c: (seq, 0, blk(i, c))),
                pl.BlockSpec((LEN, 128), lambda i, c: (seq, 0)),
            ],
            out_specs=[
                pl.BlockSpec((width, FB), lambda i, c: (0, jnp.minimum(i, half - 1))),
                pl.BlockSpec((width, FB), lambda i, c: (0, jnp.maximum(i - half, 0))),
                pl.BlockSpec((width, FB), lambda i, c: (0, blk(i, c))),
                pl.BlockSpec((8, FB), lambda i, c: (0, blk(i, c))),
            ],
            scratch_shapes=[
                pltpu.VMEM((heads, LEN, HD), bf16),
                pltpu.VMEM((heads, LEN, FB), f32),
                pltpu.VMEM((width, FB), f32),
            ],
        ),
        out_shape=[
            jax.ShapeDtypeStruct((width, LEN // 2), bf16),
            jax.ShapeDtypeStruct((width, LEN // 2), bf16),
            hbm((width, LEN), f32),
            hbm((8, LEN), f32),
        ],
        compiler_params=params(16),
        cost_estimate=cost(8 * LEN * LEN * width, 12 * LEN * width, heads * LEN * LEN),
        name="attend",
    )(core, *stay(*wait), q, k, v, ids_rows, ids_rows, ids_cols)


def norm_two_kernel(c_ref, x_ref, *refs):
    groups = (len(refs) - 5) // 2
    ctx_refs, wo_refs = refs[:groups], refs[groups : 2 * groups]
    bias_ref, gain_ref, beta_ref, resid_ref, normed_ref = refs[2 * groups :]
    attn = bias_ref[...]
    for ctx_ref, wo_ref in zip(ctx_refs, wo_refs):
        attn = attn + mm(ctx_ref[...], wo_ref[...], TN).astype(bf16).astype(f32)
    resid = x_ref[...].astype(f32) + attn
    resid_ref[...] = resid
    xhat, _ = standardize(resid)
    normed_ref[...] = (xhat * gain_ref[...] + beta_ref[...]).astype(bf16)


def norm_two(seq, core, patches, ctxs, wos, bias, gain, beta, wait=()):
    width, rows = ctxs[0].shape
    d = patches.shape[1]
    steps = rows // RB
    blk = pl.BlockSpec((RB, d), lambda i, c: (i, 0))
    whole = lambda *shape: pl.BlockSpec(shape, lambda i, c: (0,) * len(shape), pipeline_mode=pl.Buffered(1))
    return pl.pallas_call(
        ignoring(len(wait), norm_two_kernel),
        grid_spec=pltpu.PrefetchScalarGridSpec(
            num_scalar_prefetch=1,
            grid=(steps,),
            in_specs=[ANY] * len(wait)
            + [pl.BlockSpec((RB, d), lambda i, c: ((2 * seq + c[0]) * steps + i, 0))]
            + [pl.BlockSpec((width, RB), lambda i, c: (0, i))] * len(ctxs)
            + [whole(width, d)] * len(wos)
            + [whole(1, d)] * 3,
            out_specs=[blk, blk],
        ),
        out_shape=[hbm((rows, d), f32), hbm((rows, d), bf16)],
        compiler_params=params(8),
        cost_estimate=cost(2 * len(ctxs) * rows * d * width, 12 * rows * d),
        name="norm_two",
    )(core, *stay(*wait), *stay(patches), *ctxs, *wos, bias, gain, beta)


def store_halves(mine, outs, sums):
    count = outs[0].shape[0]
    for out, half in zip(outs, (1 - mine, mine)):
        for k in range(count):
            at = 0
            for acc in sums:
                rows = acc.shape[0] // (2 * count)
                spot = pl.ds(pl.multiple_of((half * count + k) * rows, 8), rows)
                out[k, at : at + rows, :] = acc[spot, :].astype(bf16)
                at += rows


def feed_kernel(first, last, c_ref, *refs):
    refs = list(refs)
    own_ref, other_ref, og_ref, up_ref, upb_ref, down_ref = refs[:6]
    refs = refs[6:]
    if not first:
        small0_ref, up0_ref, down0_ref = refs[:3]
        refs = refs[3:]
    mlp_send, mlp_keep, n2_send, n2_keep, small_out = refs[:5]
    outs = refs[5:-4]
    up_acc, down_acc, up_sum, down_sum = refs[-4:]
    step = pl.program_id(0)
    steps = pl.num_programs(0)
    half = steps // 2

    @pl.when(step == 0)
    def _():
        if first:
            up_acc[...] = jnp.zeros_like(up_acc)
            down_acc[...] = jnp.zeros_like(down_acc)
            up_sum[...] = jnp.zeros_like(up_sum)
            down_sum[...] = jnp.zeros_like(down_sum)
        else:
            up_acc[...] = up0_ref[...]
            down_acc[...] = down0_ref[...]
            up_sum[...] = small0_ref[0:1, :]
            down_sum[...] = small0_ref[1:2, :]

    normed = jnp.where(step < half, other_ref[...], own_ref[...])
    og = og_ref[...]
    pre = mm(normed, up_ref[...]) + upb_ref[...]
    phi_cap = 0.5 * (1.0 + lax.erf(pre * SQRT_HALF))
    hidden = (pre * phi_cap).astype(bf16)
    mlp = mm(hidden, down_ref[...]).astype(bf16)
    slope = phi_cap + pre * (jnp.exp(-0.5 * pre * pre) * INV_SQRT_2PI)
    grad = mm(og, down_ref[...], NT)
    pre_grad = (grad * slope).astype(bf16)
    n2 = mm(pre_grad, up_ref[...], NT).astype(bf16)
    down_acc[...] += mm(hidden, og, TN)
    up_acc[...] += mm(normed, pre_grad, TN)
    up_sum[...] += jnp.sum(pre_grad.astype(f32), axis=0, keepdims=True)
    down_sum[...] += jnp.sum(og.astype(f32), axis=0, keepdims=True)

    @pl.when(step < half)
    def _():
        mlp_send[...] = mlp
        n2_send[...] = n2

    @pl.when(step >= half)
    def _():
        mlp_keep[...] = mlp
        n2_keep[...] = n2

    @pl.when(step == steps - 1)
    def _():
        if last:
            store_halves(c_ref[1], outs, (up_acc, down_acc))
        else:
            outs[0][...] = up_acc[...]
            outs[1][...] = down_acc[...]
        small_out[0:1, :] = up_sum[...]
        small_out[1:2, :] = down_sum[...]
        small_out[2:8, :] = jnp.zeros((6, up_sum.shape[1]), f32)


def feed(seq, core, own, other, out_grad, up, up_bias, down, before=None, last=0, wait=()):
    d, units = up.shape
    steps = LEN // FB
    half = steps // 2
    first = before is None
    whole = lambda *shape: pl.BlockSpec(shape, lambda i, c: (0,) * len(shape), pipeline_mode=pl.Buffered(1))
    low = pl.BlockSpec((FB, d), lambda i, c: (jnp.minimum(i, half - 1), 0))
    high = pl.BlockSpec((FB, d), lambda i, c: (jnp.maximum(i - half, 0), 0))
    blk = lambda i, c: seq * steps + lax.rem(i + half * (1 - c[0]), steps)
    in_specs = [ANY] * len(wait) + [
        high, low,
        pl.BlockSpec((FB, d), lambda i, c: (blk(i, c), 0)),
        whole(d, units), whole(1, units), whole(units, d),
    ]
    args = [core, *stay(*wait), *stay(own), other, *stay(out_grad), up, up_bias, down]
    if not first:
        in_specs += [whole(8, d), whole(d, units), whole(units, d)]
        args += list(before)
    if last:
        grads = [(last, (d + units) // (2 * last), d)] * 2
        kind = bf16
    else:
        grads = [(d, units), (units, d)]
        kind = f32
    rows = jax.ShapeDtypeStruct((LEN // 2, d), bf16)
    return pl.pallas_call(
        ignoring(len(wait), functools.partial(feed_kernel, first, last)),
        grid_spec=pltpu.PrefetchScalarGridSpec(
            num_scalar_prefetch=1,
            grid=(steps,),
            in_specs=in_specs,
            out_specs=[low, high, low, high, whole(8, d)] + [whole(*g) for g in grads],
            scratch_shapes=[
                pltpu.VMEM((d, units), f32),
                pltpu.VMEM((units, d), f32),
                pltpu.VMEM((1, units), f32),
                pltpu.VMEM((1, d), f32),
            ],
        ),
        out_shape=[hbm(rows.shape, bf16), hbm(rows.shape, bf16), hbm(rows.shape, bf16), rows, hbm((8, d), f32)]
        + [(hbm if last else jax.ShapeDtypeStruct)(g, kind) for g in grads],
        compiler_params=params(24),
        cost_estimate=cost(12 * LEN * d * units, 2 * LEN * d * 4 + 12 * d * units, 2 * LEN * units),
        name="feed",
    )(*args)


def norm_two_back_kernel(first, c_ref, *refs):
    refs = list(refs)
    mine_ref, theirs_ref, resid_ref, og_ref, gain_ref = refs[:5]
    refs = refs[5:]
    if not first:
        small0_ref = refs[0]
        refs = refs[1:]
    rgrad_ref, branch_ref, small_ref = refs
    step = pl.program_id(0)

    @pl.when(step == 0)
    def _():
        if first:
            small_ref[...] = jnp.zeros_like(small_ref)
        else:
            small_ref[...] = small0_ref[...]

    grad = mine_ref[...].astype(f32) + theirs_ref[...].astype(f32)
    xhat, inverse = standardize(resid_ref[...])
    e = grad * gain_ref[...]
    back = inverse * (
        e - jnp.mean(e, axis=-1, keepdims=True) - xhat * jnp.mean(e * xhat, axis=-1, keepdims=True)
    )
    rgrad = og_ref[...].astype(f32) + back
    rgrad_ref[...] = rgrad
    branch = rgrad.astype(bf16)
    branch_ref[...] = branch
    small_ref[0:1, :] += jnp.sum(grad * xhat, axis=0, keepdims=True)
    small_ref[1:2, :] += jnp.sum(grad, axis=0, keepdims=True)
    small_ref[2:3, :] += jnp.sum(branch.astype(f32), axis=0, keepdims=True)


def norm_two_back(seq, core, mine, theirs, resid, out_grad, gain, before=None, wait=()):
    rows, d = mine.shape
    steps = rows // RB
    first = before is None
    blk = pl.BlockSpec((RB, d), lambda i, c: (i, 0))
    vec = pl.BlockSpec((1, d), lambda i, c: (0, 0))
    small = pl.BlockSpec((8, d), lambda i, c: (0, 0))
    in_specs = [ANY] * len(wait) + [blk, blk, blk, pl.BlockSpec((RB, d), lambda i, c: ((2 * seq + c[0]) * steps + i, 0)), vec]
    args = [core, *stay(*wait), mine, theirs, *stay(resid, out_grad), gain]
    if not first:
        in_specs.append(small)
        args += stay(before)
    return pl.pallas_call(
        ignoring(len(wait), functools.partial(norm_two_back_kernel, first)),
        grid_spec=pltpu.PrefetchScalarGridSpec(
            num_scalar_prefetch=1, grid=(steps,), in_specs=in_specs, out_specs=[blk, blk, small]
        ),
        out_shape=[
            hbm((rows, d), f32),
            jax.ShapeDtypeStruct((rows, d), bf16),
            hbm((8, d), f32),
        ],
        compiler_params=params(8),
        cost_estimate=cost(20 * rows * d, 16 * rows * d),
        name="norm_two_back",
    )(*args)


def attend_back_kernel(first, c_ref, *refs):
    refs = list(refs)
    own_ref, other_ref, q_ref, k_ref, v_ref, ctx_ref, lse_ref, idr_ref, idq_ref, idc_ref, wo_ref = refs[:11]
    refs = refs[11:]
    dwo0_ref = None if first else refs.pop(0)
    low_ref, dwo_ref, keys, vals, grads_ref = refs
    step = pl.program_id(0)
    steps = pl.num_programs(0)
    half = steps // 2
    width = q_ref.shape[0]
    heads = width // HD
    blk = lax.rem(step + half * (1 - c_ref[0]), steps)
    here = pl.ds(pl.multiple_of(blk * RB, RB), RB)

    @pl.when(step == 0)
    def _():
        for h in range(heads):
            keys[h] = jnp.transpose(rows_of(k_ref, h))
            vals[h] = jnp.transpose(rows_of(v_ref, h))
        grads_ref[...] = jnp.zeros_like(grads_ref)
        dwo_ref[...] = jnp.zeros_like(dwo_ref) if first else dwo0_ref[...]

    branch = jnp.where(step < half, other_ref[...], own_ref[...])
    ctx = ctx_ref[:, here]
    dctx = mm(wo_ref[...], branch, NT).astype(bf16)
    dwo_ref[...] += mm(ctx.astype(bf16), branch)
    prod = dctx.astype(f32) * ctx
    lse = lse_ref[:, here]
    ids_q = idq_ref[...]
    lo, hi = key_range(idr_ref[...], ids_q)
    parts = []
    for h in range(heads):
        sl = slice(h * HD, (h + 1) * HD)
        parts.append((q_ref[sl, here], dctx[sl], jnp.sum(prod[sl], axis=0, keepdims=True), lse[h : h + 1]))

    def body(kb, carry):
        at = pl.multiple_of(kb * KB, KB)
        there = pl.ds(at, KB)
        same = same_image(idc_ref, at, ids_q)
        for h in range(heads):
            q_h, do_h, delta, lse_h = parts[h]
            s = mm(keys[h, there, :], q_h)
            p = jnp.exp2(jnp.where(same, s * SCALE2 - lse_h, masked_score))
            dp = mm(vals[h, there, :], do_h)
            ds = (p * (dp - delta)).astype(bf16)
            at_q, at_k, at_v = (slice(k * width + h * HD, k * width + (h + 1) * HD) for k in range(3))
            grads_ref[at_q, here] += mm(k_ref[h * HD : (h + 1) * HD, there], ds)
            grads_ref[at_k, there] += mm(q_h, ds, NT)
            grads_ref[at_v, there] += mm(do_h, p.astype(bf16), NT)
        return carry

    lax.fori_loop(lo, hi, body, 0)

    @pl.when(step == steps - 1)
    def _():
        low_ref[...] = grads_ref[...].astype(bf16)


def attend_back(seq, core, own, other, q, k, v, ctx, lse, ids_rows, ids_cols, wo, before=None, wait=()):
    width, d = wo.shape
    heads = width // HD
    steps = LEN // RB
    half = steps // 2
    first = before is None
    whole = lambda *shape: pl.BlockSpec(shape, lambda i, c: (0,) * len(shape), pipeline_mode=pl.Buffered(1))
    blk = lambda i, c: lax.rem(i + half * (1 - c[0]), steps)
    in_specs = [ANY] * len(wait) + [
        pl.BlockSpec((RB, d), lambda i, c: (jnp.maximum(i - half, 0), 0)),
        pl.BlockSpec((RB, d), lambda i, c: (jnp.minimum(i, half - 1), 0)),
        whole(width, LEN), whole(width, LEN), whole(width, LEN), whole(width, LEN), whole(8, LEN),
        pl.BlockSpec((None, 1, LEN), lambda i, c: (seq, 0, 0)),
        pl.BlockSpec((None, 1, RB), lambda i, c: (seq, 0, blk(i, c))),
        pl.BlockSpec((LEN, 128), lambda i, c: (seq, 0)),
        whole(width, d),
    ]
    q, k, v, ctx, lse, ids_cols = stay(q, k, v, ctx, lse, ids_cols)
    args = [core, *stay(*wait), own, other, q, k, v, ctx, lse, ids_rows, ids_rows, ids_cols, wo]
    if not first:
        in_specs.append(whole(width, d))
        args += stay(before)
    return pl.pallas_call(
        ignoring(len(wait), functools.partial(attend_back_kernel, first)),
        grid_spec=pltpu.PrefetchScalarGridSpec(
            num_scalar_prefetch=1, grid=(steps,), in_specs=in_specs,
            out_specs=[whole(3 * width, LEN), whole(width, d)],
            scratch_shapes=[
                pltpu.VMEM((heads, LEN, HD), bf16), pltpu.VMEM((heads, LEN, HD), bf16), pltpu.VMEM((3 * width, LEN), f32)
            ],
        ),
        out_shape=[hbm((3 * width, LEN), bf16), hbm((width, d), f32)],
        compiler_params=params(18),
        cost_estimate=cost(
            20 * LEN * LEN * width + 8 * LEN * d * width, 2 * LEN * (10 * width + d) + 8 * d * width, heads * LEN * LEN,
        ),
        name="attend_back",
    )(*args)


def project_back_kernel(c_ref, *refs):
    seqs = (refs[:4], refs[4:8])
    (wt_ref, tab_ref, grid_ref, gain_ref, beta_ref, dwo_ref, small_two_ref, small_feed_ref) = refs[8:16]
    send_away, keep_away, send_mine, keep_mine, small_ref = refs[16:21]
    outs = refs[21:23]
    dwt_acc, col_acc, rope_acc = refs[23:]
    step = pl.program_id(0)
    steps = pl.num_programs(0) // 2
    half = steps // 2
    width = seqs[0][0].shape[0]
    heads = width // HD
    second = (step < steps) != (c_ref[2] > 0)

    def pick(k):
        return jnp.where(second, seqs[1][k][...], seqs[0][k][...])

    @pl.when(step == 0)
    def _():
        for acc in (dwt_acc, col_acc, rope_acc):
            acc[...] = jnp.zeros_like(acc)

    place = grid_ref[...]
    cosine, sine = lookup(tab_ref, place)
    grads = pick(2)
    pieces = []
    angle = [None] * heads
    for k in range(2):
        turned = pick(k)
        for h in range(heads):
            b = grads[k * width + h * HD : k * width + (h + 1) * HD].astype(f32) * SCALE
            a = turned[h * HD : (h + 1) * HD].astype(f32)
            b1, b2 = b[:HALF], b[HALF:]
            co = cosine[h * HALF : (h + 1) * HALF]
            si = sine[h * HALF : (h + 1) * HALF]
            pieces.append((b1 * co + b2 * si).astype(bf16))
            pieces.append((b2 * co - b1 * si).astype(bf16))
            term = b2 * a[:HALF] - b1 * a[HALF:]
            angle[h] = term if angle[h] is None else angle[h] + term
    pieces.append(grads[2 * width :].astype(bf16))
    mixed_grad = jnp.concatenate(pieces, axis=0)
    angle = jnp.concatenate(angle, axis=0)
    rope_acc[...] += lax.dot_general(
        place.astype(f32), angle, NT, precision=lax.Precision.HIGHEST, preferred_element_type=f32
    )
    exact = mixed_grad.astype(f32)
    folded = exact[:, 0:128]
    for at in range(128, FB, 128):
        folded = folded + exact[:, at : at + 128]
    col_acc[...] += folded
    dwt_acc[...] += mm(mixed_grad, pick(3))
    partial = mm(mixed_grad, wt_ref[...], TN).astype(bf16)
    for k, out in enumerate((send_away, keep_away, send_mine, keep_mine)):
        @pl.when(step // half == k)
        def _():
            out[...] = partial

    @pl.when(step == 2 * steps - 1)
    def _():
        raw = dwt_acc[...]
        col = jnp.sum(col_acc[...], axis=1, keepdims=True)
        row_sum = jnp.sum(jnp.transpose(col_acc[...]), axis=0, keepdims=True)
        wt = wt_ref[...].astype(f32)
        small_ref[0:1, :] = jnp.sum(wt * raw, axis=0, keepdims=True)
        small_ref[1:2, :] = jnp.sum(wt * col, axis=0, keepdims=True)
        small_ref[2:5, :] = 0.5 * small_two_ref[0:3, :]
        small_ref[5:7, :] = small_feed_ref[0:2, :]
        small_ref[7:8, :] = jnp.concatenate([row_sum, rope_acc[1:2, :], rope_acc[0:1, :]], axis=1)
        dwt_acc[...] = raw * gain_ref[...] + col * beta_ref[...]
        store_halves(c_ref[1], outs, (dwt_acc, dwo_ref))


def project_back(core, seqs, wt, tab, grid, gain, beta, dwo, small_two, small_feed, pieces, wait=()):
    d = wt.shape[1]
    width = wt.shape[0] // 3
    heads = width // HD
    steps = LEN // FB
    half = steps // 2
    whole = lambda *shape: pl.BlockSpec(shape, lambda i, c: (0,) * len(shape), pipeline_mode=pl.Buffered(1))
    blk = lambda i, c: lax.rem(lax.rem(i, steps) + half * (1 - c[0]), steps)
    now = lambda i, c: jnp.where(i < steps, 1 - c[2], c[2])

    def turn(s, i, c):
        early = s == jnp.where(c[2] > 0, 0, 1)
        rest = jnp.where(early, blk(steps - 1, c), blk(0, c))
        return jnp.where(now(i, c) == s, blk(i, c), rest)

    in_specs = [ANY] * len(wait)
    args = [core, *stay(*wait)]
    for s in range(2):
        tall = lambda i, c, s=s: (0, turn(s, i, c))
        flat = lambda i, c, s=s: (turn(s, i, c), 0)
        in_specs += [
            pl.BlockSpec((width, FB), tall), pl.BlockSpec((width, FB), tall), pl.BlockSpec((3 * width, FB), tall),
            pl.BlockSpec((FB, d), flat),
        ]
        args += stay(*seqs[s])
    in_specs += [
        whole(3 * width, d), whole(*tab.shape),
        pl.BlockSpec((2, FB), lambda i, c: (0, now(i, c) * steps + blk(i, c))),
        whole(1, d), whole(1, d), whole(width, d), whole(8, d), whole(8, d),
    ]
    args += [wt, *stay(tab, grid), gain, beta, *stay(dwo, small_two, small_feed)]
    part = lambda k: pl.BlockSpec((FB, d), lambda i, c: (jnp.clip(i - k * half, 0, half - 1), 0))
    cut = (pieces, 4 * width // (2 * pieces), d)
    rows = hbm((LEN // 2, d), bf16)
    return pl.pallas_call(
        ignoring(len(wait), project_back_kernel),
        grid_spec=pltpu.PrefetchScalarGridSpec(
            num_scalar_prefetch=1, grid=(2 * steps,), in_specs=in_specs,
            out_specs=[part(0), part(1), part(2), part(3), whole(8, d), whole(*cut), whole(*cut)],
            scratch_shapes=[
                pltpu.VMEM((3 * width, d), f32),
                pltpu.VMEM((3 * width, 128), f32),
                pltpu.VMEM((2, heads * HALF), f32),
            ],
        ),
        out_shape=[rows, rows, rows, rows, hbm((8, d), f32), hbm(cut, bf16), hbm(cut, bf16)],
        compiler_params=params(30),
        cost_estimate=cost(24 * LEN * d * width, 4 * LEN * (12 * width + 3 * d), LEN * width),
        name="project_back",
    )(*args)


def norm_one_back_kernel(m_ref, mine_ref, got_ref, theirs_ref, x_ref, rg0_ref, rg1_ref, gain_ref, out_ref):
    f = (mine_ref[...].astype(f32) + got_ref[...].astype(f32) + theirs_ref[...].astype(f32)) * gain_ref[...]
    xhat, inverse = standardize(x_ref[...].astype(f32))
    back = inverse * (
        f - jnp.mean(f, axis=-1, keepdims=True) - xhat * jnp.mean(f * xhat, axis=-1, keepdims=True)
    )
    rgrad = jnp.where(m_ref[0] < 2, rg0_ref[...], rg1_ref[...])
    out_ref[...] = (rgrad + back).astype(bf16)


def norm_one_back(place, mine, got, theirs, patches, rg0, rg1, gain):
    rows, d = mine.shape
    steps = rows // RB
    blk = pl.BlockSpec((RB, d), lambda i, m: (i, 0))
    return pl.pallas_call(
        norm_one_back_kernel,
        grid_spec=pltpu.PrefetchScalarGridSpec(
            num_scalar_prefetch=1,
            grid=(steps,),
            in_specs=[
                blk, blk, blk, pl.BlockSpec((RB, d), lambda i, m: (m[0] * steps + i, 0)), blk, blk,
                pl.BlockSpec((1, d), lambda i, m: (0, 0)),
            ],
            out_specs=blk,
        ),
        out_shape=jax.ShapeDtypeStruct((rows, d), bf16),
        compiler_params=params(10),
        cost_estimate=cost(20 * rows * d, 16 * rows * d),
        name="norm_one_back",
    )(place, mine, got, theirs, *stay(patches, rg0, rg1), gain)


CORE_SWAP = [(i, i ^ 1) for i in range(4)]
CHIP_SWAP = [(i, i ^ 2) for i in range(4)]


def core_swap(value):
    return lax.ppermute(value, "mp", CORE_SWAP)


def chip_swap(value):
    return lax.ppermute(value, "mp", CHIP_SWAP)


def after(value, *events):
    return lax.optimization_barrier((value, *events))[0]


def add_low(a, b):
    return (a.astype(f32) + b.astype(f32)).astype(bf16)


def add_kernel(c_ref, a_ref, b_ref, out_ref):
    out_ref[...] = (a_ref[...].astype(f32) + b_ref[...].astype(f32)).astype(bf16)


def full(shape):
    return pl.BlockSpec(shape, lambda i, c: (0,) * len(shape))


def add_parts(core, a, b, wait=()):
    return pl.pallas_call(
        ignoring(len(wait), add_kernel),
        grid_spec=pltpu.PrefetchScalarGridSpec(
            num_scalar_prefetch=1, grid=(1,), in_specs=[ANY] * len(wait) + [full(a.shape)] * 2, out_specs=full(a.shape),
        ),
        out_shape=hbm(a.shape, bf16),
        compiler_params=params(10),
        cost_estimate=cost(a.size, 6 * a.size),
        name="add_parts",
    )(core, *stay(*wait), *stay(a), b)


def sum_parts_kernel(c_ref, parts_ref, *refs):
    out_ref = refs[-1]
    total = parts_ref[0].astype(f32)
    for k in range(1, parts_ref.shape[0]):
        total = total + parts_ref[k].astype(f32)
    rows = total.shape[0]
    total = total.astype(bf16)
    for k in range(out_ref.shape[0]):
        out_ref[k, 0:rows, :] = total
    if len(refs) > 1:
        small = refs[0][...]
        high = small.astype(bf16)
        low = (small - high.astype(f32)).astype(bf16)
        for k in range(out_ref.shape[0]):
            out_ref[k, rows : rows + 8, :] = high
            out_ref[k, rows + 8 : rows + 16, :] = low


def sum_parts(core, parts, small=None, copies=None, wait=()):
    count, rows, d = parts.shape
    extra = () if small is None else (small,)
    out = (copies or count, rows + 16 * len(extra), d)
    return pl.pallas_call(
        ignoring(len(wait), sum_parts_kernel),
        grid_spec=pltpu.PrefetchScalarGridSpec(
            num_scalar_prefetch=1, grid=(1,),
            in_specs=[ANY] * len(wait) + [full(parts.shape)] + [full(e.shape) for e in extra],
            out_specs=full(out),
        ),
        out_shape=jax.ShapeDtypeStruct(out, bf16),
        compiler_params=params(10),
        cost_estimate=cost(count * rows * d, 4 * count * rows * d),
        name="sum_parts",
    )(core, *stay(*wait), parts, *extra)


def place_parts_kernel(with_small, c_ref, mine_ref, theirs_ref, *refs):
    outs = refs[: len(refs) - 3 * with_small]
    count = mine_ref.shape[0]
    small = None
    for ref, half in ((mine_ref, c_ref[1]), (theirs_ref, 1 - c_ref[1])):
        for k in range(count):
            at = 0
            for out in outs:
                rows = out.shape[0] // (2 * count)
                spot = pl.ds(pl.multiple_of((half * count + k) * rows, 8), rows)
                out[spot, :] = ref[k, at : at + rows, :].astype(f32)
                at += rows
            if with_small:
                part = ref[k, at : at + 8, :].astype(f32) + ref[k, at + 8 : at + 16, :].astype(f32)
                small = part if small is None else small + part
    if with_small:
        small_ref, bias_ref, rope_ref = refs[-3:]
        small_ref[...] = small
        width = bias_ref.shape[1]
        heads = rope_ref.shape[0]
        for k in range(3):
            bias_ref[k : k + 1, :] = small[7:8, k * width : (k + 1) * width]
        for h in range(heads):
            for k in range(2):
                at = 3 * width + (k * heads + h) * HALF
                rope_ref[h : h + 1, k * HALF : (k + 1) * HALF] = small[7:8, at : at + HALF]


def place_parts(core, mine, theirs, splits, with_small=()):
    d = mine.shape[2]
    shapes = [(rows, d) for rows in splits] + list(with_small)
    return pl.pallas_call(
        functools.partial(place_parts_kernel, bool(with_small)),
        grid_spec=pltpu.PrefetchScalarGridSpec(
            num_scalar_prefetch=1, grid=(1,), in_specs=[full(mine.shape)] * 2, out_specs=[full(t) for t in shapes],
        ),
        out_shape=[jax.ShapeDtypeStruct(t, f32) for t in shapes],
        compiler_params=params(18),
        cost_estimate=cost(sum(splits) * d, 6 * sum(splits) * d),
        name="place_parts",
    )(core, mine, theirs)


def half_swap(value):
    return lax.ppermute(value, "dp", [(i, i ^ 1) for i in range(lax.axis_size("dp"))])


def quarter_trade(parts):
    return lax.all_to_all(parts, "dp", 0, 0, axis_index_groups=[[0, 2, 4, 6], [1, 3, 5, 7]])


def hold(values, *events):
    return list(lax.optimization_barrier((*values, *events))[: len(values)])


def local(patches, image_ids, patch_grid, first_norm_gain, first_norm_bias, qkv_weight, qkv_bias, rope_freq,
          out_weight, out_bias, second_norm_gain, second_norm_bias, up_weight, up_bias, down_weight, down_bias,
          out_grad):
    all_rows, d = patches.shape
    seqs = all_rows // LEN
    assert lax.axis_size("mp") == 4 and seqs == 2
    devices = lax.axis_size("dp")
    tree = devices == 8
    pieces = 4 if tree else 1
    heads = rope_freq.shape[0]
    width = heads * HD
    units = up_weight.shape[1]
    place = lax.axis_index("mp").astype(jnp.int32)
    half = lax.axis_index("dp").astype(jnp.int32) % 2 if tree else jnp.int32(0)
    core = jnp.stack([place % 2, half, place // 2])
    place_arr = place.reshape(1)
    far = place >= 2
    row = lambda v: v.reshape(1, -1)

    tab, bias_cols = prepare(rope_freq, qkv_bias)
    wt = qkv_weight.transpose(1, 2, 0).reshape(3 * width, d)
    ids_rows = image_ids.reshape(seqs, 1, LEN)
    ids_cols = jnp.broadcast_to(image_ids[:, None], (all_rows, 128))
    gain1, beta1 = row(first_norm_gain), row(first_norm_bias)
    gain2, beta2 = row(second_norm_gain), row(second_norm_bias)

    wo_core = core_swap(out_weight)
    proj_args = (patches, patch_grid, tab, wt, bias_cols, gain1, beta1)
    made0 = project(0, core, *proj_args)
    send0, keep0, ctx0, lse0 = attend(0, core, *made0[1:], ids_rows, ids_cols)
    core0, far_keep0 = core_swap(send0), chip_swap(keep0)
    made1 = project(1, core, *proj_args, wait=[lse0, wo_core])
    far_core0, wo_far = chip_swap(core0), chip_swap(out_weight)
    send1, keep1, ctx1, lse1 = attend(1, core, *made1[1:], ids_rows, ids_cols, wait=[made1[0]])
    core1, far_keep1 = core_swap(send1), chip_swap(keep1)
    wos = [out_weight, wo_core, wo_far, core_swap(wo_far)]
    norm_args = (row(out_bias), gain2, beta2)
    resid0, normed0 = norm_two(
        0, core, patches, [keep0, core0, far_keep0, far_core0], wos, *norm_args, wait=[lse1]
    )
    normed0, core1, far_keep1 = hold([normed0, core1, far_keep1])
    far_core1 = chip_swap(core1)
    feed_args = (out_grad, up_weight, row(up_bias), down_weight)
    mlp_send0, mlp_keep0, n2_send0, n2_keep0, *sums = feed(
        0, core, normed0, core_swap(normed0), *feed_args
    )
    n2_send0, far_core1 = hold([n2_send0, far_core1])
    n20 = add_low(n2_keep0, core_swap(n2_send0))
    resid1, normed1 = norm_two(
        1, core, patches, [keep1, core1, far_keep1, far_core1], wos, *norm_args, wait=[sums[0]]
    )
    n2_far0 = chip_swap(n20)
    mlp_send1, mlp_keep1, n2_send1, n2_keep1, small_feed, feed_send, feed_keep = feed(
        1, core, normed1, core_swap(normed1), *feed_args, before=sums, last=pieces, wait=[n20]
    )
    if tree:
        feed_got = half_swap(feed_send)
    n21 = add_low(n2_keep1, core_swap(n2_send1))
    mlp0 = add_low(mlp_keep0, core_swap(mlp_send0))
    mlp1 = add_low(mlp_keep1, core_swap(mlp_send1))
    mlp_away, mlp_mine = jnp.where(far, mlp0, mlp1), jnp.where(far, mlp1, mlp0)
    rgrad0, branch0, small_two = norm_two_back(
        0, core, n20, n2_far0, resid0, out_grad, gain2, wait=[small_feed]
    )
    n2_far1 = chip_swap(n21)
    grads0, dwo = attend_back(
        0, core, branch0, core_swap(branch0), *made0[1:], ctx0, lse0, ids_rows, ids_cols, out_weight, wait=[n21]
    )
    event = dwo
    if tree:
        feed_part = add_low(feed_keep, after(feed_got, dwo, n2_far1))
        event = feed_part
        feed_got = quarter_trade(feed_part)
    rgrad1, branch1, small_two = norm_two_back(
        1, core, n21, n2_far1, resid1, out_grad, gain2, before=small_two, wait=[event]
    )
    mlp_theirs = chip_swap(mlp_away)
    grads1, dwo = attend_back(
        1, core, branch1, core_swap(branch1), *made1[1:], ctx1, lse1, ids_rows, ids_cols, out_weight, before=dwo,
        wait=[mlp_away],
    )
    event = dwo
    if tree:
        feed_sum = sum_parts(core, feed_got, wait=[dwo, mlp_theirs])
        event = feed_sum
        feed_all = quarter_trade(feed_sum)
    n1_send_away, n1_away, n1_send, n1_keep, small, grad_send, grad_keep = project_back(
        core, [(*made[1:3], grads, made[0]) for made, grads in ((made0, grads0), (made1, grads1))],
        wt, tab, patch_grid, gain1, beta1, dwo, small_two, small_feed, pieces, wait=[event],
    )
    n1_away = add_low(n1_away, core_swap(n1_send_away))
    n1_got = core_swap(n1_send)
    shared = lax.broadcasted_iota(jnp.int32, small.shape, 0) < 5
    for swap in (core_swap, chip_swap):
        small = small + jnp.where(shared, swap(small), 0.0)
    theirs = chip_swap(after(n1_away, small))
    if tree:
        grad_got = half_swap(grad_send)
        grad_got = quarter_trade(add_parts(core, grad_keep, grad_got, wait=[feed_all]))
        feed_other = half_swap(feed_all)
        grad_sum = quarter_trade(sum_parts(core, after(grad_got, feed_other), small))
        grad_other = half_swap(grad_sum)
    else:
        small, grad_send, grad_keep, feed_send, feed_keep = lax.psum(
            (small, grad_send, grad_keep, feed_send, feed_keep), "dp"
        )
        feed_all, feed_other = feed_keep, feed_send
        grad_sum = sum_parts(core, grad_keep, small)
        grad_other = sum_parts(core, grad_send, jnp.zeros_like(small))

    out_rows = (
        jnp.where(far, resid1, resid0)
        + (mlp_mine.astype(f32) + mlp_theirs.astype(f32))
        + row(down_bias)
    ).astype(bf16)
    grad_rows = norm_one_back(place_arr, n1_keep, n1_got, theirs, patches, rgrad0, rgrad1, gain1)
    up_grad, down_grad = place_parts(core, feed_all, feed_other, (d, units))
    (grad_other,) = hold([grad_other], grad_rows)
    qkv_grad, out_grad_w, small, bias_grad, rope_grad = place_parts(
        core, grad_sum, grad_other, (3 * width, width), ((8, d), (3, width), (heads, HD))
    )
    return (
        out_rows,
        grad_rows,
        small[0],
        small[1],
        qkv_grad.reshape(3, width, d).transpose(2, 0, 1),
        bias_grad,
        rope_grad,
        out_grad_w,
        small[4],
        small[2],
        small[3],
        up_grad,
        small[5],
        down_grad,
        small[6],
    )


def solution(mesh):
    placed = (
        P("dp", None),
        P("dp"),
        P(None, "dp"),
        P(),
        P(),
        P(None, None, "mp"),
        P(None, "mp"),
        P("mp", None),
        P("mp", None),
        P(),
        P(),
        P(),
        P(None, "mp"),
        P("mp"),
        P("mp", None),
        P(),
        P("dp", None),
    )
    return jax.shard_map(
        local,
        mesh=mesh,
        in_specs=placed,
        out_specs=(
            P(("dp", "mp"), None),
            P(("dp", "mp"), None),
            P(),
            P(),
            P(None, None, "mp"),
            P(None, "mp"),
            P("mp", None),
            P("mp", None),
            P(),
            P(),
            P(),
            P(None, "mp"),
            P("mp"),
            P("mp", None),
            P(),
        ),
        check_vma=False,
    )
```
